128 devices in a mesh: dp: 16 (over y, z), fsdp: 8 (over x, core).
Axes of the slice: x: 4, y: 4, z: 4, core: 2. Of those that a mesh axis runs over, the one named last changes fastest.
Arguments:
- tokens: bfloat16 [128, 8, 64, 768], P(('dp', 'fsdp')), may hold values from -6 to 6
- cotangent: bfloat16 [128, 8, 64, 768], P(('dp', 'fsdp')), may hold values from -6 to 6
- lengths: int32 [128], P(('dp', 'fsdp')), may hold values from 32 to 64
- row_offset: int32 [128], P(('dp', 'fsdp')), may hold values from 0 to 1016
- col_offset: int32 [128], P(('dp', 'fsdp')), may hold values from 0 to 960
- norm_gain: bfloat16 [3, 768], P(None, ('dp', 'fsdp')), may hold values from 0.099609375 to 1.8984375
- norm_bias: bfloat16 [3, 768], P(None, ('dp', 'fsdp')), may hold values from -1.75 to 1.75
- row_qkv: bfloat16 [3, 768, 768], P(None, ('dp', 'fsdp')), may hold values from -0.21875 to 0.21875
- row_out: bfloat16 [768, 768], P(('dp', 'fsdp')), may hold values from -1.25 to 1.25
- row_bias: bfloat16 [3, 768], P(None, ('dp', 'fsdp')), may hold values from -1.75 to 1.75
- col_qkv: bfloat16 [3, 768, 768], P(None, ('dp', 'fsdp')), may hold values from -0.21875 to 0.21875
- col_out: bfloat16 [768, 768], P(('dp', 'fsdp')), may hold values from -0.4375 to 0.4375
- col_bias: bfloat16 [3, 768], P(None, ('dp', 'fsdp')), may hold values from -1.75 to 1.75
- ffn_up: bfloat16 [768, 3072], P(('dp', 'fsdp')), may hold values from -0.21875 to 0.21875
- up_bias: bfloat16 [3072], P(('dp', 'fsdp')), may hold values from -1.75 to 1.75
- ffn_down: bfloat16 [3072, 768], P(('dp', 'fsdp')), may hold values from -0.15625 to 0.15625
- down_bias: bfloat16 [768], P(('dp', 'fsdp')), may hold values from -1.75 to 1.75
- pos_tables: bfloat16 [2, 1024, 768], P(None, ('dp', 'fsdp')), may hold values from -3 to 3
Outputs:
- activations: bfloat16 [128, 8, 64, 768], P(('dp', 'fsdp'))
- tokens_grad: float32 [128, 8, 64, 768], P(('dp', 'fsdp'))
- norm_gain_grad: float32 [3, 768], P(None, ('dp', 'fsdp'))
- norm_bias_grad: float32 [3, 768], P(None, ('dp', 'fsdp'))
- row_qkv_grad: float32 [3, 768, 768], P(None, ('dp', 'fsdp'))
- row_out_grad: float32 [768, 768], P(('dp', 'fsdp'))
- row_bias_grad: float32 [3, 768], P(None, ('dp', 'fsdp'))
- col_qkv_grad: float32 [3, 768, 768], P(None, ('dp', 'fsdp'))
- col_out_grad: float32 [768, 768], P(('dp', 'fsdp'))
- col_bias_grad: float32 [3, 768], P(None, ('dp', 'fsdp'))
- ffn_up_grad: float32 [768, 3072], P(('dp', 'fsdp'))
- up_bias_grad: float32 [3072], P(('dp', 'fsdp'))
- ffn_down_grad: float32 [3072, 768], P(('dp', 'fsdp'))
- down_bias_grad: float32 [768], P(('dp', 'fsdp'))
- pos_tables_grad: float32 [2, 1024, 768], P(None, ('dp', 'fsdp'))
The draws below stay inside these ranges and needn't reach their ends.
All inputs are finite; a program needn't handle non-finite values.
Results may differ from the reference program's by a relative error of at most 0.018.
Values may be sent and summed in bfloat16 or wider, within the bound.
No kernel may reach another device: no remote copies, remote signals or barrier semaphores. Data moves between devices by JAX's collectives and lax.ppermute only.
A program may use at most 256 MiB of HBM per device.

```python
import math
import jax
import jax.numpy as jnp
from jax import lax

D = 768
FF = 3072
HEADS = 12
HEAD_DIM = 64
POSITIONS = 1024
ROWS = 8
COLS = 64
ALIGNS = 128


def plant(values, rng, smallest, high):
    dims = values.shape
    spot = [jax.random.randint(jax.random.fold_in(rng, axis), (), 0, dims[axis]) for axis in range(len(dims))]
    values = values.at[tuple(spot)].set(smallest)
    longest = dims.index(max(dims))
    spot[longest] = (spot[longest] + 1) % dims[longest]
    return values.at[tuple(spot)].set(high)


def shard_levels(stream_key, shape, shards, low, largest):
    def one(axis_at, shards_of):
        heights = jax.random.uniform(jax.random.fold_in(jax.random.fold_in(stream_key, 6), axis_at), (shards_of,), jnp.float32, low / len(shards), largest / len(shards))
        return jnp.repeat(jnp.exp(heights), shape[axis_at] // shards_of).reshape((-1,) + (1,) * (len(shape) - axis_at - 1))

    level = one(*shards[0])
    for cut in shards[1:]:
        level = level * one(*cut)
    return level


def bell_draw(rng, extent, scale, most, shards=(), kind=jnp.bfloat16):
    drawn = scale * jax.random.normal(rng, extent, jnp.float32)
    if shards:
        drawn = drawn * shard_levels(rng, extent, shards, -0.22, 0.18)
    return jnp.clip(drawn, -most, most).astype(kind)


def setup_inputs(seed: int = 0) -> dict:
    key_of = jax.random.split(jax.random.key(seed), 19)
    tokens = bell_draw(key_of[0], (ALIGNS, ROWS, COLS, D), 1.0, 6.0, ((0, 128),))
    cotangent = bell_draw(key_of[1], (ALIGNS, ROWS, COLS, D), 1.0, 6.0, ((0, 128),))
    lengths = plant(jax.random.randint(key_of[2], (ALIGNS,), COLS // 2, COLS + 1), jax.random.fold_in(key_of[2], 1), COLS // 2, COLS).astype(jnp.int32)
    row_offset = plant(jax.random.randint(key_of[3], (ALIGNS,), 0, POSITIONS - ROWS + 1), jax.random.fold_in(key_of[3], 1), 0, POSITIONS - ROWS).astype(jnp.int32)
    col_offset = plant(jax.random.randint(key_of[4], (ALIGNS,), 0, POSITIONS - COLS + 1), jax.random.fold_in(key_of[4], 1), 0, POSITIONS - COLS).astype(jnp.int32)
    norm_gain = jnp.clip(1.0 + 0.18 * jax.random.normal(key_of[5], (3, D), jnp.float32), 0.099609375, 1.8984375).astype(jnp.bfloat16)
    norm_bias = bell_draw(key_of[6], (3, D), 0.3, 1.75, ((1, 128),))
    row_qkv = bell_draw(key_of[7], (3, D, D), D ** -0.5, 0.21875, ((1, 128),))
    row_out = bell_draw(key_of[8], (D, D), (D // 32) ** -0.5, 1.25, ((0, 128),))
    row_bias = bell_draw(key_of[9], (3, D), 0.3, 1.75, ((1, 128),))
    col_qkv = bell_draw(key_of[10], (3, D, D), D ** -0.5, 0.21875, ((1, 128),))
    col_out = bell_draw(key_of[11], (D, D), (D // 4) ** -0.5, 0.4375, ((0, 128),))
    col_bias = bell_draw(key_of[12], (3, D), 0.3, 1.75, ((1, 128),))
    ffn_up = bell_draw(key_of[13], (D, FF), D ** -0.5, 0.21875, ((0, 128),))
    up_bias = bell_draw(key_of[14], (FF,), 0.3, 1.75, ((0, 128),))
    ffn_down = bell_draw(key_of[15], (FF, D), (FF // 2) ** -0.5, 0.15625, ((0, 128),))
    down_bias = bell_draw(key_of[16], (D,), 0.3, 1.75, ((0, 128),))
    pos_tables = bell_draw(key_of[17], (2, POSITIONS, D), 0.5, 3.0, ((1, 128),))
    return dict(tokens=tokens, cotangent=cotangent, lengths=lengths, row_offset=row_offset, col_offset=col_offset, norm_gain=norm_gain, norm_bias=norm_bias, row_qkv=row_qkv, row_out=row_out, row_bias=row_bias, col_qkv=col_qkv, col_out=col_out, col_bias=col_bias, ffn_up=ffn_up, up_bias=up_bias, ffn_down=ffn_down, down_bias=down_bias, pos_tables=pos_tables)


highest = lax.Precision.HIGHEST
eps = 1e-05
row_forms = ('rihe,rjhe->hij', 'hij,rjhe->rihe', 'hij,rihe->rjhe')
col_forms = ('rche,tche->chrt', 'chrt,tche->rche', 'chrt,rche->tche')

@jax.custom_vjp
def low(v):
    return lax.optimization_barrier(v.astype(jnp.bfloat16)).astype(jnp.float32)

@jax.custom_vjp
def low_back(v):
    return v

def low_keep(v):
    return (low(v), None)

def low_pass(kept, grad):
    return (grad,)

def back_keep(v):
    return (v, None)

def back_low(kept, grad):
    return (low(grad),)
low.defvjp(low_keep, low_pass)
low_back.defvjp(back_keep, back_low)

def matmul(left_arr, right_arr):
    return jnp.dot(left_arr, right_arr, precision=highest)

def layer_norm(hidden, gain_vec, shift_vec):
    centred = hidden - lax.optimization_barrier(jnp.mean(hidden, axis=-1, keepdims=True))
    spread = lax.optimization_barrier(jnp.mean(centred * centred, axis=-1, keepdims=True))
    return centred * lax.rsqrt(spread + eps) * gain_vec + shift_vec

def attention(normed, projection, out_proj, biases, score_scale, key_mask, einsum_forms):
    shape_heads = (ROWS, COLS, HEADS, HEAD_DIM)
    queries = low_back(low(matmul(normed, projection[0]) + biases[0])).reshape(shape_heads)
    key_act = low_back(low(matmul(normed, projection[1]))).reshape(shape_heads)
    value_act = low_back(low(matmul(normed, projection[2]) + biases[1])).reshape(shape_heads)
    scores = jnp.einsum(einsum_forms[0], queries, key_act, precision=highest) * score_scale
    if key_mask is not None:
        scores = jnp.where(key_mask, scores, -1e+30)
    softmax_out = low(jax.nn.softmax(low_back(scores), axis=-1))
    mixed_heads = jnp.einsum(einsum_forms[1], softmax_out, value_act, precision=highest)
    mixed_heads = low_back(low(mixed_heads)).reshape(normed.shape)
    return low_back(matmul(mixed_heads, out_proj) + biases[2])

def one_alignment(params, tokens_one, row_start, col_start, length):
    norm_gains, norm_shifts, row_proj, row_output, row_biases, col_proj, col_output, col_biases, up_weight, up_biases, down_weight, down_biases, tables = params
    row_pos = lax.dynamic_slice_in_dim(tables[0], row_start, ROWS, 0)
    col_pos = lax.dynamic_slice_in_dim(tables[1], col_start, COLS, 0)
    hidden_in = (tokens_one + row_pos[:, None, :] + col_pos[None, :, :]).reshape(ROWS * COLS, D)
    key_mask = (jnp.arange(COLS) < length)[None, None, :]
    normed = low(layer_norm(hidden_in, norm_gains[0], norm_shifts[0]))
    hidden_mid = hidden_in + attention(normed, row_proj, row_output, row_biases, 1.0 / math.sqrt(HEAD_DIM * ROWS), key_mask, row_forms)
    normed = low(layer_norm(hidden_mid, norm_gains[1], norm_shifts[1]))
    hidden_late = hidden_mid + attention(normed, col_proj, col_output, col_biases, 1.0 / math.sqrt(HEAD_DIM), None, col_forms)
    normed = low(layer_norm(hidden_late, norm_gains[2], norm_shifts[2]))
    pre_act = low_back(matmul(normed, up_weight) + up_biases)
    act_value = low_back(low(jax.nn.gelu(pre_act, approximate=False)))
    hidden_out = hidden_late + low_back(matmul(act_value, down_weight) + down_biases)
    return hidden_out.reshape(ROWS, COLS, D)

def reference(tokens, cotangent, lengths, row_offset, col_offset, norm_gain, norm_bias, row_qkv, row_out, row_bias, col_qkv, col_out, col_bias, ffn_up, up_bias, ffn_down, down_bias, pos_tables):
    params = tuple((member.astype(jnp.float32) for member in (norm_gain, norm_bias, row_qkv, row_out, row_bias, col_qkv, col_out, col_bias, ffn_up, up_bias, ffn_down, down_bias, pos_tables)))
    group_size = 8
    blocks = ALIGNS // group_size
    stacked = (tokens.reshape((blocks, group_size, ROWS, COLS, D)), cotangent.reshape((blocks, group_size, ROWS, COLS, D)), lengths.reshape((blocks, group_size)), row_offset.reshape((blocks, group_size)), col_offset.reshape((blocks, group_size)))

    def scan_step(totals, entry):
        tok_block, cot_block, len_block, row_block, col_block = entry

        def layer_block(weights, hidden):
            return jax.vmap(one_alignment, in_axes=(None, 0, 0, 0, 0))(weights, hidden, row_block, col_block, len_block)
        outputs, pullback = jax.vjp(layer_block, params, tok_block.astype(jnp.float32))
        valid_cols = (jnp.arange(COLS)[None, :] < len_block[:, None]).astype(jnp.float32)
        weight_grads, grad_tokens = pullback(cot_block.astype(jnp.float32) * valid_cols[:, None, :, None])
        totals = jax.tree.map(lambda total_grad, new_grad: total_grad + new_grad, totals, weight_grads)
        return (totals, (outputs.astype(jnp.bfloat16), grad_tokens))
    zero_grads = jax.tree.map(jnp.zeros_like, params)
    totals, (outputs, grad_tokens) = lax.scan(scan_step, zero_grads, stacked)
    return (outputs.reshape((ALIGNS, ROWS, COLS, D)), grad_tokens.reshape((ALIGNS, ROWS, COLS, D)), totals[0], totals[1], totals[2], totals[3], totals[4], totals[5], totals[6], totals[7], totals[8], totals[9], totals[10], totals[11], totals[12])
```

```python
import math

import jax
import jax.numpy as jnp
from jax import lax
from jax.sharding import Mesh, PartitionSpec as P

HEADS = 12
HEAD_DIM = 64
POSITIONS = 1024


eps = 1e-05
row_forms = ("rihe,rjhe->hij", "hij,rjhe->rihe", "hij,rihe->rjhe")
col_forms = ("rche,tche->chrt", "chrt,tche->rche", "chrt,rche->tche")

AXES = ("y", "z", "x", "c")

DEVICES = 128
LANES = 128


def gather_weights(*pieces):
    flat = jnp.concatenate([piece.reshape(-1) for piece, _ in pieces])
    count = flat.shape[0]
    padded = -(-count // (8 * LANES)) * 8 * LANES
    flat = jnp.pad(flat, (0, padded - count)).reshape(-1, LANES)
    whole = lax.all_gather(flat, AXES, axis=0, tiled=False).reshape(DEVICES, padded)
    outs, start = [], 0
    for piece, dim in pieces:
        part = whole[:, start : start + piece.size].reshape((DEVICES,) + piece.shape)
        start += piece.size
        part = jnp.moveaxis(part, 0, dim)
        outs.append(
            part.reshape(piece.shape[:dim] + (DEVICES * piece.shape[dim],) + piece.shape[dim + 1 :])
        )
    return outs


def take(value, index, dim):
    return lax.squeeze(lax.dynamic_slice_in_dim(value, index, 1, dim), (dim,))


def shift(value, axis, forward):
    pairs = []
    for place in range(4):
        for core in range(2):
            step = 1 if (core == 0) == forward else -1
            pairs.append((place * 2 + core, ((place + step) % 4) * 2 + core))
    return lax.ppermute(value, (axis, "c"), pairs)


def ring_scatter(value, axis, dim):
    place, step = lax.axis_index(axis), 1 - 2 * lax.axis_index("c")
    far = shift(take(value, (place + 2) % 4, dim), axis, True)
    behind = shift(take(value, (place - step) % 4, dim), axis, False)
    ahead = take(value, (place + step) % 4, dim).astype(jnp.float32) + far.astype(jnp.float32)
    ahead = shift(ahead.astype(jnp.bfloat16), axis, True)
    own = take(value, place, dim).astype(jnp.float32)
    return (own + behind.astype(jnp.float32) + ahead.astype(jnp.float32)).astype(jnp.bfloat16)


def reduce_packed(packed):
    core = lax.axis_index("c")
    swapped = lax.ppermute(take(packed, 1 - core, 3), "c", [(0, 1), (1, 0)])
    both = take(packed, core, 3).astype(jnp.float32) + swapped.astype(jnp.float32)
    both = both.astype(jnp.bfloat16)
    third = both.shape[3] // 3
    one, two, three = (both[..., i * third : (i + 1) * third, :] for i in range(3))
    one, two, three = ring_scatter(one, "x", 2), ring_scatter(two, "y", 0), ring_scatter(three, "z", 1)
    one, two, three = ring_scatter(one, "y", 0), ring_scatter(two, "z", 0), ring_scatter(three, "x", 1)
    one, two, three = ring_scatter(one, "z", 0), ring_scatter(two, "x", 0), ring_scatter(three, "y", 0)
    return jnp.concatenate([one, two, three], 0)


def scatter_grads(*pieces):
    parts = []
    for piece, dim in pieces:
        shape = piece.shape
        split = piece.reshape(shape[:dim] + (DEVICES, shape[dim] // DEVICES) + shape[dim + 1 :])
        parts.append(jnp.moveaxis(split, dim, 0).reshape(DEVICES, -1).astype(jnp.bfloat16))
    flat = jnp.concatenate(parts, 1)
    count = flat.shape[1]
    padded = -(-count // (24 * LANES)) * 24 * LANES
    flat = jnp.pad(flat, ((0, 0), (0, padded - count))).reshape(4, 4, 4, 2, -1, LANES)
    mine = reduce_packed(flat).reshape(-1)
    outs, start = [], 0
    for piece, dim in pieces:
        shape = piece.shape[:dim] + (piece.shape[dim] // DEVICES,) + piece.shape[dim + 1 :]
        size = math.prod(shape)
        outs.append(mine[start : start + size].reshape(shape).astype(jnp.float32))
        start += size
    return outs


def product(left_arr, right_arr):
    return jnp.dot(left_arr, right_arr, preferred_element_type=jnp.float32)


def product_t(left_arr, right_arr):
    return lax.dot_general(
        left_arr, right_arr, (((0,), (0,)), ((), ())), preferred_element_type=jnp.float32
    )


def product_nt(left_arr, right_arr):
    return lax.dot_general(
        left_arr, right_arr, (((1,), (1,)), ((), ())), preferred_element_type=jnp.float32
    )


def rounded(value):
    return lax.optimization_barrier(value.astype(jnp.bfloat16)).astype(jnp.float32)


def gelu_exact(value):
    return jax.nn.gelu(value, approximate=False)


def norm_forward(hidden, gain_vec, shift_vec):
    centred = hidden - jnp.mean(hidden, axis=-1, keepdims=True)
    inverse = lax.rsqrt(jnp.mean(centred * centred, axis=-1, keepdims=True) + eps)
    unit_value = centred * inverse
    return (unit_value * gain_vec + shift_vec, unit_value, inverse)


def norm_backward(grad_norm, unit_value, inverse, gain_vec):
    grad_unit = grad_norm * gain_vec
    grad_in = inverse * (
        grad_unit
        - jnp.mean(grad_unit, axis=-1, keepdims=True)
        - unit_value * jnp.mean(grad_unit * unit_value, axis=-1, keepdims=True)
    )
    return (grad_in, jnp.sum(grad_norm * unit_value, axis=0), jnp.sum(grad_norm, axis=0))


def attend(normed, projection, out_proj, biases, shape_heads, score_scale, key_mask, einsum_forms):
    queries = (product(normed, projection[0]) + biases[0]).astype(jnp.bfloat16).reshape(shape_heads)
    key_act = product(normed, projection[1]).astype(jnp.bfloat16).reshape(shape_heads)
    value_act = (
        (product(normed, projection[2]) + biases[1]).astype(jnp.bfloat16).reshape(shape_heads)
    )
    scores = (
        jnp.einsum(einsum_forms[0], queries, key_act, preferred_element_type=jnp.float32)
        * score_scale
    )
    if key_mask is not None:
        scores = jnp.where(key_mask, scores, -1e30)
    softmax_out = jax.nn.softmax(scores, axis=-1)
    softmax_low = softmax_out.astype(jnp.bfloat16)
    mixed_heads = jnp.einsum(
        einsum_forms[1], softmax_low, value_act, preferred_element_type=jnp.float32
    )
    mixed_heads = mixed_heads.astype(jnp.bfloat16).reshape(normed.shape)
    branch = product(mixed_heads, out_proj) + biases[2]
    return (branch, (queries, key_act, value_act, softmax_out, softmax_low, mixed_heads))


def attend_back(grad_branch, normed, projection, out_proj, saved_state, score_scale, einsum_forms):
    queries, key_act, value_act, softmax_out, softmax_low, mixed_heads = saved_state
    grad_low = grad_branch.astype(jnp.bfloat16)
    out_grad = product_t(mixed_heads, grad_low)
    grad_mixed = product_nt(grad_low, out_proj).astype(jnp.bfloat16).reshape(queries.shape)
    grad_soft = jnp.einsum(
        einsum_forms[0], grad_mixed, value_act, preferred_element_type=jnp.float32
    )
    grad_value = jnp.einsum(
        einsum_forms[2], softmax_low, grad_mixed, preferred_element_type=jnp.float32
    )
    grad_value = grad_value.astype(jnp.bfloat16).reshape(normed.shape)
    grad_scores = softmax_out * (
        grad_soft - jnp.sum(grad_soft * softmax_out, axis=-1, keepdims=True)
    )
    grad_scores = grad_scores.astype(jnp.bfloat16)
    grad_query = (
        jnp.einsum(einsum_forms[1], grad_scores, key_act, preferred_element_type=jnp.float32)
        * score_scale
    )
    grad_query = grad_query.astype(jnp.bfloat16).reshape(normed.shape)
    grad_key = (
        jnp.einsum(einsum_forms[2], grad_scores, queries, preferred_element_type=jnp.float32)
        * score_scale
    )
    grad_key = grad_key.astype(jnp.bfloat16).reshape(normed.shape)
    proj_grad = jnp.stack(
        [product_t(normed, grad_query), product_t(normed, grad_key), product_t(normed, grad_value)]
    )
    bias_grad = jnp.stack(
        [
            jnp.sum(grad_query.astype(jnp.float32), axis=0),
            jnp.sum(grad_value.astype(jnp.float32), axis=0),
            jnp.sum(grad_low.astype(jnp.float32), axis=0),
        ]
    )
    grad_normed = (
        product_nt(grad_query, projection[0])
        + product_nt(grad_key, projection[1])
        + product_nt(grad_value, projection[2])
    )
    return (grad_normed, proj_grad, out_grad, bias_grad)


def on_device(
    tokens,
    cotangent,
    lengths,
    row_offset,
    col_offset,
    norm_gain,
    norm_bias,
    row_qkv,
    row_out,
    row_bias,
    col_qkv,
    col_out,
    col_bias,
    ffn_up,
    up_bias,
    ffn_down,
    down_bias,
    pos_tables,
):
    row_count, col_count, model_width = (tokens.shape[1], tokens.shape[2], tokens.shape[3])
    token_count = row_count * col_count
    shape_heads = (row_count, col_count, HEADS, HEAD_DIM)
    row_scale = 1.0 / math.sqrt(HEAD_DIM * row_count)
    col_scale = 1.0 / math.sqrt(HEAD_DIM)
    (
        norm_gains,
        norm_shifts,
        row_proj,
        row_output,
        row_biases,
        col_proj,
        col_output,
        col_biases,
        up_weight,
        up_biases,
        down_weight,
        down_biases,
        tables,
    ) = gather_weights(
        (norm_gain, 1),
        (norm_bias, 1),
        (row_qkv, 1),
        (row_out, 0),
        (row_bias, 1),
        (col_qkv, 1),
        (col_out, 0),
        (col_bias, 1),
        (ffn_up, 0),
        (up_bias, 0),
        (ffn_down, 0),
        (down_bias, 0),
        (pos_tables, 1),
    )
    gain_rows = norm_gains.astype(jnp.float32)
    shift_rows = norm_shifts.astype(jnp.float32)
    key_mask = jnp.arange(col_count)[None, None, :] < lengths[0]
    valid_cols = (jnp.arange(col_count) < lengths[0]).astype(jnp.float32)
    token_start = tokens[0].astype(jnp.float32)
    row_pos = lax.dynamic_slice_in_dim(tables[0], row_offset[0], row_count, 0).astype(jnp.float32)
    col_pos = lax.dynamic_slice_in_dim(tables[1], col_offset[0], col_count, 0).astype(jnp.float32)
    hidden_in = (token_start + row_pos[:, None, :] + col_pos[None, :, :]).reshape(
        token_count, model_width
    )
    normed_one, unit_one, inverse_one = norm_forward(hidden_in, gain_rows[0], shift_rows[0])
    normed_one = normed_one.astype(jnp.bfloat16)
    row_branch, row_saved = attend(
        normed_one, row_proj, row_output, row_biases, shape_heads, row_scale, key_mask, row_forms
    )
    hidden_mid = hidden_in + row_branch
    normed_two, unit_two, inverse_two = norm_forward(hidden_mid, gain_rows[1], shift_rows[1])
    normed_two = normed_two.astype(jnp.bfloat16)
    col_branch, col_saved = attend(
        normed_two, col_proj, col_output, col_biases, shape_heads, col_scale, None, col_forms
    )
    hidden_late = hidden_mid + col_branch
    normed_three, unit_three, inverse_three = norm_forward(hidden_late, gain_rows[2], shift_rows[2])
    normed_three = normed_three.astype(jnp.bfloat16)
    pre_act = product(normed_three, up_weight) + up_biases
    act_value, gelu_back = jax.vjp(gelu_exact, pre_act)
    act_low = act_value.astype(jnp.bfloat16)
    hidden_out = hidden_late + product(act_low, down_weight) + down_biases
    activations = hidden_out.reshape(tokens.shape).astype(jnp.bfloat16)
    grad_out = (cotangent[0].astype(jnp.float32) * valid_cols[None, :, None]).reshape(
        token_count, model_width
    )
    grad_low = grad_out.astype(jnp.bfloat16)
    down_grad = product_t(act_low, grad_low)
    down_bias_grad = jnp.sum(grad_low.astype(jnp.float32), axis=0)
    grad_act = rounded(product_nt(grad_low, down_weight))
    grad_pre = gelu_back(grad_act)[0].astype(jnp.bfloat16)
    up_grad = product_t(normed_three, grad_pre)
    up_bias_grad = jnp.sum(grad_pre.astype(jnp.float32), axis=0)
    grad_in_three, gain_grad_three, shift_grad_three = norm_backward(
        product_nt(grad_pre, up_weight), unit_three, inverse_three, gain_rows[2]
    )
    grad_late = grad_out + grad_in_three
    grad_col_normed, col_proj_grad, col_output_grad, col_bias_grad = attend_back(
        grad_late, normed_two, col_proj, col_output, col_saved, col_scale, col_forms
    )
    grad_in_two, gain_grad_two, shift_grad_two = norm_backward(
        grad_col_normed, unit_two, inverse_two, gain_rows[1]
    )
    grad_mid = grad_late + grad_in_two
    grad_row_normed, row_proj_grad, row_output_grad, row_bias_grad = attend_back(
        grad_mid, normed_one, row_proj, row_output, row_saved, row_scale, row_forms
    )
    grad_in_one, gain_grad_one, shift_grad_one = norm_backward(
        grad_row_normed, unit_one, inverse_one, gain_rows[0]
    )
    grad_input = grad_mid + grad_in_one
    grid_grad = grad_input.reshape(row_count, col_count, model_width)
    zero_table = jnp.zeros((POSITIONS, model_width), jnp.float32)
    table_grad = jnp.stack(
        [
            lax.dynamic_update_slice_in_dim(
                zero_table, jnp.sum(grid_grad, axis=1), row_offset[0], 0
            ),
            lax.dynamic_update_slice_in_dim(
                zero_table, jnp.sum(grid_grad, axis=0), col_offset[0], 0
            ),
        ]
    )
    gain_grad = jnp.stack([gain_grad_one, gain_grad_two, gain_grad_three])
    shift_grad = jnp.stack([shift_grad_one, shift_grad_two, shift_grad_three])
    (
        gain_grad,
        shift_grad,
        row_proj_grad,
        row_output_grad,
        row_bias_grad,
        col_proj_grad,
        col_output_grad,
        col_bias_grad,
        up_grad,
        up_bias_grad,
        down_grad,
        down_bias_grad,
        table_grad,
    ) = scatter_grads(
        (gain_grad, 1),
        (shift_grad, 1),
        (row_proj_grad, 1),
        (row_output_grad, 0),
        (row_bias_grad, 1),
        (col_proj_grad, 1),
        (col_output_grad, 0),
        (col_bias_grad, 1),
        (up_grad, 0),
        (up_bias_grad, 0),
        (down_grad, 0),
        (down_bias_grad, 0),
        (table_grad, 1),
    )
    tokens_grad = grad_input.reshape(tokens.shape)
    return (
        activations,
        tokens_grad,
        gain_grad,
        shift_grad,
        row_proj_grad,
        row_output_grad,
        row_bias_grad,
        col_proj_grad,
        col_output_grad,
        col_bias_grad,
        up_grad,
        up_bias_grad,
        down_grad,
        down_bias_grad,
        table_grad,
    )


def solution(mesh):
    mesh = Mesh(mesh.devices.reshape(4, 4, 4, 2), AXES)
    in_specs = (
        P(AXES, None, None, None),
        P(AXES, None, None, None),
        P(AXES),
        P(AXES),
        P(AXES),
        P(None, AXES),
        P(None, AXES),
        P(None, AXES, None),
        P(AXES, None),
        P(None, AXES),
        P(None, AXES, None),
        P(AXES, None),
        P(None, AXES),
        P(AXES, None),
        P(AXES),
        P(AXES, None),
        P(AXES),
        P(None, AXES, None),
    )
    out_specs = (
        P(AXES, None, None, None),
        P(AXES, None, None, None),
        P(None, AXES),
        P(None, AXES),
        P(None, AXES, None),
        P(AXES, None),
        P(None, AXES),
        P(None, AXES, None),
        P(AXES, None),
        P(None, AXES),
        P(AXES, None),
        P(AXES),
        P(AXES, None),
        P(AXES),
        P(None, AXES, None),
    )
    return jax.shard_map(
        on_device, mesh=mesh, in_specs=in_specs, out_specs=out_specs, check_vma=False
    )
```

```python
import math

import jax
import jax.numpy as jnp
from jax import lax
from jax.experimental import pallas as pl
from jax.experimental.pallas import tpu as pltpu
from jax.sharding import Mesh, PartitionSpec as P

AXES = ("y", "z", "x", "c")
DEVICES = 128
GROUPS = 32
MEMBERS = 4
D = 768
FF = 3072
HEAD_DIM = 64
POSITIONS = 1024
ROWS = 8
COLS = 64
TOKENS = ROWS * COLS
SLAB = 24
PACK = 112
PAIRS = 6
EPS = 1e-05
MASKED = -1e30
ROW_SCALE = 1.0 / math.sqrt(HEAD_DIM * ROWS)
COL_SCALE = 1.0 / math.sqrt(HEAD_DIM)
BF16 = jnp.bfloat16
F32 = jnp.float32
GAIN, SHIFT, ROW_BIAS, COL_BIAS, DOWN_BIAS = 0, 3, 6, 9, 12
A1, Q1, K1, V1, M1, A2, Q2, K2, V2, M2 = range(10)


def dot(left, right):
    return jnp.dot(left, right, preferred_element_type=F32)


def dot_nt(left, right):
    return lax.dot_general(left, right, (((1,), (1,)), ((), ())), preferred_element_type=F32)


def dot_tn(left, right):
    return lax.dot_general(left, right, (((0,), (0,)), ((), ())), preferred_element_type=F32)


def chunk(index, size):
    return pl.ds(pl.multiple_of(index * size, size), size)


def loop(count, body, unroll=1):
    def step(index, carry):
        body(index)
        return carry

    lax.fori_loop(0, count, step, 0, unroll=unroll)


def unit_of(hidden):
    centred = hidden - jnp.mean(hidden, axis=-1, keepdims=True)
    inverse = lax.rsqrt(jnp.mean(centred * centred, axis=-1, keepdims=True) + EPS)
    return centred * inverse, inverse


def norm(hidden, small, which):
    unit, _ = unit_of(hidden)
    gain, shift = small[GAIN + which : GAIN + which + 1, :], small[SHIFT + which : SHIFT + which + 1, :]
    return (unit * gain + shift).astype(BF16)


def norm_back(grad, hidden, gain):
    unit, inverse = unit_of(hidden)
    inner = grad * gain
    mean = jnp.mean(inner, axis=-1, keepdims=True)
    cross = jnp.mean(inner * unit, axis=-1, keepdims=True)
    return inverse * (inner - mean - unit * cross), grad * unit


def total(value):
    return jnp.sum(value, axis=0, keepdims=True)


def first_head(shape):
    return (lax.broadcasted_iota(jnp.int32, shape, 1) & 127) < HEAD_DIM


def stack_heads(value):
    keep = jnp.where(first_head(value.shape), 1.0, 0.0)
    return jnp.concatenate([value * keep.astype(BF16), value * (1.0 - keep).astype(BF16)], axis=0)


def merge_heads(value):
    half = value.shape[0] // 2
    return jnp.where(first_head((half, value.shape[1])), value[:half], value[half:])


def softmax(scores):
    top = jnp.max(scores, axis=-1, keepdims=True)
    raised = jnp.exp(scores - top)
    return raised / jnp.sum(raised, axis=-1, keepdims=True)


class RowHeads:
    count = PAIRS
    unroll = 2

    def __init__(self, length):
        self.length = length

    def load(self, ref, plane, index):
        lanes = chunk(index, 128)
        return jnp.concatenate(
            [ref[plane, r * COLS : (r + 1) * COLS, lanes] for r in range(ROWS)], axis=1
        )

    def store(self, ref, plane, index, value):
        lanes = chunk(index, 128)
        for r in range(ROWS):
            ref[plane, r * COLS : (r + 1) * COLS, lanes] = value[:, r * 128 : (r + 1) * 128]

    def weights(self, queries, keys):
        scores = dot_nt(queries, keys) * ROW_SCALE
        live = lax.broadcasted_iota(jnp.int32, scores.shape, 1) < self.length
        return softmax(jnp.where(live, scores, MASKED))

    scale = ROW_SCALE


class ColHeads:
    count = 4 * PAIRS
    unroll = 2

    def load(self, ref, plane, index):
        lanes = chunk(index // 4, 128)
        return jnp.concatenate(
            [ref[plane, self.rows(index, r), lanes] for r in range(ROWS)], axis=0
        )

    def rows(self, index, r):
        return pl.ds(pl.multiple_of(r * COLS + (index % 4) * 16, 16), 16)

    def store(self, ref, plane, index, value):
        lanes = chunk(index // 4, 128)
        for r in range(ROWS):
            ref[plane, self.rows(index, r), lanes] = value[16 * r : 16 * r + 16]

    def weights(self, queries, keys):
        scores = dot_nt(queries, keys) * COL_SCALE
        row = lax.broadcasted_iota(jnp.int32, scores.shape, 0) & 15
        same = row == (lax.broadcasted_iota(jnp.int32, scores.shape, 1) & 15)
        return softmax(jnp.where(same, scores, MASKED))

    scale = COL_SCALE


def attend(heads, ref, q, k, v, m):
    def body(index):
        probs = heads.weights(stack_heads(heads.load(ref, q, index)), heads.load(ref, k, index))
        mixed = merge_heads(dot(probs.astype(BF16), heads.load(ref, v, index)))
        heads.store(ref, m, index, mixed.astype(BF16))

    loop(heads.count, body, heads.unroll)


def attend_back(heads, ref, q, k, v, dm):
    def body(index):
        queries = stack_heads(heads.load(ref, q, index))
        keys, values = heads.load(ref, k, index), heads.load(ref, v, index)
        mixed = stack_heads(heads.load(ref, dm, index))
        probs = heads.weights(queries, keys)
        grad = dot_nt(mixed, values)
        grad_values = dot_tn(probs.astype(BF16), mixed)
        inner = probs * (grad - jnp.sum(grad * probs, axis=-1, keepdims=True))
        inner = inner.astype(BF16)
        grad_queries = merge_heads(dot(inner, keys)) * heads.scale
        grad_keys = dot_tn(inner, queries) * heads.scale
        heads.store(ref, q, index, grad_queries.astype(BF16))
        heads.store(ref, k, index, grad_keys.astype(BF16))
        heads.store(ref, v, index, grad_values.astype(BF16))

    loop(heads.count, body, heads.unroll)


def whole(ref, index):
    return ref[index].reshape(D, D)


def project(ref, source, planes, weights, first, small, bias_row):
    def body(index):
        rows = chunk(index, 256)
        normed = ref[source, rows, :]
        for i, plane in enumerate(planes):
            value = dot(normed, whole(weights, first + i))
            if i != 1:
                row = bias_row + (0 if i == 0 else 1)
                value = value + small[row : row + 1, :]
            ref[plane, rows, :] = value.astype(BF16)

    loop(2, body)


class Copies:
    def __init__(self, sems):
        self.sems, self.used = sems, 0

    def start(self, source, target):
        copy = pltpu.make_async_copy(source, target, self.sems.at[self.used])
        self.used += 1
        copy.start()
        return copy

    def send(self, core, parity, source, own, other):
        sem = self.sems.at[self.used]
        self.used += 1
        here = pltpu.make_async_copy(source, own, sem)
        there = pltpu.make_async_copy(source, other, sem)
        pl.when(core == parity)(here.start)
        pl.when(core != parity)(there.start)
        return here


def position_rows(window, offset, count):
    shape = (count, window.shape[0])
    pick = lax.broadcasted_iota(jnp.int32, shape, 1) == (
        lax.broadcasted_iota(jnp.int32, shape, 0) + offset % 8
    )
    return dot(jnp.where(pick, 1.0, 0.0).astype(BF16), window)


def forward_kernel(
    ints, tokens, cotangent, small, up_bias, gathered,
    act_out, g2_out, saved_out, hidden_out, own, other, sums,
    weights, down, window, act, hidden, h2, a3, gy, wide, y, da, sems,
):
    grads = weights
    length, row_offset, col_offset, core = ints[0], ints[1], ints[2], ints[3]
    copies = Copies(sems)
    near = []
    for i in range(2):
        dev = jnp.minimum(row_offset // 8 + i, DEVICES - 1)
        near.append(
            copies.start(gathered.at[dev // 4, dev % 4, 96:104, :], window.at[8 * i : 8 * i + 8, :])
        )
    for i in range(9):
        dev = jnp.minimum(col_offset // 8 + i, DEVICES - 1)
        near.append(
            copies.start(
                gathered.at[dev // 4, dev % 4, 104:112, :], window.at[16 + 8 * i : 24 + 8 * i, :]
            )
        )
    loads = [
        copies.start(gathered.at[:, i % 4, 24 * (i // 4) : 24 * (i // 4) + 24, :], weights.at[i])
        for i in range(12)
    ]
    loads += [
        copies.start(gathered.at[8 * f : 8 * f + 8, :, 72:96, :], down.at[f]) for f in range(4)
    ]
    for copy in near:
        copy.wait()
    row_pos = position_rows(window[0:16, :], row_offset, ROWS)
    col_pos = position_rows(window[16:88, :], col_offset, COLS)
    for r in range(ROWS):
        rows = slice(r * COLS, (r + 1) * COLS)
        value = tokens[rows, :].astype(F32) + row_pos[r : r + 1, :] + col_pos
        hidden[0, rows, :] = value
        act[A1, rows, :] = norm(value, small, 0)
    stores = [copies.start(hidden.at[0], hidden_out.at[0]), copies.start(act.at[A1], saved_out.at[A1])]

    def branch(first, source, planes, heads, bias, target, which, last):
        for i in range(3):
            loads[first + i].wait()
        project(act, source, planes[:3], weights, first, small, bias)
        for plane in planes[:3]:
            stores.append(copies.start(act.at[plane], saved_out.at[plane]))
        attend(heads, act, *planes)
        stores.append(copies.start(act.at[planes[3]], saved_out.at[planes[3]]))
        loads[first + 3].wait()

        def body(index):
            rows = chunk(index, 256)
            branch_out = dot(act[planes[3], rows, :], whole(weights, first + 3))
            before = hidden[which - 1, rows, :]
            after = before + (branch_out + small[bias + 2 : bias + 3, :])
            if last:
                h2[rows, :] = after
                a3[rows, :] = norm(after, small, which)
            else:
                hidden[which, rows, :] = after
                act[target, rows, :] = norm(after, small, which)

        loop(2, body)

    branch(0, A1, (Q1, K1, V1, M1), RowHeads(length), ROW_BIAS, A2, 1, False)
    stores.append(copies.start(hidden.at[1], hidden_out.at[1]))
    stores.append(copies.start(act.at[A2], saved_out.at[A2]))
    branch(4, A2, (Q2, K2, V2, M2), ColHeads(), COL_BIAS, None, 2, True)

    in_use = lax.broadcasted_iota(jnp.int32, (COLS, D), 0) < length
    for r in range(ROWS):
        rows = slice(r * COLS, (r + 1) * COLS)
        gy[rows, :] = jnp.where(in_use, cotangent[rows, :].astype(F32), 0.0).astype(BF16)
    for copy in loads[8:]:
        copy.wait()

    def ffn(f):
        up, low = whole(weights, 8 + f), down[f].reshape(D, D)
        bias = up_bias[pl.ds(f, 1), :]

        def body(index):
            rows = chunk(index, 256)
            z = dot(a3[rows, :], up) + bias
            cdf = 0.5 * (1.0 + lax.erf(z * math.sqrt(0.5)))
            slope = cdf + z * (jnp.exp(-0.5 * z * z) * (1.0 / math.sqrt(2.0 * math.pi)))
            u = (z * cdf).astype(BF16)
            wide[0, rows, :] = u
            du = dot_nt(gy[rows, :], low).astype(BF16).astype(F32)
            dz = (du * slope).astype(BF16)
            wide[1, rows, :] = dz
            more, more_da = dot(u, low), dot_nt(dz, up)

            @pl.when(f == 0)
            def _():
                y[rows, :] = more
                da[rows, :] = more_da

            @pl.when(f != 0)
            def _():
                y[rows, :] += more
                da[rows, :] += more_da

        loop(2, body)
        sums[pl.ds(f, 1), :] = total(wide[1].astype(F32))

        def back(index):
            cols = chunk(index, 384)
            value = dot_tn(wide[0, :, cols], gy[...]).astype(BF16).reshape(4, 4, SLAB, D)
            for m in range(MEMBERS):
                grads[4 + f, pl.ds(8 * m + 4 * index, 4)] = value[:, m]
            value = dot_tn(a3[:, cols], wide[1]).astype(BF16).reshape(16, SLAB, D)
            grads[f, chunk(index, 16)] = value

        loop(2, back)

    loop(4, ffn)
    sends = []
    for f in range(4):
        sends.append(
            copies.send(
                core, f % 2, grads.at[f],
                own.at[:, f // 2, 0:SLAB, :], other.at[:, f // 2, 0:SLAB, :],
            )
        )
        for m in range(MEMBERS):
            place = (slice(8 * f, 8 * f + 8), m // 2, slice(SLAB, 2 * SLAB))
            sends.append(
                copies.send(
                    core, m % 2, grads.at[4 + f, 8 * m : 8 * m + 8], own.at[place], other.at[place]
                )
            )

    gain = small[GAIN + 2 : GAIN + 3, :]

    def finish(index, carry):
        rows = chunk(index, 64)
        late = h2[rows, :]
        act_out[rows, :] = (late + (y[rows, :] + small[DOWN_BIAS : DOWN_BIAS + 1, :])).astype(BF16)
        grad = da[rows, :]
        inner, unit = norm_back(grad, late, gain)
        cot = gy[rows, :].astype(F32)
        g2_out[rows, :] = cot + inner
        return carry[0] + total(unit), carry[1] + total(grad), carry[2] + total(cot)

    zero = jnp.zeros((1, D), F32)
    gain_sum, shift_sum, down_sum = lax.fori_loop(0, 8, finish, (zero, zero, zero))
    sums[4:5, :] = down_sum
    sums[5:6, :] = gain_sum
    sums[6:7, :] = shift_sum
    sums[7:8, :] = zero
    for copy in stores + sends:
        copy.wait()


def back_kernel(column, *refs):
    if column:
        (ints, grad_in, small, gathered, saved, hidden_saved,
         grad_out, own, other, sums,
         weights, act, hidden, da, grads, sems) = refs
        first, which, bias, planes = 24, 1, COL_BIAS, (A2, Q2, K2, V2, M2)
        heads = ColHeads()
    else:
        (ints, grad_in, small, gathered, saved, hidden_saved,
         grad_out, own, other, sums,
         weights, act, hidden, da, grads, zeros, table, lines, sems) = refs
        first, which, bias, planes = 0, 0, ROW_BIAS, (A1, Q1, K1, V1, M1)
        heads = RowHeads(ints[0])
    core = ints[3]
    copies = Copies(sems)
    out_load = copies.start(gathered.at[:, 3, first : first + SLAB, :], weights.at[3])
    act_loads = [copies.start(saved.at[plane], act.at[i]) for i, plane in enumerate(planes)]
    loads = [
        copies.start(gathered.at[:, i, first : first + SLAB, :], weights.at[i]) for i in range(3)
    ]
    hidden_load = copies.start(hidden_saved.at[which], hidden)
    sends = []
    if not column:
        zeros[...] = jnp.zeros_like(zeros)
        fills = [copies.start(zeros, out.at[:, :, 144:240, :]) for out in (own, other)]

    def send(member):
        if column:
            place = (slice(None), member // 2)
            sends.append(
                copies.send(core, member % 2, grads.at[member], own.at[place], other.at[place])
            )
            return
        for t in range(6):
            place = (slice(None), member // 2, slice(SLAB * t, SLAB * t + SLAB))
            lanes = slice(128 * t, 128 * t + 128)
            sends.append(
                copies.send(
                    core, member % 2, grads.at[member, :, :, lanes], own.at[place], other.at[place]
                )
            )

    def low(index, carry):
        rows = chunk(index, 64)
        value = grad_in[rows, :].astype(BF16)
        act[5, rows, :] = value
        return carry + total(value.astype(F32))

    out_sum = lax.fori_loop(0, 8, low, jnp.zeros((1, D), F32))
    for copy in act_loads:
        copy.wait()
    out_load.wait()

    def out_back(index):
        cols = chunk(index, 384)
        value = dot_tn(act[4, :, cols], act[5]).astype(BF16)
        grads[3, chunk(index, 16)] = value.reshape(16, SLAB, D)

    loop(2, out_back)
    send(3)

    def mixed_back(index):
        rows = chunk(index, 256)
        act[4, rows, :] = dot_nt(act[5, rows, :], whole(weights, 3)).astype(BF16)

    loop(2, mixed_back)
    attend_back(heads, act, 1, 2, 3, 4)
    for copy in loads:
        copy.wait()

    def weight_back(index):
        which_weight, half = index // 2, index % 2
        cols = chunk(half, 384)
        value = dot_tn(act[0, :, cols], act[1 + which_weight]).astype(BF16)
        grads[which_weight, chunk(half, 16)] = value.reshape(16, SLAB, D)

    loop(6, weight_back)
    for member in range(3):
        send(member)

    def input_back(index):
        rows = chunk(index, 256)
        value = dot_nt(act[1, rows, :], whole(weights, 0))
        value = value + dot_nt(act[2, rows, :], whole(weights, 1))
        da[rows, :] = value + dot_nt(act[3, rows, :], whole(weights, 2))

    loop(2, input_back)
    hidden_load.wait()
    gain = small[GAIN + which : GAIN + which + 1, :]

    def finish(index, carry):
        rows = chunk(index, 64)
        grad = da[rows, :]
        inner, unit = norm_back(grad, hidden[rows, :], gain)
        value = grad_in[rows, :] + inner
        grad_out[rows, :] = value
        if not column:
            lines[pl.ds(index, 1), :] = total(value)
        extra = (total(act[1, rows, :].astype(F32)), total(act[3, rows, :].astype(F32)))
        added = (total(unit), total(grad)) + extra
        return tuple(a + b for a, b in zip(carry[:4], added)) + ((carry[4] + value,) if not column else ())

    carry = (jnp.zeros((1, D), F32),) * 4
    if not column:
        carry = carry + (jnp.zeros((COLS, D), F32),)
    carry = lax.fori_loop(0, 8, finish, carry)
    for i, value in enumerate(carry[:4] + (out_sum,)):
        sums[i : i + 1, :] = value
    sums[5:8, :] = jnp.zeros((3, D), F32)
    if not column:
        send_tables(ints, copies, fills, lines[...], carry[4], table, own, other)
    for copy in sends:
        copy.wait()


def send_tables(ints, copies, fills, row_lines, col_lines, table, own, other):
    core = ints[3]

    def placed(values, offset, count):
        shape = (count, values.shape[0])
        here = lax.broadcasted_iota(jnp.int32, shape, 0) == (
            lax.broadcasted_iota(jnp.int32, shape, 1) + offset % 8
        )
        return dot(jnp.where(here, 1.0, 0.0).astype(BF16), values.astype(BF16)).astype(BF16)

    spots = []
    for first, count, values, offset, start in (
        (0, 2, row_lines, ints[1], 144),
        (2, 9, col_lines, ints[2], 192),
    ):
        aligned = placed(values, offset, 8 * count).reshape(count, 8, D)
        for t in range(6):
            table[first : first + count, 8 * t : 8 * t + 8, :] = aligned[:, :, 128 * t : 128 * t + 128]
        spots += [(first + i, offset // 8 + i, start) for i in range(count)]
    for copy in fills:
        copy.wait()
    waits = []
    for slot, owner, start in spots:
        real, dev = owner < DEVICES, jnp.minimum(owner, DEVICES - 1)
        place = (dev // 4, (dev % 4) // 2, slice(start, start + 48))
        sem = copies.sems.at[copies.used]
        copies.used += 1
        here = pltpu.make_async_copy(table.at[slot], own.at[place], sem)
        there = pltpu.make_async_copy(table.at[slot], other.at[place], sem)
        pl.when(real & (dev % 2 == core))(here.start)
        pl.when(real & (dev % 2 != core))(there.start)
        waits.append((real, here))
    for real, copy in waits:
        pl.when(real)(copy.wait)


VMEM = pl.BlockSpec(memory_space=pltpu.VMEM)
ANY = pl.BlockSpec(memory_space=pl.ANY)
SMEM = pl.BlockSpec(memory_space=pltpu.SMEM)
SHAPE = jax.ShapeDtypeStruct


def params():
    return pltpu.CompilerParams(vmem_limit_bytes=62 * 1024 * 1024)


def cost(flops, traffic):
    return pl.CostEstimate(flops=flops, transcendentals=0, bytes_accessed=traffic)


def forward_call(ints, tokens, cotangent, small, up_bias, gathered):
    plane = (TOKENS, D)
    return pl.pallas_call(
        forward_kernel,
        name="forward",
        in_specs=[SMEM, VMEM, VMEM, VMEM, VMEM, ANY],
        out_shape=(
            SHAPE(plane, BF16),
            SHAPE(plane, F32),
            SHAPE((10,) + plane, BF16),
            SHAPE((2,) + plane, F32),
            SHAPE((GROUPS, 2, 2 * SLAB, D), BF16),
            SHAPE((GROUPS, 2, 2 * SLAB, D), BF16),
            SHAPE((8, D), F32),
        ),
        out_specs=(VMEM, VMEM, ANY, ANY, ANY, ANY, VMEM),
        scratch_shapes=[
            pltpu.VMEM((12, GROUPS, SLAB, D), BF16),
            pltpu.VMEM((4, 8, MEMBERS, SLAB, D), BF16),
            pltpu.VMEM((88, D), BF16),
            pltpu.VMEM((10,) + plane, BF16),
            pltpu.VMEM((2,) + plane, F32),
            pltpu.VMEM(plane, F32),
            pltpu.VMEM(plane, BF16),
            pltpu.VMEM(plane, BF16),
            pltpu.VMEM((2,) + plane, BF16),
            pltpu.VMEM(plane, F32),
            pltpu.VMEM(plane, F32),
            pltpu.SemaphoreType.DMA((64,)),
        ],
        compiler_params=params(),
        cost_estimate=cost(24 * 10**9, 50 * 10**6),
    )(ints, tokens, cotangent, small, up_bias, gathered)


def back_call(column, ints, grad, small, gathered, saved, hidden):
    plane = (TOKENS, D)
    share = (GROUPS, 2, SLAB, D) if column else (GROUPS, 2, 240, 128)
    scratch = [
        pltpu.VMEM((4, GROUPS, SLAB, D), BF16),
        pltpu.VMEM((6,) + plane, BF16),
        pltpu.VMEM(plane, F32),
        pltpu.VMEM(plane, F32),
        pltpu.VMEM((4, GROUPS, SLAB, D), BF16),
    ]
    if not column:
        scratch += [
            pltpu.VMEM((GROUPS, 2, 96, 128), BF16),
            pltpu.VMEM((11, 48, 128), BF16),
            pltpu.VMEM((ROWS, D), F32),
        ]
    return pl.pallas_call(
        lambda *refs: back_kernel(column, *refs),
        name="column_back" if column else "row_back",
        in_specs=[SMEM, VMEM, VMEM, ANY, ANY, ANY],
        out_shape=(SHAPE(plane, F32), SHAPE(share, BF16), SHAPE(share, BF16), SHAPE((8, D), F32)),
        out_specs=(VMEM, ANY, ANY, VMEM),
        scratch_shapes=scratch + [pltpu.SemaphoreType.DMA((64,))],
        compiler_params=params(),
        cost_estimate=cost(10 * 10**9, 20 * 10**6),
    )(ints, grad, small, gathered, saved, hidden)


def take(value, index, dim):
    return lax.squeeze(lax.dynamic_slice_in_dim(value, index, 1, dim), (dim,))


def add(*values):
    total_value = values[0].astype(F32)
    for value in values[1:]:
        total_value = total_value + value.astype(F32)
    return total_value.astype(BF16)


def exchange(blocks):
    me = (lax.axis_index("x") % 2) * 2 + lax.axis_index("c")
    parts = []
    for flip in range(4):
        part = take(blocks, me ^ flip, 0)
        if flip:
            pairs = [(i, (i // 4) * 4 + ((i % 4) ^ flip)) for i in range(8)]
            part = lax.ppermute(part, ("x", "c"), pairs)
        parts.append(part)
    odd, high = (me & 1) == 1, (me & 2) == 2
    pairs = [jnp.where(odd, parts[i ^ 1], parts[i]) for i in range(4)]
    return [jnp.where(high, pairs[i ^ 2], pairs[i]) for i in range(4)]


def shift(value, axis, forward):
    pairs = []
    for place in range(4):
        for core in range(2):
            step = 1 if (core == 0) == forward else -1
            pairs.append((place * 2 + core, ((place + step) % 4) * 2 + core))
    return lax.ppermute(value, (axis, "c"), pairs)


def ring_scatter(value, axis, dim):
    place, step = lax.axis_index(axis), 1 - 2 * lax.axis_index("c")
    far = shift(take(value, (place + 2) % 4, dim), axis, True)
    behind = shift(take(value, (place - step) % 4, dim), axis, False)
    ahead = shift(add(take(value, (place + step) % 4, dim), far), axis, True)
    return add(take(value, place, dim), behind, ahead)


def reduce_thirds(one, two, three):
    one, two, three = ring_scatter(one, "x", 2), ring_scatter(two, "y", 0), ring_scatter(three, "z", 1)
    one, two, three = ring_scatter(one, "y", 0), ring_scatter(two, "z", 0), ring_scatter(three, "x", 1)
    return ring_scatter(one, "z", 0), ring_scatter(two, "x", 0), ring_scatter(three, "y", 0)


def swap(value):
    return lax.ppermute(value, "c", [(0, 1), (1, 0)])


def reduce_shares(own, other, extra=None):
    both = add(own, swap(other))
    both = both.reshape((4, 4, 4) + both.shape[2:])
    third = both.shape[3] // 3
    parts = [both[..., i * third : (i + 1) * third, :] for i in range(3)]
    if extra is not None:
        parts[2] = jnp.concatenate([parts[2], extra], axis=3)
    return jnp.concatenate(reduce_thirds(*parts), axis=0)


def small_shares(*sums):
    sixes = jnp.concatenate([part[first:last] for part, first, last in sums[:-1]], axis=0)
    sixes = sixes.reshape(-1, DEVICES, 6).transpose(1, 0, 2).reshape(DEVICES, -1)
    values = jnp.concatenate([sixes, sums[-1].reshape(DEVICES, SLAB)], axis=1).astype(BF16)
    values = jnp.pad(values, ((0, 0), (0, 128 - values.shape[1]))).reshape(4, 4, 4, 2, 1, 128)
    core = lax.axis_index("c")
    both = add(take(values, core, 3), swap(take(values, 1 - core, 3)))
    return jnp.pad(both, ((0, 0), (0, 0), (0, 0), (0, 7), (0, 0)))


def gather(norm_gain, norm_bias, row_qkv, row_out, row_bias, col_qkv, col_out, col_bias,
           ffn_up, up_bias, ffn_down, down_bias, pos_tables):
    row = jnp.concatenate([row_qkv, row_out[None]], axis=0)
    col = jnp.concatenate([col_qkv, col_out[None]], axis=0)
    up = ffn_up.reshape(6, MEMBERS, D).transpose(1, 0, 2)
    slabs = jnp.stack(exchange(jnp.stack([row, col, up], axis=1)), axis=1)
    packed = jnp.concatenate(
        [slabs.reshape(3 * SLAB, D), ffn_down, pos_tables[0], pos_tables[1]], axis=0
    )
    gathered = lax.all_gather(packed, AXES, axis=0, tiled=False)
    sixes = jnp.concatenate([norm_gain, norm_bias, row_bias, col_bias, down_bias[None]], axis=0)
    line = jnp.pad(jnp.concatenate([sixes.reshape(-1), up_bias]), (0, 26))
    lines = lax.all_gather(line, AXES, axis=0, tiled=False).astype(F32)
    small = lines[:, :78].reshape(DEVICES, 13, 6).transpose(1, 0, 2).reshape(13, D)
    small = jnp.pad(small, ((0, 3), (0, 0)))
    return gathered.reshape(GROUPS, MEMBERS, PACK, D), small, lines[:, 78:102].reshape(4, D)


def on_device(tokens, cotangent, lengths, row_offset, col_offset, *weights):
    gathered, small, up_bias = gather(*weights)
    core = lax.axis_index("c").astype(jnp.int32)
    ints = jnp.concatenate([lengths, row_offset, col_offset, core[None]])
    act, g2, saved, hidden, ffn_own, ffn_other, ffn_sums = forward_call(
        ints, tokens.reshape(TOKENS, D), cotangent.reshape(TOKENS, D), small, up_bias, gathered
    )
    ffn_part = reduce_shares(ffn_own, ffn_other)
    g1, col_own, col_other, col_sums = back_call(True, ints, g2, small, gathered, saved, hidden)
    col_part = reduce_shares(col_own, col_other)
    g0, row_own, row_other, row_sums = back_call(False, ints, g1, small, gathered, saved, hidden)
    extra = small_shares(
        (row_sums, 0, 5), (col_sums, 0, 5), (ffn_sums, 4, 7), ffn_sums[:4]
    )
    row_part = reduce_shares(row_own, row_other, extra)
    return (act.reshape(tokens.shape), g0.reshape(tokens.shape)) + owned(ffn_part, col_part, row_part)


def owned(ffn_part, col_part, row_part):
    lanes = row_part[:240].reshape(-1, 128)
    row = lanes[:144].reshape(6, SLAB, 128).transpose(1, 0, 2).reshape(SLAB, D)
    tables = lanes[144:240].reshape(2, 6, 8, 128).transpose(0, 2, 1, 3).reshape(2, 8, D)
    blocks = jnp.stack([row, col_part, ffn_part[:SLAB]], axis=0).reshape(3, MEMBERS, 6, D)
    mine = jnp.stack(exchange(blocks.transpose(1, 0, 2, 3)), axis=0).astype(F32)
    line = row_part[240].astype(F32)
    sixes = line[:78].reshape(13, 6)
    row_sums, col_sums, ffn_sums = sixes[0:5], sixes[5:10], sixes[10:13]
    gain = jnp.stack([row_sums[0], col_sums[0], ffn_sums[1]])
    shift_grad = jnp.stack([row_sums[1], col_sums[1], ffn_sums[2]])
    return (
        gain,
        shift_grad,
        mine[:3, 0],
        mine[3, 0],
        row_sums[2:5],
        mine[:3, 1],
        mine[3, 1],
        col_sums[2:5],
        mine[:, 2].transpose(1, 0, 2).reshape(6, FF),
        line[78:102],
        ffn_part[SLAB:].astype(F32),
        ffn_sums[0],
        tables.astype(F32),
    )


def solution(mesh):
    mesh = Mesh(mesh.devices.reshape(4, 4, 4, 2), AXES)
    first, second = P(AXES), P(None, AXES)
    weights = (second, second, second, first, second, second, first, second) + (first,) * 4 + (second,)
    return jax.shard_map(
        on_device,
        mesh=mesh,
        in_specs=(first,) * 5 + weights,
        out_specs=(first, first) + weights,
        check_vma=False,
    )
```

```python
import math

import jax
import jax.numpy as jnp
from jax import lax
from jax.experimental import pallas as pl
from jax.experimental.pallas import tpu as pltpu
from jax.sharding import Mesh, PartitionSpec as P

AXES = ("y", "z", "x", "c")
DEVICES = 128
GROUPS = 32
MEMBERS = 4
D = 768
FF = 3072
HEAD_DIM = 64
POSITIONS = 1024
ROWS = 8
COLS = 64
TOKENS = ROWS * COLS
SLAB = 24
PACK = 112
PAIRS = 6
EPS = 1e-05
MASKED = -1e30
ROW_SCALE = 1.0 / math.sqrt(HEAD_DIM * ROWS)
COL_SCALE = 1.0 / math.sqrt(HEAD_DIM)
BF16 = jnp.bfloat16
F32 = jnp.float32
GAIN, SHIFT, ROW_BIAS, COL_BIAS, DOWN_BIAS = 0, 3, 6, 9, 12
A1, Q1, K1, V1, M1, A2, Q2, K2, V2, M2 = range(10)


def dot(left, right):
    return jnp.dot(left, right, preferred_element_type=F32)


def dot_nt(left, right):
    return lax.dot_general(left, right, (((1,), (1,)), ((), ())), preferred_element_type=F32)


def dot_tn(left, right):
    return lax.dot_general(left, right, (((0,), (0,)), ((), ())), preferred_element_type=F32)


def chunk(index, size):
    return pl.ds(pl.multiple_of(index * size, size), size)


def loop(count, body, unroll=1):
    def step(index, carry):
        body(index)
        return carry

    lax.fori_loop(0, count, step, 0, unroll=unroll)


def unit_of(hidden):
    centred = hidden - jnp.mean(hidden, axis=-1, keepdims=True)
    inverse = lax.rsqrt(jnp.mean(centred * centred, axis=-1, keepdims=True) + EPS)
    return centred * inverse, inverse


def norm(hidden, small, which):
    unit, _ = unit_of(hidden)
    gain, shift = small[GAIN + which : GAIN + which + 1, :], small[SHIFT + which : SHIFT + which + 1, :]
    return (unit * gain + shift).astype(BF16)


def norm_back(grad, hidden, gain):
    unit, inverse = unit_of(hidden)
    inner = grad * gain
    mean = jnp.mean(inner, axis=-1, keepdims=True)
    cross = jnp.mean(inner * unit, axis=-1, keepdims=True)
    return inverse * (inner - mean - unit * cross), grad * unit


def total(value):
    return jnp.sum(value, axis=0, keepdims=True)


def first_head(shape):
    return (lax.broadcasted_iota(jnp.int32, shape, 1) & 127) < HEAD_DIM


def stack_heads(value):
    keep = jnp.where(first_head(value.shape), 1.0, 0.0)
    return jnp.concatenate([value * keep.astype(BF16), value * (1.0 - keep).astype(BF16)], axis=0)


def merge_heads(value):
    half = value.shape[0] // 2
    return jnp.where(first_head((half, value.shape[1])), value[:half], value[half:])


def softmax(scores):
    top = jnp.max(scores, axis=-1, keepdims=True)
    raised = jnp.exp(scores - top)
    return raised / jnp.sum(raised, axis=-1, keepdims=True)


class RowHeads:
    scale = ROW_SCALE
    steps = 2

    def __init__(self, length):
        self.length = length

    def blocks(self, step):
        return [chunk(3 * step + i, 128) for i in range(3)]

    def load(self, ref, plane, lanes):
        return jnp.concatenate(
            [ref[plane, r * COLS : (r + 1) * COLS, lanes] for r in range(ROWS)], axis=1
        )

    def store(self, ref, plane, lanes, value):
        for r in range(ROWS):
            ref[plane, r * COLS : (r + 1) * COLS, lanes] = value[:, r * 128 : (r + 1) * 128]

    def mask(self):
        shape = (2 * COLS, COLS)
        return lax.broadcasted_iota(jnp.int32, shape, 1) < self.length


class ColHeads:
    scale = COL_SCALE
    steps = PAIRS

    def blocks(self, step):
        return [(i * 16, chunk(step, 128)) for i in range(4)]

    def load(self, ref, plane, block):
        start, lanes = block
        return jnp.concatenate(
            [ref[plane, r * COLS + start : r * COLS + start + 16, lanes] for r in range(ROWS)], axis=0
        )

    def store(self, ref, plane, block, value):
        start, lanes = block
        for r in range(ROWS):
            ref[plane, r * COLS + start : r * COLS + start + 16, lanes] = value[16 * r : 16 * r + 16]

    def mask(self):
        row = lax.broadcasted_iota(jnp.int32, (256, 128), 0) & 15
        return row == (lax.broadcasted_iota(jnp.int32, (256, 128), 1) & 15)


def each(function, *lists):
    return [function(*values) for values in zip(*lists)]


def weights_of(heads, queries, keys):
    mask = heads.mask()
    scores = each(dot_nt, queries, keys)
    return each(lambda s: softmax(jnp.where(mask, s * heads.scale, MASKED)), scores)


def attend(heads, ref, q, k, v, m):
    def body(step):
        blocks = heads.blocks(step)
        queries, keys, values = (
            [heads.load(ref, plane, block) for block in blocks] for plane in (q, k, v)
        )
        probs = weights_of(heads, each(stack_heads, queries), keys)
        mixed = each(lambda p, value: dot(p.astype(BF16), value), probs, values)
        for block, value in zip(blocks, mixed):
            heads.store(ref, m, block, merge_heads(value).astype(BF16))

    loop(heads.steps, body)


def attend_back(heads, ref, q, k, v, dm):
    def body(step):
        blocks = heads.blocks(step)
        queries, keys, values, mixed = (
            [heads.load(ref, plane, block) for block in blocks] for plane in (q, k, v, dm)
        )
        queries, mixed = each(stack_heads, queries), each(stack_heads, mixed)
        probs = weights_of(heads, queries, keys)
        grad = each(dot_nt, mixed, values)
        grad_values = each(lambda p, value: dot_tn(p.astype(BF16), value), probs, mixed)
        inner = each(
            lambda p, g: (p * (g - jnp.sum(g * p, axis=-1, keepdims=True))).astype(BF16), probs, grad
        )
        grad_queries = each(lambda i, key: merge_heads(dot(i, key)) * heads.scale, inner, keys)
        grad_keys = each(lambda i, query: dot_tn(i, query) * heads.scale, inner, queries)
        for i, block in enumerate(blocks):
            heads.store(ref, q, block, grad_queries[i].astype(BF16))
            heads.store(ref, k, block, grad_keys[i].astype(BF16))
            heads.store(ref, v, block, grad_values[i].astype(BF16))

    loop(heads.steps, body)


def whole(ref, index):
    return ref[index].reshape(D, D)


def project(ref, source, planes, weights, first, small, bias_row):
    def body(index):
        rows = chunk(index, 256)
        normed = ref[source, rows, :]
        for i, plane in enumerate(planes):
            value = dot(normed, whole(weights, first + i))
            if i != 1:
                row = bias_row + (0 if i == 0 else 1)
                value = value + small[row : row + 1, :]
            ref[plane, rows, :] = value.astype(BF16)

    loop(2, body)


def by_halves(grads, which, index, value):
    value = value.astype(BF16).reshape(8, 2, SLAB, D)
    for half in range(2):
        grads[which, pl.ds(16 * half + 8 * index, 8)] = value[:, half]


class Copies:
    def __init__(self, sems):
        self.sems, self.used = sems, 0

    def start(self, source, target):
        copy = pltpu.make_async_copy(source, target, self.sems.at[self.used])
        self.used += 1
        copy.start()
        return copy

    def send(self, core, parity, source, own, other):
        sem = self.sems.at[self.used]
        self.used += 1
        here = pltpu.make_async_copy(source, own, sem)
        there = pltpu.make_async_copy(source, other, sem)
        pl.when(core == parity)(here.start)
        pl.when(core != parity)(there.start)
        return here


def position_rows(window, offset, count):
    shape = (count, window.shape[0])
    pick = lax.broadcasted_iota(jnp.int32, shape, 1) == (
        lax.broadcasted_iota(jnp.int32, shape, 0) + offset % 8
    )
    return dot(jnp.where(pick, 1.0, 0.0).astype(BF16), window)


def forward_kernel(
    ints, tokens, cotangent, small, up_bias, gathered,
    act_out, g2_out, saved_out, hidden_out, shares, sums,
    weights, down, window, act, hidden, h2, a3, gy, wide, y, da, sems,
):
    grads = weights
    length, row_offset, col_offset = ints[0], ints[1], ints[2]
    copies = Copies(sems)
    near = []
    for i in range(2):
        dev = jnp.minimum(row_offset // 8 + i, DEVICES - 1)
        near.append(
            copies.start(gathered.at[dev // 4, dev % 4, 96:104, :], window.at[8 * i : 8 * i + 8, :])
        )
    for i in range(9):
        dev = jnp.minimum(col_offset // 8 + i, DEVICES - 1)
        near.append(
            copies.start(
                gathered.at[dev // 4, dev % 4, 104:112, :], window.at[16 + 8 * i : 24 + 8 * i, :]
            )
        )
    loads = [
        copies.start(gathered.at[:, i % 4, 24 * (i // 4) : 24 * (i // 4) + 24, :], weights.at[i])
        for i in range(12)
    ]
    loads += [
        copies.start(gathered.at[8 * f : 8 * f + 8, :, 72:96, :], down.at[f]) for f in range(4)
    ]
    for copy in near:
        copy.wait()
    row_pos = position_rows(window[0:16, :], row_offset, ROWS)
    col_pos = position_rows(window[16:88, :], col_offset, COLS)
    for r in range(ROWS):
        rows = slice(r * COLS, (r + 1) * COLS)
        value = tokens[rows, :].astype(F32) + row_pos[r : r + 1, :] + col_pos
        hidden[0, rows, :] = value
        act[A1, rows, :] = norm(value, small, 0)
    stores = [copies.start(hidden.at[0], hidden_out.at[0]), copies.start(act.at[A1], saved_out.at[A1])]

    def branch(first, source, planes, heads, bias, target, which, last):
        for i in range(3):
            loads[first + i].wait()
        project(act, source, planes[:3], weights, first, small, bias)
        for plane in planes[:3]:
            stores.append(copies.start(act.at[plane], saved_out.at[plane]))
        attend(heads, act, *planes)
        stores.append(copies.start(act.at[planes[3]], saved_out.at[planes[3]]))
        loads[first + 3].wait()

        def body(index):
            rows = chunk(index, 256)
            branch_out = dot(act[planes[3], rows, :], whole(weights, first + 3))
            before = hidden[which - 1, rows, :]
            after = before + (branch_out + small[bias + 2 : bias + 3, :])
            if last:
                h2[rows, :] = after
                a3[rows, :] = norm(after, small, which)
            else:
                hidden[which, rows, :] = after
                act[target, rows, :] = norm(after, small, which)

        loop(2, body)

    branch(0, A1, (Q1, K1, V1, M1), RowHeads(length), ROW_BIAS, A2, 1, False)
    stores.append(copies.start(hidden.at[1], hidden_out.at[1]))
    stores.append(copies.start(act.at[A2], saved_out.at[A2]))
    branch(4, A2, (Q2, K2, V2, M2), ColHeads(), COL_BIAS, None, 2, True)

    in_use = lax.broadcasted_iota(jnp.int32, (COLS, D), 0) < length
    for r in range(ROWS):
        rows = slice(r * COLS, (r + 1) * COLS)
        gy[rows, :] = jnp.where(in_use, cotangent[rows, :].astype(F32), 0.0).astype(BF16)
    for copy in loads[8:]:
        copy.wait()

    def ffn(f):
        up, low = whole(weights, 8 + f), down[f].reshape(D, D)
        bias = up_bias[pl.ds(f, 1), :]

        def body(index):
            rows = chunk(index, 256)
            z = dot(a3[rows, :], up) + bias
            cdf = 0.5 * (1.0 + lax.erf(z * math.sqrt(0.5)))
            slope = cdf + z * (jnp.exp(-0.5 * z * z) * (1.0 / math.sqrt(2.0 * math.pi)))
            u = (z * cdf).astype(BF16)
            wide[0, rows, :] = u
            du = dot_nt(gy[rows, :], low).astype(BF16).astype(F32)
            dz = (du * slope).astype(BF16)
            wide[1, rows, :] = dz
            more, more_da = dot(u, low), dot_nt(dz, up)

            @pl.when(f == 0)
            def _():
                y[rows, :] = more
                da[rows, :] = more_da

            @pl.when(f != 0)
            def _():
                y[rows, :] += more
                da[rows, :] += more_da

        loop(2, body)
        sums[pl.ds(f, 1), :] = total(wide[1].astype(F32))

        def back(index):
            cols = chunk(index, 384)
            value = dot_tn(wide[0, :, cols], gy[...]).astype(BF16).reshape(2, 8, SLAB, D)
            for k in range(8):
                grads[4 + f, pl.ds(4 * k + 2 * index, 2)] = value[:, k]
            by_halves(grads, f, index, dot_tn(a3[:, cols], wide[1]))

        loop(2, back)
        for copy in ffn_sends(f):
            copy.start()

    first_sem = copies.used

    def ffn_sends(f):
        sends = []
        for half in range(2):
            place = (4 * half + f, slice(None), slice(0, SLAB))
            sends.append((grads.at[f, 16 * half : 16 * half + 16], shares.at[place]))
        for k in range(8):
            place = (k, pl.ds(4 * f, 4), slice(SLAB, 2 * SLAB))
            sends.append((grads.at[4 + f, 4 * k : 4 * k + 4], shares.at[place]))
        return [
            pltpu.make_async_copy(source, target, sems.at[first_sem + 10 * f + i])
            for i, (source, target) in enumerate(sends)
        ]

    loop(4, ffn)
    gain = small[GAIN + 2 : GAIN + 3, :]

    def finish(index, carry):
        rows = chunk(index, 64)
        late = h2[rows, :]
        act_out[rows, :] = (late + (y[rows, :] + small[DOWN_BIAS : DOWN_BIAS + 1, :])).astype(BF16)
        grad = da[rows, :]
        inner, unit = norm_back(grad, late, gain)
        cot = gy[rows, :].astype(F32)
        g2_out[rows, :] = cot + inner
        return carry[0] + total(unit), carry[1] + total(grad), carry[2] + total(cot)

    zero = jnp.zeros((1, D), F32)
    gain_sum, shift_sum, down_sum = lax.fori_loop(0, 8, finish, (zero, zero, zero))
    sums[4:5, :] = down_sum
    sums[5:6, :] = gain_sum
    sums[6:7, :] = shift_sum
    sums[7:8, :] = zero
    for copy in stores + [copy for f in range(4) for copy in ffn_sends(f)]:
        copy.wait()


def heads_kernel(column, ints, grad_in, gathered, saved, grads_out, weight, act, sems):
    first, planes = (24, (Q2, K2, V2)) if column else (0, (Q1, K1, V1))
    heads = ColHeads() if column else RowHeads(ints[0])
    copies = Copies(sems)
    load = copies.start(gathered.at[:, 3, first : first + SLAB, :], weight.at[0])
    act_loads = [copies.start(saved.at[plane], act.at[i]) for i, plane in enumerate(planes)]
    load.wait()

    def mixed_back(index):
        rows = chunk(index, 256)
        act[3, rows, :] = dot_nt(grad_in[rows, :].astype(BF16), whole(weight, 0)).astype(BF16)

    loop(2, mixed_back)
    for copy in act_loads:
        copy.wait()
    attend_back(heads, act, 0, 1, 2, 3)
    stores = [copies.start(act.at[i], grads_out.at[i]) for i in range(3)]
    for copy in stores:
        copy.wait()


class Shares:
    def __init__(self, core, copies, own, other):
        self.core, self.copies, self.own, self.other, self.sent = core, copies, own, other, []

    def send(self, grads, member):
        every, parity = slice(None), member % 2
        for half in range(2):
            x = 2 * half + member // 2
            place = (x,) if parity == 0 else (every, x)
            self.sent.append(
                self.copies.send(
                    self.core, parity, grads.at[member, half], self.own.at[place], self.other.at[place]
                )
            )

    def wait(self):
        for copy in self.sent:
            copy.wait()


def keep(grads, which, part, value):
    value = value.astype(BF16).reshape(2, 4, 2, SLAB, D)
    for half in range(2):
        grads[which, half, pl.ds(2 * part, 2)] = value[:, :, half]


def weight_grads(loads, grad_in, act, out_grad, normed, mixed, grads, shares):
    def low(index):
        rows = chunk(index, 128)
        out_grad[rows, :] = grad_in[rows, :].astype(BF16)

    loop(4, low)
    loads["mixed"].wait()

    def out_back(index):
        keep(grads, 3, index, dot_tn(mixed[:, chunk(index, 384)], out_grad[...]))

    loop(2, out_back)
    shares.send(grads, 3)
    loads["normed"].wait()
    for i in range(3):
        loads[i].wait()

    def weight_back(index):
        which, part = index // 2, index % 2
        keep(grads, which, part, dot_tn(normed[:, chunk(part, 384)], act[which]))

    loop(6, weight_back)
    for member in range(3):
        shares.send(grads, member)


def input_grads(loads, grad_in, gain, act, weights, hidden, da, grad_out, sums, lines=None):
    for i in range(3):
        for copy in loads["inputs"][i]:
            copy.wait()

        def input_back(index):
            rows = chunk(index, 256)
            value = dot_nt(act[i, rows, :], whole(weights, i))
            da[rows, :] = value if i == 0 else da[rows, :] + value

        loop(2, input_back)
    loads["hidden"].wait()

    def finish(index, carry):
        rows = chunk(index, 64)
        grad, before = da[rows, :], grad_in[rows, :]
        inner, unit = norm_back(grad, hidden[rows, :], gain)
        value = before + inner
        grad_out[rows, :] = value
        added = [unit, grad, act[0, rows, :], act[2, rows, :], before.astype(BF16)]
        added = [total(extra.astype(F32)) for extra in added]
        if lines is not None:
            lines[pl.ds(index, 1), :] = total(value)
            added.append(value)
        return tuple(a + b for a, b in zip(carry, added))

    carry = (jnp.zeros((1, D), F32),) * 5
    if lines is not None:
        carry = carry + (jnp.zeros((COLS, D), F32),)
    carry = lax.fori_loop(0, 8, finish, carry)
    for i in range(5):
        sums[i : i + 1, :] = carry[i]
    sums[5:8, :] = jnp.zeros((3, D), F32)
    return carry[-1]


def column_kernel(
    ints, grad_in, small, gathered, saved, hidden_saved, grads_in,
    grad_out, own, other, sums,
    weights, act, out_grad, normed, mixed, hidden, da, grads, sems,
):
    copies = Copies(sems)
    shares = Shares(ints[3], copies, own, other)
    loads = {"mixed": copies.start(saved.at[M2], mixed), "normed": copies.start(saved.at[A2], normed)}
    for i in range(3):
        loads[i] = copies.start(grads_in.at[i], act.at[i])
    loads["inputs"] = [
        [copies.start(gathered.at[:, i, SLAB : 2 * SLAB, :], weights.at[i])] for i in range(3)
    ]
    loads["hidden"] = copies.start(hidden_saved.at[1], hidden)
    weight_grads(loads, grad_in, act, out_grad, normed, mixed, grads, shares)
    input_grads(loads, grad_in, small[GAIN + 1 : GAIN + 2, :], act, weights, hidden, da, grad_out, sums)
    shares.wait()


def row_weights_kernel(
    ints, grad_in, saved, grads_in, own, other, act, out_grad, normed, mixed, grads, sems
):
    copies = Copies(sems)
    shares = Shares(ints[3], copies, own, other)
    loads = {"mixed": copies.start(saved.at[M1], mixed), "normed": copies.start(saved.at[A1], normed)}
    for i in range(3):
        loads[i] = copies.start(grads_in.at[i], act.at[i])
    weight_grads(loads, grad_in, act, out_grad, normed, mixed, grads, shares)
    shares.wait()


def row_input_kernel(
    ints, grad_in, small, gathered, hidden_saved, grads_in,
    grad_out, own, other, sums,
    weights, act, hidden, da, zeros, table, lines, sems,
):
    copies = Copies(sems)
    loads = {"inputs": []}
    for i in range(3):
        slab = gathered.at[:, i, 0:SLAB, :]
        loads["inputs"].append(
            [copies.start(grads_in.at[i], act.at[i]), copies.start(slab, weights.at[i])]
        )
    loads["hidden"] = copies.start(hidden_saved.at[0], hidden)
    zeros[...] = jnp.zeros_like(zeros)
    fills = [copies.start(zeros, out) for out in (own, other)]
    gain = small[GAIN : GAIN + 1, :]
    col_lines = input_grads(loads, grad_in, gain, act, weights, hidden, da, grad_out, sums, lines)
    send_tables(ints, copies, fills, lines[...], col_lines, table, own, other)


def send_tables(ints, copies, fills, row_lines, col_lines, table, own, other):
    core = ints[3]

    def placed(values, offset, count):
        shape = (count, values.shape[0])
        here = lax.broadcasted_iota(jnp.int32, shape, 0) == (
            lax.broadcasted_iota(jnp.int32, shape, 1) + offset % 8
        )
        return dot(jnp.where(here, 1.0, 0.0).astype(BF16), values.astype(BF16)).astype(BF16)

    spots = []
    for first, count, values, offset, start in (
        (0, 2, row_lines, ints[1], 0),
        (2, 9, col_lines, ints[2], 8),
    ):
        table[first : first + count] = placed(values, offset, 8 * count).reshape(count, 8, D)
        spots += [(first + i, offset // 8 + i, start) for i in range(count)]
    for copy in fills:
        copy.wait()
    waits = []
    for slot, owner, start in spots:
        real, dev = owner < DEVICES, jnp.minimum(owner, DEVICES - 1)
        x, y, z = (dev // 2) % 4, dev // 32, (dev // 8) % 4
        odd = dev % 2 == 1
        place = (jnp.where(odd, y, x), jnp.where(odd, x, y), z, slice(start, start + 8))
        sem = copies.sems.at[copies.used]
        copies.used += 1
        here = pltpu.make_async_copy(table.at[slot], own.at[place], sem)
        there = pltpu.make_async_copy(table.at[slot], other.at[place], sem)
        pl.when(real & (dev % 2 == core))(here.start)
        pl.when(real & (dev % 2 != core))(there.start)
        waits.append((real, here))
    for real, copy in waits:
        pl.when(real)(copy.wait)


VMEM = pl.BlockSpec(memory_space=pltpu.VMEM)
ANY = pl.BlockSpec(memory_space=pl.ANY)
SMEM = pl.BlockSpec(memory_space=pltpu.SMEM)
SHAPE = jax.ShapeDtypeStruct


def params():
    return pltpu.CompilerParams(vmem_limit_bytes=62 * 1024 * 1024)


def cost(flops, traffic):
    return pl.CostEstimate(flops=flops, transcendentals=0, bytes_accessed=traffic)


def forward_call(ints, tokens, cotangent, small, up_bias, gathered):
    plane = (TOKENS, D)
    return pl.pallas_call(
        forward_kernel,
        name="forward",
        in_specs=[SMEM, VMEM, VMEM, VMEM, VMEM, ANY],
        out_shape=(
            SHAPE(plane, BF16),
            SHAPE(plane, F32),
            SHAPE((10,) + plane, BF16),
            SHAPE((2,) + plane, F32),
            SHAPE((8, 16, 2 * SLAB, D), BF16),
            SHAPE((8, D), F32),
        ),
        out_specs=(VMEM, VMEM, ANY, ANY, ANY, VMEM),
        scratch_shapes=[
            pltpu.VMEM((12, GROUPS, SLAB, D), BF16),
            pltpu.VMEM((4, 8, MEMBERS, SLAB, D), BF16),
            pltpu.VMEM((88, D), BF16),
            pltpu.VMEM((10,) + plane, BF16),
            pltpu.VMEM((2,) + plane, F32),
            pltpu.VMEM(plane, F32),
            pltpu.VMEM(plane, BF16),
            pltpu.VMEM(plane, BF16),
            pltpu.VMEM((2,) + plane, BF16),
            pltpu.VMEM(plane, F32),
            pltpu.VMEM(plane, F32),
            pltpu.SemaphoreType.DMA((96,)),
        ],
        compiler_params=params(),
        cost_estimate=cost(24 * 10**9, 50 * 10**6),
    )(ints, tokens, cotangent, small, up_bias, gathered)


def heads_call(column, ints, grad, gathered, saved):
    plane = (TOKENS, D)
    return pl.pallas_call(
        lambda *refs: heads_kernel(column, *refs),
        name="column_heads" if column else "row_heads",
        in_specs=[SMEM, VMEM, ANY, ANY],
        out_shape=SHAPE((3,) + plane, BF16),
        out_specs=ANY,
        scratch_shapes=[
            pltpu.VMEM((1, GROUPS, SLAB, D), BF16),
            pltpu.VMEM((4,) + plane, BF16),
            pltpu.SemaphoreType.DMA((8,)),
        ],
        compiler_params=params(),
        cost_estimate=cost(10**10, 10**7),
    )(ints, grad, gathered, saved)


PLANE = (TOKENS, D)


def share_of(rows):
    return SHAPE((4, 4, 4, rows, D), BF16)


def column_call(ints, grad, small, gathered, saved, hidden, grads):
    return pl.pallas_call(
        column_kernel,
        name="column_weights",
        in_specs=[SMEM, VMEM, VMEM, ANY, ANY, ANY, ANY],
        out_shape=(SHAPE(PLANE, F32), share_of(SLAB), share_of(SLAB), SHAPE((8, D), F32)),
        out_specs=(VMEM, ANY, ANY, VMEM),
        scratch_shapes=[
            pltpu.VMEM((3, GROUPS, SLAB, D), BF16),
            pltpu.VMEM((3,) + PLANE, BF16),
            pltpu.VMEM(PLANE, BF16),
            pltpu.VMEM(PLANE, BF16),
            pltpu.VMEM(PLANE, BF16),
            pltpu.VMEM(PLANE, F32),
            pltpu.VMEM(PLANE, F32),
            pltpu.VMEM((4, 2, 4, 4, SLAB, D), BF16),
            pltpu.SemaphoreType.DMA((32,)),
        ],
        compiler_params=params(),
        cost_estimate=cost(10**10, 10**7),
    )(ints, grad, small, gathered, saved, hidden, grads)


def row_weights_call(ints, grad, saved, grads):
    return pl.pallas_call(
        row_weights_kernel,
        name="row_weights",
        in_specs=[SMEM, VMEM, ANY, ANY],
        out_shape=(share_of(SLAB), share_of(SLAB)),
        out_specs=(ANY, ANY),
        scratch_shapes=[
            pltpu.VMEM((3,) + PLANE, BF16),
            pltpu.VMEM(PLANE, BF16),
            pltpu.VMEM(PLANE, BF16),
            pltpu.VMEM(PLANE, BF16),
            pltpu.VMEM((4, 2, 4, 4, SLAB, D), BF16),
            pltpu.SemaphoreType.DMA((32,)),
        ],
        compiler_params=params(),
        cost_estimate=cost(10**10, 10**7),
    )(ints, grad, saved, grads)


def row_input_call(ints, grad, small, gathered, hidden, grads):
    return pl.pallas_call(
        row_input_kernel,
        name="row_input",
        in_specs=[SMEM, VMEM, VMEM, ANY, ANY, ANY],
        out_shape=(SHAPE(PLANE, F32), share_of(16), share_of(16), SHAPE((8, D), F32)),
        out_specs=(VMEM, ANY, ANY, VMEM),
        scratch_shapes=[
            pltpu.VMEM((3, GROUPS, SLAB, D), BF16),
            pltpu.VMEM((3,) + PLANE, BF16),
            pltpu.VMEM(PLANE, F32),
            pltpu.VMEM(PLANE, F32),
            pltpu.VMEM((4, 4, 4, 16, D), BF16),
            pltpu.VMEM((11, 8, D), BF16),
            pltpu.VMEM((ROWS, D), F32),
            pltpu.SemaphoreType.DMA((32,)),
        ],
        compiler_params=params(),
        cost_estimate=cost(10**10, 10**7),
    )(ints, grad, small, gathered, hidden, grads)


def take(value, index, dim):
    return lax.squeeze(lax.dynamic_slice_in_dim(value, index, 1, dim), (dim,))


def add(*values):
    total_value = values[0].astype(F32)
    for value in values[1:]:
        total_value = total_value + value.astype(F32)
    return total_value.astype(BF16)


def exchange(blocks):
    me = (lax.axis_index("x") % 2) * 2 + lax.axis_index("c")
    parts = []
    for flip in range(4):
        part = take(blocks, me ^ flip, 0)
        if flip:
            pairs = [(i, (i // 4) * 4 + ((i % 4) ^ flip)) for i in range(8)]
            part = lax.ppermute(part, ("x", "c"), pairs)
        parts.append(part)
    odd, high = (me & 1) == 1, (me & 2) == 2
    pairs = [jnp.where(odd, parts[i ^ 1], parts[i]) for i in range(4)]
    return [jnp.where(high, pairs[i ^ 2], pairs[i]) for i in range(4)]


def swap(value):
    return lax.ppermute(value, "c", [(0, 1), (1, 0)])


def scatter_chip_rows(shares):
    return lax.psum_scatter(shares, ("x", "c"), scatter_dimension=0, tiled=False)


STAGES = (("x", "y"), ("y", "x"), ("z", "z"))
STRIDES = {"y": 32, "z": 8, "x": 2}


def direct(value, axes):
    place = jnp.where(lax.axis_index("c") == 0, lax.axis_index(axes[0]), lax.axis_index(axes[1]))
    parts = [take(value, place, 0)]
    for hop in range(1, 4):
        pairs = []
        for dev in range(DEVICES):
            stride = STRIDES[axes[dev % 2]]
            at = dev // stride % 4
            pairs.append((dev, dev + ((at + hop) % 4 - at) * stride))
        parts.append(lax.ppermute(take(value, (place + hop) % 4, 0), AXES, pairs))
    return add(*parts)


def small_shares(*sums):
    sixes = jnp.concatenate([part[first:last] for part, first, last in sums[:-1]], axis=0)
    sixes = sixes.reshape(-1, DEVICES, 6).transpose(1, 0, 2).reshape(DEVICES, -1)
    values = jnp.concatenate([sixes, sums[-1].reshape(DEVICES, SLAB)], axis=1).astype(BF16)
    values = jnp.pad(values, ((0, 0), (0, 128 - values.shape[1]))).reshape(4, 4, 4, 2, 1, 128)
    even, odd = values[:, :, :, 0].transpose(2, 0, 1, 3, 4), values[:, :, :, 1].transpose(0, 2, 1, 3, 4)
    first = lax.axis_index("c") == 0
    both = add(jnp.where(first, even, odd), swap(jnp.where(first, odd, even)))
    return jnp.pad(both, ((0, 0), (0, 0), (0, 0), (0, 7), (0, D - 128)))


def gather(norm_gain, norm_bias, row_qkv, row_out, row_bias, col_qkv, col_out, col_bias,
           ffn_up, up_bias, ffn_down, down_bias, pos_tables):
    row = jnp.concatenate([row_qkv, row_out[None]], axis=0)
    col = jnp.concatenate([col_qkv, col_out[None]], axis=0)
    up = ffn_up.reshape(6, MEMBERS, D).transpose(1, 0, 2)
    slabs = jnp.stack(exchange(jnp.stack([row, col, up], axis=1)), axis=1)
    packed = jnp.concatenate(
        [slabs.reshape(3 * SLAB, D), ffn_down, pos_tables[0], pos_tables[1]], axis=0
    )
    gathered = lax.all_gather(packed, AXES, axis=0, tiled=False)
    sixes = jnp.concatenate([norm_gain, norm_bias, row_bias, col_bias, down_bias[None]], axis=0)
    line = jnp.pad(jnp.concatenate([sixes.reshape(-1), up_bias]), (0, 26))
    lines = lax.all_gather(line, AXES, axis=0, tiled=False).astype(F32)
    small = lines[:, :78].reshape(DEVICES, 13, 6).transpose(1, 0, 2).reshape(13, D)
    small = jnp.pad(small, ((0, 3), (0, 0)))
    return gathered.reshape(GROUPS, MEMBERS, PACK, D), small, lines[:, 78:102].reshape(4, D)


def on_device(tokens, cotangent, lengths, row_offset, col_offset, *weights):
    gathered, small, up_bias = gather(*weights)
    core = lax.axis_index("c").astype(jnp.int32)
    ints = jnp.concatenate([lengths, row_offset, col_offset, core[None]])
    act, g2, saved, hidden, ffn_shares, ffn_sums = forward_call(
        ints, tokens.reshape(TOKENS, D), cotangent.reshape(TOKENS, D), small, up_bias, gathered
    )
    barrier = lax.optimization_barrier
    ffn = scatter_chip_rows(ffn_shares)
    col_heads = heads_call(True, ints, g2, gathered, saved)
    g1, own, other, col_sums = column_call(ints, g2, small, gathered, saved, hidden, col_heads)
    row_heads = heads_call(False, ints, g1, gathered, saved)
    col, row_heads = barrier((add(own, swap(other)), row_heads))
    col = direct(col, STAGES[0])
    g0, table_own, table_other, row_sums = row_input_call(ints, g1, small, gathered, hidden, row_heads)
    own, other = row_weights_call(ints, g1, saved, row_heads)
    table_other, col = barrier((table_other, col))
    other, table_other = barrier((other, swap(table_other)))
    extra = small_shares((row_sums, 0, 5), (col_sums, 0, 5), (ffn_sums, 4, 7), ffn_sums[:4])
    other = swap(other)
    table = jnp.concatenate([add(table_own, table_other), extra], axis=3)
    table = direct(table, STAGES[0])
    other, ffn = barrier((other, ffn))
    ffn = lax.psum_scatter(ffn.reshape(4, 4, 2 * SLAB, D), "y", scatter_dimension=0, tiled=False)
    row = direct(add(own, other), STAGES[0])
    rows = direct(jnp.concatenate([row, table, col], axis=2), STAGES[1])
    rows = direct(jnp.concatenate([rows, ffn], axis=1), STAGES[2])
    return (act.reshape(tokens.shape), g0.reshape(tokens.shape)) + owned(rows)


def rows_of(*slabs):
    blocks = jnp.stack(slabs, axis=0).reshape(len(slabs), MEMBERS, 6, D)
    return jnp.stack(exchange(blocks.transpose(1, 0, 2, 3)), axis=0).astype(F32)


def owned(rows):
    row, table, col, up, down = (rows[i * SLAB : (i + 1) * SLAB] for i in range(5))
    mine = rows_of(row, col, up)
    line = table[16, :128].astype(F32)
    sixes = line[:78].reshape(13, 6)
    row_sums, col_sums, ffn_sums = sixes[0:5], sixes[5:10], sixes[10:13]
    gain = jnp.stack([row_sums[0], col_sums[0], ffn_sums[1]])
    shift_grad = jnp.stack([row_sums[1], col_sums[1], ffn_sums[2]])
    return (
        gain,
        shift_grad,
        mine[:3, 0],
        mine[3, 0],
        row_sums[2:5],
        mine[:3, 1],
        mine[3, 1],
        col_sums[2:5],
        mine[:, 2].transpose(1, 0, 2).reshape(6, FF),
        line[78:102],
        down.astype(F32),
        ffn_sums[0],
        table[:16].reshape(2, 8, D).astype(F32),
    )


def solution(mesh):
    mesh = Mesh(mesh.devices.reshape(4, 4, 4, 2), AXES)
    first, second = P(AXES), P(None, AXES)
    weights = (second, second, second, first, second, second, first, second) + (first,) * 4 + (second,)
    return jax.shard_map(
        on_device,
        mesh=mesh,
        in_specs=(first,) * 5 + weights,
        out_specs=(first, first) + weights,
        check_vma=False,
    )
```

```python
import math

import jax
import jax.numpy as jnp
from jax import lax
from jax.experimental import pallas as pl
from jax.experimental.pallas import tpu as pltpu
from jax.sharding import Mesh, PartitionSpec as P

AXES = ("y", "z", "x", "c")
DEVICES = 128
GROUPS = 32
MEMBERS = 4
D = 768
FF = 3072
HEAD_DIM = 64
POSITIONS = 1024
ROWS = 8
COLS = 64
TOKENS = ROWS * COLS
SLAB = 24
PACK = 112
PAIRS = 6
EPS = 1e-05
MASKED = -1e30
ROW_SCALE = 1.0 / math.sqrt(HEAD_DIM * ROWS)
COL_SCALE = 1.0 / math.sqrt(HEAD_DIM)
BF16 = jnp.bfloat16
F32 = jnp.float32
GAIN, SHIFT, ROW_BIAS, COL_BIAS, DOWN_BIAS = 0, 3, 6, 9, 12
A1, Q1, K1, V1, M1, A2, Q2, K2, V2, M2 = range(10)


def dot(left, right):
    return jnp.dot(left, right, preferred_element_type=F32)


def dot_nt(left, right):
    return lax.dot_general(left, right, (((1,), (1,)), ((), ())), preferred_element_type=F32)


def dot_tn(left, right):
    return lax.dot_general(left, right, (((0,), (0,)), ((), ())), preferred_element_type=F32)


def chunk(index, size):
    return pl.ds(pl.multiple_of(index * size, size), size)


def loop(count, body, unroll=1):
    def step(index, carry):
        body(index)
        return carry

    lax.fori_loop(0, count, step, 0, unroll=unroll)


def unit_of(hidden):
    centred = hidden - jnp.mean(hidden, axis=-1, keepdims=True)
    inverse = lax.rsqrt(jnp.mean(centred * centred, axis=-1, keepdims=True) + EPS)
    return centred * inverse, inverse


def norm(hidden, small, which):
    unit, _ = unit_of(hidden)
    gain, shift = small[GAIN + which : GAIN + which + 1, :], small[SHIFT + which : SHIFT + which + 1, :]
    return (unit * gain + shift).astype(BF16)


def norm_back(grad, hidden, gain):
    unit, inverse = unit_of(hidden)
    inner = grad * gain
    mean = jnp.mean(inner, axis=-1, keepdims=True)
    cross = jnp.mean(inner * unit, axis=-1, keepdims=True)
    return inverse * (inner - mean - unit * cross), grad * unit


def total(value):
    return jnp.sum(value, axis=0, keepdims=True)


def first_head(shape):
    return (lax.broadcasted_iota(jnp.int32, shape, 1) & 127) < HEAD_DIM


def stack_heads(value):
    keep = jnp.where(first_head(value.shape), 1.0, 0.0)
    return jnp.concatenate([value * keep.astype(BF16), value * (1.0 - keep).astype(BF16)], axis=0)


def merge_heads(value):
    half = value.shape[0] // 2
    return jnp.where(first_head((half, value.shape[1])), value[:half], value[half:])


def softmax(scores):
    top = jnp.max(scores, axis=-1, keepdims=True)
    raised = jnp.exp(scores - top)
    return raised / jnp.sum(raised, axis=-1, keepdims=True)


class RowHeads:
    scale = ROW_SCALE
    steps = 2

    def __init__(self, length):
        self.length = length

    def blocks(self, step):
        return [chunk(3 * step + i, 128) for i in range(3)]

    def load(self, ref, plane, lanes):
        return jnp.concatenate(
            [ref[plane, r * COLS : (r + 1) * COLS, lanes] for r in range(ROWS)], axis=1
        )

    def store(self, ref, plane, lanes, value):
        for r in range(ROWS):
            ref[plane, r * COLS : (r + 1) * COLS, lanes] = value[:, r * 128 : (r + 1) * 128]

    def mask(self):
        shape = (2 * COLS, COLS)
        return lax.broadcasted_iota(jnp.int32, shape, 1) < self.length


class ColHeads:
    scale = COL_SCALE
    steps = PAIRS

    def blocks(self, step):
        return [(i * 16, chunk(step, 128)) for i in range(4)]

    def load(self, ref, plane, block):
        start, lanes = block
        return jnp.concatenate(
            [ref[plane, r * COLS + start : r * COLS + start + 16, lanes] for r in range(ROWS)], axis=0
        )

    def store(self, ref, plane, block, value):
        start, lanes = block
        for r in range(ROWS):
            ref[plane, r * COLS + start : r * COLS + start + 16, lanes] = value[16 * r : 16 * r + 16]

    def mask(self):
        row = lax.broadcasted_iota(jnp.int32, (256, 128), 0) & 15
        return row == (lax.broadcasted_iota(jnp.int32, (256, 128), 1) & 15)


def each(function, *lists):
    return [function(*values) for values in zip(*lists)]


def weights_of(heads, queries, keys):
    mask = heads.mask()
    scores = each(dot_nt, queries, keys)
    return each(lambda s: softmax(jnp.where(mask, s * heads.scale, MASKED)), scores)


def attend(heads, ref, q, k, v, m):
    def body(step):
        blocks = heads.blocks(step)
        queries, keys, values = (
            [heads.load(ref, plane, block) for block in blocks] for plane in (q, k, v)
        )
        probs = weights_of(heads, each(stack_heads, queries), keys)
        mixed = each(lambda p, value: dot(p.astype(BF16), value), probs, values)
        for block, value in zip(blocks, mixed):
            heads.store(ref, m, block, merge_heads(value).astype(BF16))

    loop(heads.steps, body)


def attend_back(heads, ref, q, k, v, dm):
    def body(step):
        blocks = heads.blocks(step)
        queries, keys, values, mixed = (
            [heads.load(ref, plane, block) for block in blocks] for plane in (q, k, v, dm)
        )
        queries, mixed = each(stack_heads, queries), each(stack_heads, mixed)
        probs = weights_of(heads, queries, keys)
        grad = each(dot_nt, mixed, values)
        grad_values = each(lambda p, value: dot_tn(p.astype(BF16), value), probs, mixed)
        inner = each(
            lambda p, g: (p * (g - jnp.sum(g * p, axis=-1, keepdims=True))).astype(BF16), probs, grad
        )
        grad_queries = each(lambda i, key: merge_heads(dot(i, key)) * heads.scale, inner, keys)
        grad_keys = each(lambda i, query: dot_tn(i, query) * heads.scale, inner, queries)
        for i, block in enumerate(blocks):
            heads.store(ref, q, block, grad_queries[i].astype(BF16))
            heads.store(ref, k, block, grad_keys[i].astype(BF16))
            heads.store(ref, v, block, grad_values[i].astype(BF16))

    loop(heads.steps, body)


def whole(ref, index):
    return ref[index].reshape(D, D)


def project(ref, source, planes, weights, first, small, bias_row):
    def body(index):
        rows = chunk(index, 256)
        normed = ref[source, rows, :]
        for i, plane in enumerate(planes):
            value = dot(normed, whole(weights, first + i))
            if i != 1:
                row = bias_row + (0 if i == 0 else 1)
                value = value + small[row : row + 1, :]
            ref[plane, rows, :] = value.astype(BF16)

    loop(2, body)


def by_halves(grads, which, index, value):
    value = value.astype(BF16).reshape(8, 2, SLAB, D)
    for half in range(2):
        grads[which, pl.ds(16 * half + 8 * index, 8)] = value[:, half]


class Copies:
    def __init__(self, sems):
        self.sems, self.used = sems, 0

    def start(self, source, target):
        copy = pltpu.make_async_copy(source, target, self.sems.at[self.used])
        self.used += 1
        copy.start()
        return copy

    def send(self, core, parity, source, own, other):
        sem = self.sems.at[self.used]
        self.used += 1
        here = pltpu.make_async_copy(source, own, sem)
        there = pltpu.make_async_copy(source, other, sem)
        pl.when(core == parity)(here.start)
        pl.when(core != parity)(there.start)
        return here


def position_rows(window, offset, count):
    shape = (count, window.shape[0])
    pick = lax.broadcasted_iota(jnp.int32, shape, 1) == (
        lax.broadcasted_iota(jnp.int32, shape, 0) + offset % 8
    )
    return dot(jnp.where(pick, 1.0, 0.0).astype(BF16), window)


def forward_kernel(
    ints, tokens, cotangent, small, up_bias, gathered,
    act_out, g2_out, saved_out, hidden_out, shares, sums,
    weights, down, window, act, hidden, h2, a3, gy, wide, y, da, sems,
):
    grads = weights
    length, row_offset, col_offset = ints[0], ints[1], ints[2]
    copies = Copies(sems)
    near = []
    for i in range(2):
        dev = jnp.minimum(row_offset // 8 + i, DEVICES - 1)
        near.append(
            copies.start(gathered.at[dev // 4, dev % 4, 96:104, :], window.at[8 * i : 8 * i + 8, :])
        )
    for i in range(9):
        dev = jnp.minimum(col_offset // 8 + i, DEVICES - 1)
        near.append(
            copies.start(
                gathered.at[dev // 4, dev % 4, 104:112, :], window.at[16 + 8 * i : 24 + 8 * i, :]
            )
        )
    loads = [
        copies.start(gathered.at[:, i % 4, 24 * (i // 4) : 24 * (i // 4) + 24, :], weights.at[i])
        for i in range(12)
    ]
    loads += [
        copies.start(gathered.at[8 * f : 8 * f + 8, :, 72:96, :], down.at[f]) for f in range(4)
    ]
    for copy in near:
        copy.wait()
    row_pos = position_rows(window[0:16, :], row_offset, ROWS)
    col_pos = position_rows(window[16:88, :], col_offset, COLS)
    for r in range(ROWS):
        rows = slice(r * COLS, (r + 1) * COLS)
        value = tokens[rows, :].astype(F32) + row_pos[r : r + 1, :] + col_pos
        hidden[0, rows, :] = value
        act[A1, rows, :] = norm(value, small, 0)
    stores = [copies.start(hidden.at[0], hidden_out.at[0]), copies.start(act.at[A1], saved_out.at[A1])]

    def branch(first, source, planes, heads, bias, target, which, last):
        for i in range(3):
            loads[first + i].wait()
        project(act, source, planes[:3], weights, first, small, bias)
        for plane in planes[:3]:
            stores.append(copies.start(act.at[plane], saved_out.at[plane]))
        attend(heads, act, *planes)
        stores.append(copies.start(act.at[planes[3]], saved_out.at[planes[3]]))
        loads[first + 3].wait()

        def body(index):
            rows = chunk(index, 256)
            branch_out = dot(act[planes[3], rows, :], whole(weights, first + 3))
            before = hidden[which - 1, rows, :]
            after = before + (branch_out + small[bias + 2 : bias + 3, :])
            if last:
                h2[rows, :] = after
                a3[rows, :] = norm(after, small, which)
            else:
                hidden[which, rows, :] = after
                act[target, rows, :] = norm(after, small, which)

        loop(2, body)

    branch(0, A1, (Q1, K1, V1, M1), RowHeads(length), ROW_BIAS, A2, 1, False)
    stores.append(copies.start(hidden.at[1], hidden_out.at[1]))
    stores.append(copies.start(act.at[A2], saved_out.at[A2]))
    branch(4, A2, (Q2, K2, V2, M2), ColHeads(), COL_BIAS, None, 2, True)

    in_use = lax.broadcasted_iota(jnp.int32, (COLS, D), 0) < length
    for r in range(ROWS):
        rows = slice(r * COLS, (r + 1) * COLS)
        gy[rows, :] = jnp.where(in_use, cotangent[rows, :].astype(F32), 0.0).astype(BF16)
    for copy in loads[8:]:
        copy.wait()

    def ffn(f):
        up, low = whole(weights, 8 + f), down[f].reshape(D, D)
        bias = up_bias[pl.ds(f, 1), :]

        def body(index):
            rows = chunk(index, 256)
            z = dot(a3[rows, :], up) + bias
            cdf = 0.5 * (1.0 + lax.erf(z * math.sqrt(0.5)))
            slope = cdf + z * (jnp.exp(-0.5 * z * z) * (1.0 / math.sqrt(2.0 * math.pi)))
            u = (z * cdf).astype(BF16)
            wide[0, rows, :] = u
            du = dot_nt(gy[rows, :], low).astype(BF16).astype(F32)
            dz = (du * slope).astype(BF16)
            wide[1, rows, :] = dz
            more, more_da = dot(u, low), dot_nt(dz, up)

            @pl.when(f == 0)
            def _():
                y[rows, :] = more
                da[rows, :] = more_da

            @pl.when(f != 0)
            def _():
                y[rows, :] += more
                da[rows, :] += more_da

        loop(2, body)
        sums[pl.ds(f, 1), :] = total(wide[1].astype(F32))

        def back(index):
            cols = chunk(index, 384)
            value = dot_tn(wide[0, :, cols], gy[...]).astype(BF16).reshape(2, 8, SLAB, D)
            for k in range(8):
                grads[4 + f, pl.ds(4 * k + 2 * index, 2)] = value[:, k]
            by_halves(grads, f, index, dot_tn(a3[:, cols], wide[1]))

        loop(2, back)
        for copy in ffn_sends(f):
            copy.start()

    first_sem = copies.used

    def ffn_sends(f):
        sends = []
        for half in range(2):
            place = (4 * half + f, slice(None), slice(0, SLAB))
            sends.append((grads.at[f, 16 * half : 16 * half + 16], shares.at[place]))
        for k in range(8):
            place = (k, pl.ds(4 * f, 4), slice(SLAB, 2 * SLAB))
            sends.append((grads.at[4 + f, 4 * k : 4 * k + 4], shares.at[place]))
        return [
            pltpu.make_async_copy(source, target, sems.at[first_sem + 10 * f + i])
            for i, (source, target) in enumerate(sends)
        ]

    loop(4, ffn)
    gain = small[GAIN + 2 : GAIN + 3, :]

    def finish(index, carry):
        rows = chunk(index, 64)
        late = h2[rows, :]
        act_out[rows, :] = (late + (y[rows, :] + small[DOWN_BIAS : DOWN_BIAS + 1, :])).astype(BF16)
        grad = da[rows, :]
        inner, unit = norm_back(grad, late, gain)
        cot = gy[rows, :].astype(F32)
        g2_out[rows, :] = cot + inner
        return carry[0] + total(unit), carry[1] + total(grad), carry[2] + total(cot)

    zero = jnp.zeros((1, D), F32)
    gain_sum, shift_sum, down_sum = lax.fori_loop(0, 8, finish, (zero, zero, zero))
    sums[4:5, :] = down_sum
    sums[5:6, :] = gain_sum
    sums[6:7, :] = shift_sum
    sums[7:8, :] = zero
    for copy in stores + [copy for f in range(4) for copy in ffn_sends(f)]:
        copy.wait()


def heads_kernel(column, ints, grad_in, gathered, saved, grads_out, weight, act, sems):
    first, planes = (24, (Q2, K2, V2)) if column else (0, (Q1, K1, V1))
    heads = ColHeads() if column else RowHeads(ints[0])
    copies = Copies(sems)
    load = copies.start(gathered.at[:, 3, first : first + SLAB, :], weight.at[0])
    act_loads = [copies.start(saved.at[plane], act.at[i]) for i, plane in enumerate(planes)]
    load.wait()

    def mixed_back(index):
        rows = chunk(index, 256)
        act[3, rows, :] = dot_nt(grad_in[rows, :].astype(BF16), whole(weight, 0)).astype(BF16)

    loop(2, mixed_back)
    for copy in act_loads:
        copy.wait()
    attend_back(heads, act, 0, 1, 2, 3)
    stores = [copies.start(act.at[i], grads_out.at[i]) for i in range(3)]
    for copy in stores:
        copy.wait()


class Shares:
    def __init__(self, core, copies, own, other):
        self.core, self.copies, self.own, self.other, self.sent = core, copies, own, other, []

    def send(self, grads, member):
        every, parity = slice(None), member % 2
        for half in range(2):
            x = 2 * half + member // 2
            if parity == 0:
                places = [(grads.at[member, half], (every, every, x))]
            else:
                places = [(grads.at[member, half, y], (every, y, x)) for y in range(4)]
            for source, place in places:
                self.sent.append(
                    self.copies.send(self.core, parity, source, self.own.at[place], self.other.at[place])
                )

    def wait(self):
        for copy in self.sent:
            copy.wait()


def keep(grads, which, part, value):
    value = value.astype(BF16).reshape(2, 4, 2, SLAB, D)
    for half in range(2):
        grads[which, half, pl.ds(2 * part, 2)] = value[:, :, half]


def weight_grads(loads, grad_in, act, out_grad, normed, mixed, grads, shares):
    def low(index):
        rows = chunk(index, 128)
        out_grad[rows, :] = grad_in[rows, :].astype(BF16)

    loop(4, low)
    loads["mixed"].wait()

    def out_back(index):
        keep(grads, 3, index, dot_tn(mixed[:, chunk(index, 384)], out_grad[...]))

    loop(2, out_back)
    shares.send(grads, 3)
    loads["normed"].wait()
    for i in range(3):
        loads[i].wait()

    def weight_back(index):
        which, part = index // 2, index % 2
        keep(grads, which, part, dot_tn(normed[:, chunk(part, 384)], act[which]))

    loop(6, weight_back)
    for member in range(3):
        shares.send(grads, member)


def input_grads(loads, grad_in, gain, act, weights, hidden, da, grad_out, sums, lines=None):
    for i in range(3):
        for copy in loads["inputs"][i]:
            copy.wait()

        def input_back(index):
            rows = chunk(index, 256)
            value = dot_nt(act[i, rows, :], whole(weights, i))
            da[rows, :] = value if i == 0 else da[rows, :] + value

        loop(2, input_back)
    loads["hidden"].wait()

    def finish(index, carry):
        rows = chunk(index, 64)
        grad, before = da[rows, :], grad_in[rows, :]
        inner, unit = norm_back(grad, hidden[rows, :], gain)
        value = before + inner
        grad_out[rows, :] = value
        added = [unit, grad, act[0, rows, :], act[2, rows, :], before.astype(BF16)]
        added = [total(extra.astype(F32)) for extra in added]
        if lines is not None:
            lines[pl.ds(index, 1), :] = total(value)
            added.append(value)
        return tuple(a + b for a, b in zip(carry, added))

    carry = (jnp.zeros((1, D), F32),) * 5
    if lines is not None:
        carry = carry + (jnp.zeros((COLS, D), F32),)
    carry = lax.fori_loop(0, 8, finish, carry)
    for i in range(5):
        sums[i : i + 1, :] = carry[i]
    sums[5:8, :] = jnp.zeros((3, D), F32)
    return carry[-1]


def column_kernel(
    ints, grad_in, small, gathered, saved, hidden_saved, grads_in,
    grad_out, own, other, sums,
    weights, act, out_grad, normed, mixed, hidden, da, grads, sems,
):
    copies = Copies(sems)
    shares = Shares(ints[3], copies, own, other)
    loads = {"mixed": copies.start(saved.at[M2], mixed), "normed": copies.start(saved.at[A2], normed)}
    for i in range(3):
        loads[i] = copies.start(grads_in.at[i], act.at[i])
    loads["inputs"] = [
        [copies.start(gathered.at[:, i, SLAB : 2 * SLAB, :], weights.at[i])] for i in range(3)
    ]
    loads["hidden"] = copies.start(hidden_saved.at[1], hidden)
    weight_grads(loads, grad_in, act, out_grad, normed, mixed, grads, shares)
    input_grads(loads, grad_in, small[GAIN + 1 : GAIN + 2, :], act, weights, hidden, da, grad_out, sums)
    shares.wait()


def row_weights_kernel(
    ints, grad_in, saved, grads_in, own, other, act, out_grad, normed, mixed, grads, sems
):
    copies = Copies(sems)
    shares = Shares(ints[3], copies, own, other)
    loads = {"mixed": copies.start(saved.at[M1], mixed), "normed": copies.start(saved.at[A1], normed)}
    for i in range(3):
        loads[i] = copies.start(grads_in.at[i], act.at[i])
    weight_grads(loads, grad_in, act, out_grad, normed, mixed, grads, shares)
    shares.wait()


def small_lines(sums, sums_col, sums_ffn):
    lines = jnp.concatenate([sums[0:5, :], sums_col[0:5, :], sums_ffn[4:7, :], sums[5:8, :]], axis=0)
    shape = (DEVICES, D)
    dev, lane = (lax.broadcasted_iota(jnp.int32, shape, axis) for axis in (0, 1))
    packed = jnp.zeros((DEVICES, 128), F32)
    for j in range(6):
        pick = jnp.where(lane == 6 * dev + j, 1.0, 0.0).astype(BF16)
        blank = [jnp.zeros((16, D), F32)] * 8
        blank[j] = lines
        packed = packed + dot_nt(pick, jnp.concatenate(blank, axis=0).astype(BF16))
    up = jnp.concatenate(
        [jnp.broadcast_to(sums_ffn[f : f + 1, :], (32, D)) for f in range(4)], axis=0
    )
    first = 24 * (dev & 31)
    up = jnp.where((lane >= first) & (lane < first + 24), up, 0.0).astype(BF16)
    shape = (128, D)
    to, lane = (lax.broadcasted_iota(jnp.int32, shape, axis) for axis in (0, 1))
    fold = jnp.where(to - 96 == lane % 24, 1.0, 0.0).astype(BF16)
    return (packed + dot_nt(up, fold)).astype(BF16)


def row_input_kernel(
    ints, grad_in, small, sums_col, sums_ffn, gathered, hidden_saved, grads_in,
    grad_out, own, other,
    weights, act, hidden, da, zeros, table, lines, sums, owned_lines, sems,
):
    copies = Copies(sems)
    loads = {"inputs": []}
    for i in range(3):
        slab = gathered.at[:, i, 0:SLAB, :]
        loads["inputs"].append(
            [copies.start(grads_in.at[i], act.at[i]), copies.start(slab, weights.at[i])]
        )
    loads["hidden"] = copies.start(hidden_saved.at[0], hidden)
    zeros[...] = jnp.zeros_like(zeros)
    fills = [copies.start(zeros, out) for out in (own, other)]
    gain = small[GAIN : GAIN + 1, :]
    col_lines = input_grads(loads, grad_in, gain, act, weights, hidden, da, grad_out, sums, lines)
    packed = small_lines(sums, sums_col, sums_ffn).astype(F32).reshape(4, 4, 4, 2, 1, 128)
    owned_lines[...] = jnp.broadcast_to(packed, owned_lines.shape).astype(BF16)
    for copy in fills:
        copy.wait()
    sent = []
    every = slice(None)
    places = [(0, owned_lines.at[:, :, :, 0], (every, every))]
    places += [(1, owned_lines.at[y, :, :, 1], (every, y)) for y in range(4)]
    for parity, source, place in places:
        place = place + (every, slice(16, 24), slice(0, 128))
        sent.append(copies.send(ints[3], parity, source, own.at[place], other.at[place]))
    send_tables(ints, copies, lines[...], col_lines, table, own, other)
    for copy in sent:
        copy.wait()


def send_tables(ints, copies, row_lines, col_lines, table, own, other):
    core = ints[3]

    def placed(values, offset, count):
        shape = (count, values.shape[0])
        here = lax.broadcasted_iota(jnp.int32, shape, 0) == (
            lax.broadcasted_iota(jnp.int32, shape, 1) + offset % 8
        )
        return dot(jnp.where(here, 1.0, 0.0).astype(BF16), values.astype(BF16)).astype(BF16)

    spots = []
    for first, count, values, offset, start in (
        (0, 2, row_lines, ints[1], 0),
        (2, 9, col_lines, ints[2], 8),
    ):
        table[first : first + count] = placed(values, offset, 8 * count).reshape(count, 8, D)
        spots += [(first + i, offset // 8 + i, start) for i in range(count)]
    waits = []
    for slot, owner, start in spots:
        real, dev = owner < DEVICES, jnp.minimum(owner, DEVICES - 1)
        x, y, z = (dev // 2) % 4, dev // 32, (dev // 8) % 4
        odd = dev % 2 == 1
        place = (jnp.where(odd, z, y), jnp.where(odd, y, z), x, slice(start, start + 8))
        sem = copies.sems.at[copies.used]
        copies.used += 1
        here = pltpu.make_async_copy(table.at[slot], own.at[place], sem)
        there = pltpu.make_async_copy(table.at[slot], other.at[place], sem)
        pl.when(real & (dev % 2 == core))(here.start)
        pl.when(real & (dev % 2 != core))(there.start)
        waits.append((real, here))
    for real, copy in waits:
        pl.when(real)(copy.wait)


VMEM = pl.BlockSpec(memory_space=pltpu.VMEM)
ANY = pl.BlockSpec(memory_space=pl.ANY)
SMEM = pl.BlockSpec(memory_space=pltpu.SMEM)
SHAPE = jax.ShapeDtypeStruct


def params():
    return pltpu.CompilerParams(vmem_limit_bytes=62 * 1024 * 1024)


def cost(flops, traffic):
    return pl.CostEstimate(flops=flops, transcendentals=0, bytes_accessed=traffic)


def forward_call(ints, tokens, cotangent, small, up_bias, gathered):
    plane = (TOKENS, D)
    return pl.pallas_call(
        forward_kernel,
        name="forward",
        in_specs=[SMEM, VMEM, VMEM, VMEM, VMEM, ANY],
        out_shape=(
            SHAPE(plane, BF16),
            SHAPE(plane, F32),
            SHAPE((10,) + plane, BF16),
            SHAPE((2,) + plane, F32),
            SHAPE((8, 16, 2 * SLAB, D), BF16),
            SHAPE((8, D), F32),
        ),
        out_specs=(VMEM, VMEM, ANY, ANY, ANY, VMEM),
        scratch_shapes=[
            pltpu.VMEM((12, GROUPS, SLAB, D), BF16),
            pltpu.VMEM((4, 8, MEMBERS, SLAB, D), BF16),
            pltpu.VMEM((88, D), BF16),
            pltpu.VMEM((10,) + plane, BF16),
            pltpu.VMEM((2,) + plane, F32),
            pltpu.VMEM(plane, F32),
            pltpu.VMEM(plane, BF16),
            pltpu.VMEM(plane, BF16),
            pltpu.VMEM((2,) + plane, BF16),
            pltpu.VMEM(plane, F32),
            pltpu.VMEM(plane, F32),
            pltpu.SemaphoreType.DMA((96,)),
        ],
        compiler_params=params(),
        cost_estimate=cost(24 * 10**9, 50 * 10**6),
    )(ints, tokens, cotangent, small, up_bias, gathered)


def heads_call(column, ints, grad, gathered, saved):
    plane = (TOKENS, D)
    return pl.pallas_call(
        lambda *refs: heads_kernel(column, *refs),
        name="column_heads" if column else "row_heads",
        in_specs=[SMEM, VMEM, ANY, ANY],
        out_shape=SHAPE((3,) + plane, BF16),
        out_specs=ANY,
        scratch_shapes=[
            pltpu.VMEM((1, GROUPS, SLAB, D), BF16),
            pltpu.VMEM((4,) + plane, BF16),
            pltpu.SemaphoreType.DMA((8,)),
        ],
        compiler_params=params(),
        cost_estimate=cost(10**10, 10**7),
    )(ints, grad, gathered, saved)


PLANE = (TOKENS, D)


def share_of(rows):
    return SHAPE((4, 4, 4, rows, D), BF16)


def column_call(ints, grad, small, gathered, saved, hidden, grads):
    return pl.pallas_call(
        column_kernel,
        name="column_weights",
        in_specs=[SMEM, VMEM, VMEM, ANY, ANY, ANY, ANY],
        out_shape=(SHAPE(PLANE, F32), share_of(SLAB), share_of(SLAB), SHAPE((8, D), F32)),
        out_specs=(VMEM, ANY, ANY, VMEM),
        scratch_shapes=[
            pltpu.VMEM((3, GROUPS, SLAB, D), BF16),
            pltpu.VMEM((3,) + PLANE, BF16),
            pltpu.VMEM(PLANE, BF16),
            pltpu.VMEM(PLANE, BF16),
            pltpu.VMEM(PLANE, BF16),
            pltpu.VMEM(PLANE, F32),
            pltpu.VMEM(PLANE, F32),
            pltpu.VMEM((4, 2, 4, 4, SLAB, D), BF16),
            pltpu.SemaphoreType.DMA((32,)),
        ],
        compiler_params=params(),
        cost_estimate=cost(10**10, 10**7),
    )(ints, grad, small, gathered, saved, hidden, grads)


def row_weights_call(ints, grad, saved, grads):
    return pl.pallas_call(
        row_weights_kernel,
        name="row_weights",
        in_specs=[SMEM, VMEM, ANY, ANY],
        out_shape=(share_of(SLAB), share_of(SLAB)),
        out_specs=(ANY, ANY),
        scratch_shapes=[
            pltpu.VMEM((3,) + PLANE, BF16),
            pltpu.VMEM(PLANE, BF16),
            pltpu.VMEM(PLANE, BF16),
            pltpu.VMEM(PLANE, BF16),
            pltpu.VMEM((4, 2, 4, 4, SLAB, D), BF16),
            pltpu.SemaphoreType.DMA((32,)),
        ],
        compiler_params=params(),
        cost_estimate=cost(10**6, 10**5),
    )(ints, grad, saved, grads)


def row_input_call(ints, grad, small, sums_col, sums_ffn, gathered, hidden, grads):
    return pl.pallas_call(
        row_input_kernel,
        name="row_input",
        in_specs=[SMEM, VMEM, VMEM, VMEM, VMEM, ANY, ANY, ANY],
        out_shape=(SHAPE(PLANE, F32), share_of(SLAB), share_of(SLAB)),
        out_specs=(VMEM, ANY, ANY),
        scratch_shapes=[
            pltpu.VMEM((3, GROUPS, SLAB, D), BF16),
            pltpu.VMEM((3,) + PLANE, BF16),
            pltpu.VMEM(PLANE, F32),
            pltpu.VMEM(PLANE, F32),
            pltpu.VMEM((4, 4, 4, SLAB, D), BF16),
            pltpu.VMEM((11, 8, D), BF16),
            pltpu.VMEM((ROWS, D), F32),
            pltpu.VMEM((8, D), F32),
            pltpu.VMEM((4, 4, 4, 2, 8, 128), BF16),
            pltpu.SemaphoreType.DMA((48,)),
        ],
        compiler_params=params(),
        cost_estimate=cost(2 * 10**10, 10**7),
    )(ints, grad, small, sums_col, sums_ffn, gathered, hidden, grads)


def split_kernel(place, own, other, *pieces):
    for hop in range(4):
        to = (place[0] + hop) & 3

        def body(j):
            pieces[hop][j] = (own[to, j].astype(F32) + other[to, j].astype(F32)).astype(BF16)

        loop(4, body)


def split(own, other, place):
    return pl.pallas_call(
        split_kernel,
        name="split_shares",
        in_specs=[SMEM, VMEM, VMEM],
        out_shape=(SHAPE((4, 4, SLAB, D), BF16),) * 4,
        out_specs=(VMEM,) * 4,
        compiler_params=params(),
        cost_estimate=cost(10**6, 10**6),
    )(place, own, other)


def sum_of(pieces, *index):
    value = pieces[0][index].astype(F32)
    for piece in pieces[1:]:
        value = value + piece[index].astype(F32)
    return value


def second_kernel(place, *refs):
    groups, pieces = [refs[4 * g : 4 * g + 4] for g in range(3)], refs[12:]
    for hop in range(4):
        to = (place[0] + hop) & 3

        def body(j):
            for g, group in enumerate(groups):
                rows = slice(g * SLAB, (g + 1) * SLAB)
                pieces[hop][j, rows, :] = sum_of(group, to, j).astype(BF16)

        loop(4, body)


def second_split(row, table, col, place):
    return pl.pallas_call(
        second_kernel,
        name="second_split",
        in_specs=[SMEM] + [VMEM] * 12,
        out_shape=(SHAPE((4, 3 * SLAB, D), BF16),) * 4,
        out_specs=(VMEM,) * 4,
        compiler_params=params(),
        cost_estimate=cost(10**6, 10**6),
    )(place, *row, *table, *col)


def third_kernel(place, *refs):
    for hop in range(4):
        refs[4 + hop][...] = sum_of(refs[:4], (place[0] + hop) & 3).astype(BF16)


def third_split(rows, place):
    return pl.pallas_call(
        third_kernel,
        name="third_split",
        in_specs=[SMEM] + [VMEM] * 4,
        out_shape=(SHAPE((3 * SLAB, D), BF16),) * 4,
        out_specs=(VMEM,) * 4,
        compiler_params=params(),
        cost_estimate=cost(10**6, 10**6),
    )(place, *rows)


def last_kernel(me, *refs):
    parts, ffn, (down, tables, line), pieces, held = refs[:4], refs[4:8], refs[8:11], refs[11:15], refs[15]
    down[...] = sum_of(ffn, slice(SLAB, 2 * SLAB))
    for i in range(2):
        rows = slice(SLAB + 8 * i, SLAB + 8 * i + 8)
        tables[i] = sum_of(parts, rows)
    line[...] = sum_of(parts, slice(SLAB + 16, SLAB + 24))
    for kind, (source, start) in enumerate(((parts, 0), (parts, 2 * SLAB), (ffn, 0))):
        value = sum_of(source, slice(start, start + SLAB))
        for member in range(MEMBERS):
            held[member, kind] = value[6 * member : 6 * member + 6, :]
    for flip in range(4):
        pieces[flip][...] = held[me[0] ^ flip].astype(BF16)


def last_split(me, rows, ffn):
    return pl.pallas_call(
        last_kernel,
        name="last_split",
        in_specs=[SMEM] + [VMEM] * 8,
        out_shape=(
            SHAPE((SLAB, D), F32),
            SHAPE((2, 8, D), F32),
            SHAPE((8, D), F32),
        )
        + (SHAPE((3, 6, D), BF16),) * 4,
        out_specs=(VMEM,) * 7,
        scratch_shapes=[pltpu.VMEM((MEMBERS, 3, 6, D), F32)],
        compiler_params=params(),
        cost_estimate=cost(10**6, 10**6),
    )(me, *rows, *ffn)


def outputs_kernel(me, one, two, three, four, row_qkv, row_out, col_qkv, col_out, up, held):
    for flip, piece in enumerate((one, two, three, four)):
        held[me[0] ^ flip] = piece[...].astype(F32)
    for i in range(3):
        row_qkv[i], col_qkv[i] = held[i, 0], held[i, 1]
    row_out[...], col_out[...] = held[3, 0], held[3, 1]
    for i in range(MEMBERS):
        up[:, i * D : (i + 1) * D] = held[i, 2]


def outputs(me, pieces):
    return pl.pallas_call(
        outputs_kernel,
        name="outputs",
        in_specs=[SMEM] + [VMEM] * 4,
        out_shape=(
            SHAPE((3, 6, D), F32),
            SHAPE((6, D), F32),
            SHAPE((3, 6, D), F32),
            SHAPE((6, D), F32),
            SHAPE((6, FF), F32),
        ),
        out_specs=(VMEM,) * 5,
        scratch_shapes=[pltpu.VMEM((MEMBERS, 3, 6, D), F32)],
        compiler_params=params(),
        cost_estimate=cost(10**6, 10**6),
    )(me, *pieces)


def take(value, index, dim):
    return lax.squeeze(lax.dynamic_slice_in_dim(value, index, 1, dim), (dim,))


def member():
    return (lax.axis_index("x") % 2) * 2 + lax.axis_index("c")


def trade(pieces):
    came = [pieces[0]]
    for flip in range(1, 4):
        pairs = [(i, (i // 4) * 4 + ((i % 4) ^ flip)) for i in range(8)]
        came.append(lax.ppermute(pieces[flip], ("x", "c"), pairs))
    return came


def exchange(blocks):
    me = member()
    parts = trade([take(blocks, me ^ flip, 0) for flip in range(4)])
    odd, high = (me & 1) == 1, (me & 2) == 2
    pairs = [jnp.where(odd, parts[i ^ 1], parts[i]) for i in range(4)]
    return [jnp.where(high, pairs[i ^ 2], pairs[i]) for i in range(4)]


def swap(value):
    return lax.ppermute(value, "c", [(0, 1), (1, 0)])


def scatter_chip_rows(shares):
    return lax.psum_scatter(shares, ("x", "c"), scatter_dimension=0, tiled=False)


STAGES = (("y", "z"), ("z", "y"), ("x", "x"))
STRIDES = {"y": 32, "z": 8, "x": 2}


def place_on(axes):
    here = jnp.where(lax.axis_index("c") == 0, lax.axis_index(axes[0]), lax.axis_index(axes[1]))
    return here.astype(jnp.int32)[None]


def deliver(pieces, axes):
    came = [pieces[0]]
    for hop in range(1, 4):
        pairs = []
        for dev in range(DEVICES):
            stride = STRIDES[axes[dev % 2]]
            at = dev // stride % 4
            pairs.append((dev, dev + ((at + hop) % 4 - at) * stride))
        came.append(lax.ppermute(pieces[hop], AXES, pairs))
    return came


def gather(norm_gain, norm_bias, row_qkv, row_out, row_bias, col_qkv, col_out, col_bias,
           ffn_up, up_bias, ffn_down, down_bias, pos_tables):
    row = jnp.concatenate([row_qkv, row_out[None]], axis=0)
    col = jnp.concatenate([col_qkv, col_out[None]], axis=0)
    up = ffn_up.reshape(6, MEMBERS, D).transpose(1, 0, 2)
    slabs = jnp.stack(exchange(jnp.stack([row, col, up], axis=1)), axis=1)
    packed = jnp.concatenate(
        [slabs.reshape(3 * SLAB, D), ffn_down, pos_tables[0], pos_tables[1]], axis=0
    )
    gathered = lax.all_gather(packed, AXES, axis=0, tiled=False)
    sixes = jnp.concatenate([norm_gain, norm_bias, row_bias, col_bias, down_bias[None]], axis=0)
    line = jnp.pad(jnp.concatenate([sixes.reshape(-1), up_bias]), (0, 26))
    lines = lax.all_gather(line, AXES, axis=0, tiled=False).astype(F32)
    small = lines[:, :78].reshape(DEVICES, 13, 6).transpose(1, 0, 2).reshape(13, D)
    small = jnp.pad(small, ((0, 3), (0, 0)))
    return gathered.reshape(GROUPS, MEMBERS, PACK, D), small, lines[:, 78:102].reshape(4, D)


def on_device(tokens, cotangent, lengths, row_offset, col_offset, *weights):
    gathered, small, up_bias = gather(*weights)
    core = lax.axis_index("c").astype(jnp.int32)
    ints = jnp.concatenate([lengths, row_offset, col_offset, core[None]])
    act, g2, saved, hidden, ffn_shares, ffn_sums = forward_call(
        ints, tokens.reshape(TOKENS, D), cotangent.reshape(TOKENS, D), small, up_bias, gathered
    )
    barrier = lax.optimization_barrier
    ffn = scatter_chip_rows(ffn_shares)
    col_heads = heads_call(True, ints, g2, gathered, saved)
    g1, own, other, col_sums = column_call(ints, g2, small, gathered, saved, hidden, col_heads)
    row_heads = heads_call(False, ints, g1, gathered, saved)
    places = [place_on(axes) for axes in STAGES]
    other, row_heads = barrier((swap(other), row_heads))
    pieces, row_heads = barrier((split(own, other, places[0]), row_heads))
    col = deliver(pieces, STAGES[0])
    g0, table_own, table_other = row_input_call(
        ints, g1, small, col_sums, ffn_sums, gathered, hidden, row_heads
    )
    own, other = row_weights_call(ints, g1, saved, row_heads)
    table_other, col = barrier((table_other, col))
    other, table_other, ffn = barrier((other, swap(table_other), ffn))
    ffn = lax.psum_scatter(ffn.reshape(4, 4, 2 * SLAB, D), "y", scatter_dimension=0, tiled=False)
    table = deliver(split(table_own, table_other, places[0]), STAGES[0])
    row = deliver(split(own, swap(other), places[0]), STAGES[0])
    rows = deliver(second_split(row, table, col, places[1]), STAGES[1])
    z = lax.axis_index("z")
    ffn = deliver([take(ffn, (z + hop) % 4, 0) for hop in range(4)], ("z", "z"))
    rows = deliver(third_split(rows, places[2]), STAGES[2])
    return (act.reshape(tokens.shape), g0.reshape(tokens.shape)) + owned(rows, ffn)


def owned(rows, ffn):
    me = member().astype(jnp.int32)[None]
    down, tables, line, *pieces = last_split(me, rows, ffn)
    row_qkv, row_out, col_qkv, col_out, up = outputs(me, trade(pieces))
    sixes = line[0, :96].reshape(6, 16).T
    row_sums, col_sums, ffn_sums = sixes[0:5], sixes[5:10], sixes[10:13]
    gain = jnp.stack([row_sums[0], col_sums[0], ffn_sums[1]])
    shift_grad = jnp.stack([row_sums[1], col_sums[1], ffn_sums[2]])
    return (
        gain,
        shift_grad,
        row_qkv,
        row_out,
        row_sums[2:5],
        col_qkv,
        col_out,
        col_sums[2:5],
        up,
        line[0, 96:120],
        down,
        ffn_sums[0],
        tables,
    )


def solution(mesh):
    mesh = Mesh(mesh.devices.reshape(4, 4, 4, 2), AXES)
    first, second = P(AXES), P(None, AXES)
    weights = (second, second, second, first, second, second, first, second) + (first,) * 4 + (second,)
    return jax.shard_map(
        on_device,
        mesh=mesh,
        in_specs=(first,) * 5 + weights,
        out_specs=(first, first) + weights,
        check_vma=False,
    )
```

```python
import math

import jax
import jax.numpy as jnp
from jax import lax
from jax.experimental import pallas as pl
from jax.experimental.pallas import tpu as pltpu
from jax.sharding import Mesh, PartitionSpec as P

AXES = ("y", "z", "x", "c")
DEVICES = 128
GROUPS = 32
MEMBERS = 4
D = 768
FF = 3072
HEAD_DIM = 64
POSITIONS = 1024
ROWS = 8
COLS = 64
TOKENS = ROWS * COLS
SLAB = 24
WIDE = D + 128
PACK = 112
PAIRS = 6
EPS = 1e-05
MASKED = -1e30
ROW_SCALE = 1.0 / math.sqrt(HEAD_DIM * ROWS)
COL_SCALE = 1.0 / math.sqrt(HEAD_DIM)
BF16 = jnp.bfloat16
F32 = jnp.float32
GAIN, SHIFT, ROW_BIAS, COL_BIAS, DOWN_BIAS = 0, 3, 6, 9, 12
A1, Q1, K1, V1, M1, A2, Q2, K2, V2, M2 = range(10)


def dot(left, right):
    return jnp.dot(left, right, preferred_element_type=F32)


def dot_nt(left, right):
    return lax.dot_general(left, right, (((1,), (1,)), ((), ())), preferred_element_type=F32)


def dot_tn(left, right):
    return lax.dot_general(left, right, (((0,), (0,)), ((), ())), preferred_element_type=F32)


def chunk(index, size):
    return pl.ds(pl.multiple_of(index * size, size), size)


def loop(count, body, unroll=1):
    def step(index, carry):
        body(index)
        return carry

    lax.fori_loop(0, count, step, 0, unroll=unroll)


def unit_of(hidden):
    centred = hidden - jnp.mean(hidden, axis=-1, keepdims=True)
    inverse = lax.rsqrt(jnp.mean(centred * centred, axis=-1, keepdims=True) + EPS)
    return centred * inverse, inverse


def norm(hidden, small, which):
    unit, _ = unit_of(hidden)
    gain, shift = small[GAIN + which : GAIN + which + 1, :], small[SHIFT + which : SHIFT + which + 1, :]
    return (unit * gain + shift).astype(BF16)


def norm_back(grad, hidden, gain):
    unit, inverse = unit_of(hidden)
    inner = grad * gain
    mean = jnp.mean(inner, axis=-1, keepdims=True)
    cross = jnp.mean(inner * unit, axis=-1, keepdims=True)
    return inverse * (inner - mean - unit * cross), grad * unit


def total(value):
    return jnp.sum(value, axis=0, keepdims=True)


def first_head(shape):
    return (lax.broadcasted_iota(jnp.int32, shape, 1) & 127) < HEAD_DIM


def stack_heads(value):
    keep = jnp.where(first_head(value.shape), 1.0, 0.0)
    return jnp.concatenate([value * keep.astype(BF16), value * (1.0 - keep).astype(BF16)], axis=0)


def merge_heads(value):
    half = value.shape[0] // 2
    return jnp.where(first_head((half, value.shape[1])), value[:half], value[half:])


def softmax(scores):
    top = jnp.max(scores, axis=-1, keepdims=True)
    raised = jnp.exp(scores - top)
    return raised / jnp.sum(raised, axis=-1, keepdims=True)


class RowHeads:
    scale = ROW_SCALE
    steps = 2

    def __init__(self, length):
        self.length = length

    def blocks(self, step):
        return [chunk(3 * step + i, 128) for i in range(3)]

    def load(self, ref, plane, lanes):
        return jnp.concatenate(
            [ref[plane, r * COLS : (r + 1) * COLS, lanes] for r in range(ROWS)], axis=1
        )

    def store(self, ref, plane, lanes, value):
        for r in range(ROWS):
            ref[plane, r * COLS : (r + 1) * COLS, lanes] = value[:, r * 128 : (r + 1) * 128]

    def mask(self):
        shape = (2 * COLS, COLS)
        return lax.broadcasted_iota(jnp.int32, shape, 1) < self.length


class ColHeads:
    scale = COL_SCALE
    steps = PAIRS

    def blocks(self, step):
        return [(i * 16, chunk(step, 128)) for i in range(4)]

    def load(self, ref, plane, block):
        start, lanes = block
        return jnp.concatenate(
            [ref[plane, r * COLS + start : r * COLS + start + 16, lanes] for r in range(ROWS)], axis=0
        )

    def store(self, ref, plane, block, value):
        start, lanes = block
        for r in range(ROWS):
            ref[plane, r * COLS + start : r * COLS + start + 16, lanes] = value[16 * r : 16 * r + 16]

    def mask(self):
        row = lax.broadcasted_iota(jnp.int32, (256, 128), 0) & 15
        return row == (lax.broadcasted_iota(jnp.int32, (256, 128), 1) & 15)


def each(function, *lists):
    return [function(*values) for values in zip(*lists)]


def weights_of(heads, queries, keys):
    mask = heads.mask()
    scores = each(dot_nt, queries, keys)
    return each(lambda s: softmax(jnp.where(mask, s * heads.scale, MASKED)), scores)


def attend(heads, ref, q, k, v, m):
    def body(step):
        blocks = heads.blocks(step)
        queries, keys, values = (
            [heads.load(ref, plane, block) for block in blocks] for plane in (q, k, v)
        )
        probs = weights_of(heads, each(stack_heads, queries), keys)
        mixed = each(lambda p, value: dot(p.astype(BF16), value), probs, values)
        for block, value in zip(blocks, mixed):
            heads.store(ref, m, block, merge_heads(value).astype(BF16))

    loop(heads.steps, body)


def attend_back(heads, ref, q, k, v, dm):
    def body(step):
        blocks = heads.blocks(step)
        queries, keys, values, mixed = (
            [heads.load(ref, plane, block) for block in blocks] for plane in (q, k, v, dm)
        )
        queries, mixed = each(stack_heads, queries), each(stack_heads, mixed)
        probs = weights_of(heads, queries, keys)
        grad = each(dot_nt, mixed, values)
        grad_values = each(lambda p, value: dot_tn(p.astype(BF16), value), probs, mixed)
        inner = each(
            lambda p, g: (p * (g - jnp.sum(g * p, axis=-1, keepdims=True))).astype(BF16), probs, grad
        )
        grad_queries = each(lambda i, key: merge_heads(dot(i, key)) * heads.scale, inner, keys)
        grad_keys = each(lambda i, query: dot_tn(i, query) * heads.scale, inner, queries)
        for i, block in enumerate(blocks):
            heads.store(ref, q, block, grad_queries[i].astype(BF16))
            heads.store(ref, k, block, grad_keys[i].astype(BF16))
            heads.store(ref, v, block, grad_values[i].astype(BF16))

    loop(heads.steps, body)


def whole(ref, index):
    return ref[index].reshape(D, D)


def project(ref, source, planes, weights, first, small, bias_row):
    def body(index):
        rows = chunk(index, 256)
        normed = ref[source, rows, :]
        for i, plane in enumerate(planes):
            value = dot(normed, whole(weights, first + i))
            if i != 1:
                row = bias_row + (0 if i == 0 else 1)
                value = value + small[row : row + 1, :]
            ref[plane, rows, :] = value.astype(BF16)

    loop(2, body)


def by_halves(grads, which, index, value):
    value = value.astype(BF16).reshape(8, 2, SLAB, D)
    for half in range(2):
        grads[which, pl.ds(16 * half + 8 * index, 8)] = value[:, half]


class Copies:
    def __init__(self, sems):
        self.sems, self.used = sems, 0

    def start(self, source, target):
        copy = pltpu.make_async_copy(source, target, self.sems.at[self.used])
        self.used += 1
        copy.start()
        return copy

    def send(self, core, parity, source, own, other):
        sem = self.sems.at[self.used]
        self.used += 1
        here = pltpu.make_async_copy(source, own, sem)
        there = pltpu.make_async_copy(source, other, sem)
        pl.when(core == parity)(here.start)
        pl.when(core != parity)(there.start)
        return here


def position_rows(window, offset, count):
    shape = (count, window.shape[0])
    pick = lax.broadcasted_iota(jnp.int32, shape, 1) == (
        lax.broadcasted_iota(jnp.int32, shape, 0) + offset % 8
    )
    return dot(jnp.where(pick, 1.0, 0.0).astype(BF16), window)


def forward_kernel(
    ints, tokens, cotangent, small, up_bias, gathered,
    act_out, g2_out, saved_out, hidden_out, shares, sums,
    weights, down, window, act, hidden, h2, a3, gy, wide, y, da, sems,
):
    grads = weights
    length, row_offset, col_offset = ints[0], ints[1], ints[2]
    copies = Copies(sems)
    near = []
    for i in range(2):
        dev = jnp.minimum(row_offset // 8 + i, DEVICES - 1)
        near.append(
            copies.start(gathered.at[dev // 4, dev % 4, 96:104, :], window.at[8 * i : 8 * i + 8, :])
        )
    for i in range(9):
        dev = jnp.minimum(col_offset // 8 + i, DEVICES - 1)
        near.append(
            copies.start(
                gathered.at[dev // 4, dev % 4, 104:112, :], window.at[16 + 8 * i : 24 + 8 * i, :]
            )
        )
    loads = [
        copies.start(gathered.at[:, i % 4, 24 * (i // 4) : 24 * (i // 4) + 24, :], weights.at[i])
        for i in range(12)
    ]
    loads += [
        copies.start(gathered.at[8 * f : 8 * f + 8, :, 72:96, :], down.at[f]) for f in range(4)
    ]
    for copy in near:
        copy.wait()
    row_pos = position_rows(window[0:16, :], row_offset, ROWS)
    col_pos = position_rows(window[16:88, :], col_offset, COLS)
    for r in range(ROWS):
        rows = slice(r * COLS, (r + 1) * COLS)
        value = tokens[rows, :].astype(F32) + row_pos[r : r + 1, :] + col_pos
        hidden[0, rows, :] = value
        act[A1, rows, :] = norm(value, small, 0)
    stores = [copies.start(hidden.at[0], hidden_out.at[0]), copies.start(act.at[A1], saved_out.at[A1])]

    def branch(first, source, planes, heads, bias, target, which, last):
        for i in range(3):
            loads[first + i].wait()
        project(act, source, planes[:3], weights, first, small, bias)
        for plane in planes[:3]:
            stores.append(copies.start(act.at[plane], saved_out.at[plane]))
        attend(heads, act, *planes)
        stores.append(copies.start(act.at[planes[3]], saved_out.at[planes[3]]))
        loads[first + 3].wait()

        def body(index):
            rows = chunk(index, 256)
            branch_out = dot(act[planes[3], rows, :], whole(weights, first + 3))
            before = hidden[which - 1, rows, :]
            after = before + (branch_out + small[bias + 2 : bias + 3, :])
            if last:
                h2[rows, :] = after
                a3[rows, :] = norm(after, small, which)
            else:
                hidden[which, rows, :] = after
                act[target, rows, :] = norm(after, small, which)

        loop(2, body)

    branch(0, A1, (Q1, K1, V1, M1), RowHeads(length), ROW_BIAS, A2, 1, False)
    stores.append(copies.start(hidden.at[1], hidden_out.at[1]))
    stores.append(copies.start(act.at[A2], saved_out.at[A2]))
    branch(4, A2, (Q2, K2, V2, M2), ColHeads(), COL_BIAS, None, 2, True)

    in_use = lax.broadcasted_iota(jnp.int32, (COLS, D), 0) < length
    for r in range(ROWS):
        rows = slice(r * COLS, (r + 1) * COLS)
        gy[rows, :] = jnp.where(in_use, cotangent[rows, :].astype(F32), 0.0).astype(BF16)
    for copy in loads[8:]:
        copy.wait()

    def ffn(f):
        up, low = whole(weights, 8 + f), down[f].reshape(D, D)
        bias = up_bias[pl.ds(f, 1), :]

        def body(index):
            rows = chunk(index, 256)
            z = dot(a3[rows, :], up) + bias
            cdf = 0.5 * (1.0 + lax.erf(z * math.sqrt(0.5)))
            slope = cdf + z * (jnp.exp(-0.5 * z * z) * (1.0 / math.sqrt(2.0 * math.pi)))
            u = (z * cdf).astype(BF16)
            wide[0, rows, :] = u
            du = dot_nt(gy[rows, :], low).astype(BF16).astype(F32)
            dz = (du * slope).astype(BF16)
            wide[1, rows, :] = dz
            more, more_da = dot(u, low), dot_nt(dz, up)

            @pl.when(f == 0)
            def _():
                y[rows, :] = more
                da[rows, :] = more_da

            @pl.when(f != 0)
            def _():
                y[rows, :] += more
                da[rows, :] += more_da

        loop(2, body)
        sums[pl.ds(f, 1), :] = total(wide[1].astype(F32))

        def back(index):
            cols = chunk(index, 384)
            value = dot_tn(wide[0, :, cols], gy[...]).astype(BF16).reshape(2, 8, SLAB, D)
            for k in range(8):
                grads[4 + f, pl.ds(4 * k + 2 * index, 2)] = value[:, k]
            by_halves(grads, f, index, dot_tn(a3[:, cols], wide[1]))

        loop(2, back)
        for copy in ffn_sends(f):
            copy.start()

    first_sem = copies.used

    def ffn_sends(f):
        sends = []
        for half in range(2):
            place = (4 * half + f, slice(None), slice(0, SLAB))
            sends.append((grads.at[f, 16 * half : 16 * half + 16], shares.at[place]))
        for k in range(8):
            place = (k, pl.ds(4 * f, 4), slice(SLAB, 2 * SLAB))
            sends.append((grads.at[4 + f, 4 * k : 4 * k + 4], shares.at[place]))
        return [
            pltpu.make_async_copy(source, target, sems.at[first_sem + 10 * f + i])
            for i, (source, target) in enumerate(sends)
        ]

    loop(4, ffn)
    gain = small[GAIN + 2 : GAIN + 3, :]

    def finish(index, carry):
        rows = chunk(index, 64)
        late = h2[rows, :]
        act_out[rows, :] = (late + (y[rows, :] + small[DOWN_BIAS : DOWN_BIAS + 1, :])).astype(BF16)
        grad = da[rows, :]
        inner, unit = norm_back(grad, late, gain)
        cot = gy[rows, :].astype(F32)
        g2_out[rows, :] = cot + inner
        return carry[0] + total(unit), carry[1] + total(grad), carry[2] + total(cot)

    zero = jnp.zeros((1, D), F32)
    gain_sum, shift_sum, down_sum = lax.fori_loop(0, 8, finish, (zero, zero, zero))
    sums[4:5, :] = down_sum
    sums[5:6, :] = gain_sum
    sums[6:7, :] = shift_sum
    sums[7:8, :] = zero
    for copy in stores + [copy for f in range(4) for copy in ffn_sends(f)]:
        copy.wait()


def heads_kernel(column, ints, grad_in, gathered, saved, grads_out, weight, act, sems):
    first, planes = (24, (Q2, K2, V2)) if column else (0, (Q1, K1, V1))
    heads = ColHeads() if column else RowHeads(ints[0])
    copies = Copies(sems)
    load = copies.start(gathered.at[:, 3, first : first + SLAB, :], weight.at[0])
    act_loads = [copies.start(saved.at[plane], act.at[i]) for i, plane in enumerate(planes)]
    load.wait()

    def mixed_back(index):
        rows = chunk(index, 256)
        act[3, rows, :] = dot_nt(grad_in[rows, :].astype(BF16), whole(weight, 0)).astype(BF16)

    loop(2, mixed_back)
    for copy in act_loads:
        copy.wait()
    attend_back(heads, act, 0, 1, 2, 3)
    stores = [copies.start(act.at[i], grads_out.at[i]) for i in range(3)]
    for copy in stores:
        copy.wait()


class Shares:
    def __init__(self, core, copies, own, other):
        self.core, self.copies, self.own, self.other, self.sent = core, copies, own, other, []

    def send(self, grads, member):
        every, parity = slice(None), member % 2
        for half in range(2):
            x = 2 * half + member // 2
            if parity == 0:
                places = [(grads.at[member, half], (every, every, x))]
            else:
                places = [(grads.at[member, half, y], (every, y, x)) for y in range(4)]
            for source, place in places:
                self.sent.append(
                    self.copies.send(self.core, parity, source, self.own.at[place], self.other.at[place])
                )

    def wait(self):
        for copy in self.sent:
            copy.wait()


def keep(grads, which, part, value):
    value = value.astype(BF16).reshape(2, 4, 2, SLAB, D)
    for half in range(2):
        grads[which, half, pl.ds(2 * part, 2)] = value[:, :, half]


def weight_grads(loads, grad_in, act, out_grad, normed, mixed, grads, shares):
    def low(index):
        rows = chunk(index, 128)
        out_grad[rows, :] = grad_in[rows, :].astype(BF16)

    loop(4, low)
    loads["mixed"].wait()

    def out_back(index):
        keep(grads, 3, index, dot_tn(mixed[:, chunk(index, 384)], out_grad[...]))

    loop(2, out_back)
    shares.send(grads, 3)
    loads["normed"].wait()
    for i in range(3):
        loads[i].wait()

    def weight_back(index):
        which, part = index // 2, index % 2
        keep(grads, which, part, dot_tn(normed[:, chunk(part, 384)], act[which]))

    loop(6, weight_back)
    for member in range(3):
        shares.send(grads, member)


def input_grads(loads, grad_in, gain, act, weights, hidden, da, grad_out, sums, lines=None):
    for i in range(3):
        for copy in loads["inputs"][i]:
            copy.wait()

        def input_back(index):
            rows = chunk(index, 256)
            value = dot_nt(act[i, rows, :], whole(weights, i))
            da[rows, :] = value if i == 0 else da[rows, :] + value

        loop(2, input_back)
    loads["hidden"].wait()

    def finish(index, carry):
        rows = chunk(index, 64)
        grad, before = da[rows, :], grad_in[rows, :]
        inner, unit = norm_back(grad, hidden[rows, :], gain)
        value = before + inner
        grad_out[rows, :] = value
        added = [unit, grad, act[0, rows, :], act[2, rows, :], before.astype(BF16)]
        added = [total(extra.astype(F32)) for extra in added]
        if lines is not None:
            lines[pl.ds(index, 1), :] = total(value)
            added.append(value)
        return tuple(a + b for a, b in zip(carry, added))

    carry = (jnp.zeros((1, D), F32),) * 5
    if lines is not None:
        carry = carry + (jnp.zeros((COLS, D), F32),)
    carry = lax.fori_loop(0, 8, finish, carry)
    for i in range(5):
        sums[i : i + 1, :] = carry[i]
    sums[5:8, :] = jnp.zeros((3, D), F32)
    return carry[-1]


def column_kernel(
    ints, grad_in, small, gathered, saved, hidden_saved, grads_in,
    grad_out, own, other, sums,
    weights, act, out_grad, normed, mixed, hidden, da, grads, sems,
):
    copies = Copies(sems)
    shares = Shares(ints[3], copies, own, other)
    loads = {"mixed": copies.start(saved.at[M2], mixed), "normed": copies.start(saved.at[A2], normed)}
    for i in range(3):
        loads[i] = copies.start(grads_in.at[i], act.at[i])
    loads["inputs"] = [
        [copies.start(gathered.at[:, i, SLAB : 2 * SLAB, :], weights.at[i])] for i in range(3)
    ]
    loads["hidden"] = copies.start(hidden_saved.at[1], hidden)
    weight_grads(loads, grad_in, act, out_grad, normed, mixed, grads, shares)
    input_grads(loads, grad_in, small[GAIN + 1 : GAIN + 2, :], act, weights, hidden, da, grad_out, sums)
    shares.wait()


def row_weights_kernel(
    ints, grad_in, saved, grads_in, own, other, act, out_grad, normed, mixed, grads, sems
):
    copies = Copies(sems)
    shares = Shares(ints[3], copies, own, other)
    loads = {"mixed": copies.start(saved.at[M1], mixed), "normed": copies.start(saved.at[A1], normed)}
    for i in range(3):
        loads[i] = copies.start(grads_in.at[i], act.at[i])
    weight_grads(loads, grad_in, act, out_grad, normed, mixed, grads, shares)
    shares.wait()


def small_lines(sums, sums_col, sums_ffn):
    lines = jnp.concatenate([sums[0:5, :], sums_col[0:5, :], sums_ffn[4:7, :], sums[5:8, :]], axis=0)
    shape = (DEVICES, D)
    dev, lane = (lax.broadcasted_iota(jnp.int32, shape, axis) for axis in (0, 1))
    packed = jnp.zeros((DEVICES, 128), F32)
    for j in range(6):
        pick = jnp.where(lane == 6 * dev + j, 1.0, 0.0).astype(BF16)
        blank = [jnp.zeros((16, D), F32)] * 8
        blank[j] = lines
        packed = packed + dot_nt(pick, jnp.concatenate(blank, axis=0).astype(BF16))
    up = jnp.concatenate(
        [jnp.broadcast_to(sums_ffn[f : f + 1, :], (32, D)) for f in range(4)], axis=0
    )
    first = 24 * (dev & 31)
    up = jnp.where((lane >= first) & (lane < first + 24), up, 0.0).astype(BF16)
    shape = (128, D)
    to, lane = (lax.broadcasted_iota(jnp.int32, shape, axis) for axis in (0, 1))
    fold = jnp.where(to - 96 == lane % 24, 1.0, 0.0).astype(BF16)
    return (packed + dot_nt(up, fold)).astype(BF16)


def row_input_kernel(
    ints, grad_in, small, sums_col, sums_ffn, gathered, hidden_saved, grads_in,
    grad_out, own, other,
    weights, act, hidden, da, zeros, table, lines, sums, owned_lines, sems,
):
    copies = Copies(sems)
    loads = {"inputs": []}
    for i in range(3):
        slab = gathered.at[:, i, 0:SLAB, :]
        loads["inputs"].append(
            [copies.start(grads_in.at[i], act.at[i]), copies.start(slab, weights.at[i])]
        )
    loads["hidden"] = copies.start(hidden_saved.at[0], hidden)
    zeros[...] = jnp.zeros_like(zeros)
    fills = [copies.start(zeros, out.at[:, :, :, :, 0:D]) for out in (own, other)]
    gain = small[GAIN : GAIN + 1, :]
    col_lines = input_grads(loads, grad_in, gain, act, weights, hidden, da, grad_out, sums, lines)
    packed = small_lines(sums, sums_col, sums_ffn).astype(F32).reshape(4, 4, 4, 2, 1, 128)
    owned_lines[...] = jnp.broadcast_to(packed, owned_lines.shape).astype(BF16)
    for copy in fills:
        copy.wait()
    sent = []
    for parity in range(2):
        for x in range(4):
            source, place = owned_lines.at[:, :, x, parity], (x, slice(None), slice(None), slice(0, 16), slice(D, WIDE))
            sent.append(copies.send(ints[3], parity, source, own.at[place], other.at[place]))
    send_tables(ints, copies, lines[...], col_lines, table, own, other)
    for copy in sent:
        copy.wait()


def send_tables(ints, copies, row_lines, col_lines, table, own, other):
    core = ints[3]

    def placed(values, offset, count):
        shape = (count, values.shape[0])
        here = lax.broadcasted_iota(jnp.int32, shape, 0) == (
            lax.broadcasted_iota(jnp.int32, shape, 1) + offset % 8
        )
        return dot(jnp.where(here, 1.0, 0.0).astype(BF16), values.astype(BF16)).astype(BF16)

    spots = []
    for first, count, values, offset, start in (
        (0, 2, row_lines, ints[1], 0),
        (2, 9, col_lines, ints[2], 8),
    ):
        table[first : first + count] = placed(values, offset, 8 * count).reshape(count, 8, D)
        spots += [(first + i, offset // 8 + i, start) for i in range(count)]
    waits = []
    for slot, owner, start in spots:
        real, dev = owner < DEVICES, jnp.minimum(owner, DEVICES - 1)
        x, y, z = (dev // 2) % 4, dev // 32, (dev // 8) % 4
        place = (x, y, z, slice(start, start + 8), slice(0, D))
        sem = copies.sems.at[copies.used]
        copies.used += 1
        here = pltpu.make_async_copy(table.at[slot], own.at[place], sem)
        there = pltpu.make_async_copy(table.at[slot], other.at[place], sem)
        pl.when(real & (dev % 2 == core))(here.start)
        pl.when(real & (dev % 2 != core))(there.start)
        waits.append((real, here))
    for real, copy in waits:
        pl.when(real)(copy.wait)


VMEM = pl.BlockSpec(memory_space=pltpu.VMEM)
ANY = pl.BlockSpec(memory_space=pl.ANY)
SMEM = pl.BlockSpec(memory_space=pltpu.SMEM)
SHAPE = jax.ShapeDtypeStruct


def params():
    return pltpu.CompilerParams(vmem_limit_bytes=62 * 1024 * 1024)


def cost(flops, traffic):
    return pl.CostEstimate(flops=flops, transcendentals=0, bytes_accessed=traffic)


def forward_call(ints, tokens, cotangent, small, up_bias, gathered):
    plane = (TOKENS, D)
    return pl.pallas_call(
        forward_kernel,
        name="forward",
        in_specs=[SMEM, VMEM, VMEM, VMEM, VMEM, ANY],
        out_shape=(
            SHAPE(plane, BF16),
            SHAPE(plane, F32),
            SHAPE((10,) + plane, BF16),
            SHAPE((2,) + plane, F32),
            SHAPE((8, 16, 2 * SLAB, D), BF16),
            SHAPE((8, D), F32),
        ),
        out_specs=(VMEM, VMEM, ANY, ANY, ANY, VMEM),
        scratch_shapes=[
            pltpu.VMEM((12, GROUPS, SLAB, D), BF16),
            pltpu.VMEM((4, 8, MEMBERS, SLAB, D), BF16),
            pltpu.VMEM((88, D), BF16),
            pltpu.VMEM((10,) + plane, BF16),
            pltpu.VMEM((2,) + plane, F32),
            pltpu.VMEM(plane, F32),
            pltpu.VMEM(plane, BF16),
            pltpu.VMEM(plane, BF16),
            pltpu.VMEM((2,) + plane, BF16),
            pltpu.VMEM(plane, F32),
            pltpu.VMEM(plane, F32),
            pltpu.SemaphoreType.DMA((96,)),
        ],
        compiler_params=params(),
        cost_estimate=cost(24 * 10**9, 50 * 10**6),
    )(ints, tokens, cotangent, small, up_bias, gathered)


def heads_call(column, ints, grad, gathered, saved):
    plane = (TOKENS, D)
    return pl.pallas_call(
        lambda *refs: heads_kernel(column, *refs),
        name="column_heads" if column else "row_heads",
        in_specs=[SMEM, VMEM, ANY, ANY],
        out_shape=SHAPE((3,) + plane, BF16),
        out_specs=ANY,
        scratch_shapes=[
            pltpu.VMEM((1, GROUPS, SLAB, D), BF16),
            pltpu.VMEM((4,) + plane, BF16),
            pltpu.SemaphoreType.DMA((8,)),
        ],
        compiler_params=params(),
        cost_estimate=cost(10**10, 10**7),
    )(ints, grad, gathered, saved)


PLANE = (TOKENS, D)


def share_of(rows):
    return SHAPE((4, 4, 4, rows, D), BF16)


def column_call(ints, grad, small, gathered, saved, hidden, grads):
    return pl.pallas_call(
        column_kernel,
        name="column_weights",
        in_specs=[SMEM, VMEM, VMEM, ANY, ANY, ANY, ANY],
        out_shape=(SHAPE(PLANE, F32), share_of(SLAB), share_of(SLAB), SHAPE((8, D), F32)),
        out_specs=(VMEM, ANY, ANY, VMEM),
        scratch_shapes=[
            pltpu.VMEM((3, GROUPS, SLAB, D), BF16),
            pltpu.VMEM((3,) + PLANE, BF16),
            pltpu.VMEM(PLANE, BF16),
            pltpu.VMEM(PLANE, BF16),
            pltpu.VMEM(PLANE, BF16),
            pltpu.VMEM(PLANE, F32),
            pltpu.VMEM(PLANE, F32),
            pltpu.VMEM((4, 2, 4, 4, SLAB, D), BF16),
            pltpu.SemaphoreType.DMA((32,)),
        ],
        compiler_params=params(),
        cost_estimate=cost(10**10, 10**7),
    )(ints, grad, small, gathered, saved, hidden, grads)


def row_weights_call(ints, grad, saved, grads):
    return pl.pallas_call(
        row_weights_kernel,
        name="row_weights",
        in_specs=[SMEM, VMEM, ANY, ANY],
        out_shape=(share_of(SLAB), share_of(SLAB)),
        out_specs=(ANY, ANY),
        scratch_shapes=[
            pltpu.VMEM((3,) + PLANE, BF16),
            pltpu.VMEM(PLANE, BF16),
            pltpu.VMEM(PLANE, BF16),
            pltpu.VMEM(PLANE, BF16),
            pltpu.VMEM((4, 2, 4, 4, SLAB, D), BF16),
            pltpu.SemaphoreType.DMA((32,)),
        ],
        compiler_params=params(),
        cost_estimate=cost(10**6, 10**5),
    )(ints, grad, saved, grads)


def row_input_call(ints, grad, small, sums_col, sums_ffn, gathered, hidden, grads):
    return pl.pallas_call(
        row_input_kernel,
        name="row_input",
        in_specs=[SMEM, VMEM, VMEM, VMEM, VMEM, ANY, ANY, ANY],
        out_shape=(SHAPE(PLANE, F32),) + (SHAPE((4, 4, 4, 16, WIDE), BF16),) * 2,
        out_specs=(VMEM, ANY, ANY),
        scratch_shapes=[
            pltpu.VMEM((3, GROUPS, SLAB, D), BF16),
            pltpu.VMEM((3,) + PLANE, BF16),
            pltpu.VMEM(PLANE, F32),
            pltpu.VMEM(PLANE, F32),
            pltpu.VMEM((4, 4, 4, 16, D), BF16),
            pltpu.VMEM((11, 8, D), BF16),
            pltpu.VMEM((ROWS, D), F32),
            pltpu.VMEM((8, D), F32),
            pltpu.VMEM((4, 4, 4, 2, 16, 128), BF16),
            pltpu.SemaphoreType.DMA((48,)),
        ],
        compiler_params=params(),
        cost_estimate=cost(2 * 10**10, 10**7),
    )(ints, grad, small, sums_col, sums_ffn, gathered, hidden, grads)


def sum_of(pieces, *index):
    value = pieces[0][index].astype(F32)
    for piece in pieces[1:]:
        value = value + piece[index].astype(F32)
    return value


def split_kernel(place, *refs):
    for hop in range(4):
        refs[-4 + hop][0] = sum_of(refs[:-4], (place[0] + hop) & 3, 0).astype(BF16)


def split(inputs, place):
    shape = inputs[0].shape
    rest = (0,) * (len(shape) - 2)
    return pl.pallas_call(
        split_kernel,
        name="split_shares",
        grid=(4,),
        in_specs=[SMEM]
        + [pl.BlockSpec((4, 1) + shape[2:], lambda j: (0, j) + rest)] * len(inputs),
        out_shape=(SHAPE(shape[1:], BF16),) * 4,
        out_specs=(pl.BlockSpec((1,) + shape[2:], lambda j: (j,) + rest),) * 4,
        compiler_params=params(),
        cost_estimate=cost(10**6, 10**6),
    )(place, *inputs)


def second_kernel(place, *refs):
    for hop in range(4):
        to = (place[0] + hop) & 3
        for g in range(2):
            value = sum_of(refs[4 * g : 4 * g + 4], to, 0)
            refs[8 + hop][0, g * SLAB : (g + 1) * SLAB, :] = value.astype(BF16)


def second_split(row, col, place):
    return pl.pallas_call(
        second_kernel,
        name="second_split",
        grid=(4,),
        in_specs=[SMEM] + [pl.BlockSpec((4, 1, SLAB, D), lambda j: (0, j, 0, 0))] * 8,
        out_shape=(SHAPE((4, 2 * SLAB, D), BF16),) * 4,
        out_specs=(pl.BlockSpec((1, 2 * SLAB, D), lambda j: (j, 0, 0)),) * 4,
        compiler_params=params(),
        cost_estimate=cost(10**6, 10**6),
    )(place, *row, *col)


def third_kernel(place, ffn, *refs):
    rows, table, pieces = refs[:4], refs[4:8], refs[8:]
    for hop in range(4):
        pieces[hop][...] = sum_of(rows, (place[0] + hop) & 3).astype(BF16)
        to = (place[1] + hop) & 3
        value = sum_of(table, to).astype(BF16)
        pieces[4 + hop][0:16, :] = value[:, 0:D]
        pieces[4 + hop][16:24, :] = jnp.zeros((8, D), BF16)
        pieces[4 + hop][16:24, 0:128] = value[0:8, D:WIDE]
        pieces[4 + hop][SLAB : 3 * SLAB, :] = ffn[to]


def third_split(rows, table, ffn, place):
    return pl.pallas_call(
        third_kernel,
        name="third_split",
        in_specs=[SMEM] + [VMEM] * 9,
        out_shape=(SHAPE((2 * SLAB, D), BF16),) * 4 + (SHAPE((3 * SLAB, D), BF16),) * 4,
        out_specs=(VMEM,) * 8,
        compiler_params=params(),
        cost_estimate=cost(10**6, 10**6),
    )(place, ffn, *rows, *table)


def last_kernel(me, *refs):
    rows, rest, (down, tables, line), pieces, held = refs[:4], refs[4:8], refs[8:11], refs[11:15], refs[15]
    down[...] = sum_of(rest, slice(2 * SLAB, 3 * SLAB))
    for i in range(2):
        tables[i] = sum_of(rest, slice(8 * i, 8 * i + 8))
    line[...] = sum_of(rest, slice(16, 24))
    for kind, (source, start) in enumerate(((rows, 0), (rows, SLAB), (rest, SLAB))):
        value = sum_of(source, slice(start, start + SLAB))
        for member in range(MEMBERS):
            held[member, kind] = value[6 * member : 6 * member + 6, :]
    for flip in range(4):
        pieces[flip][...] = held[me[0] ^ flip].astype(BF16)


def last_split(me, rows, rest):
    return pl.pallas_call(
        last_kernel,
        name="last_split",
        in_specs=[SMEM] + [VMEM] * 8,
        out_shape=(
            SHAPE((SLAB, D), F32),
            SHAPE((2, 8, D), F32),
            SHAPE((8, D), F32),
        )
        + (SHAPE((3, 6, D), BF16),) * 4,
        out_specs=(VMEM,) * 7,
        scratch_shapes=[pltpu.VMEM((MEMBERS, 3, 6, D), F32)],
        compiler_params=params(),
        cost_estimate=cost(10**6, 10**6),
    )(me, *rows, *rest)


def outputs_kernel(me, one, two, three, four, row_qkv, row_out, col_qkv, col_out, up, held):
    for flip, piece in enumerate((one, two, three, four)):
        held[me[0] ^ flip] = piece[...].astype(F32)
    for i in range(3):
        row_qkv[i], col_qkv[i] = held[i, 0], held[i, 1]
    row_out[...], col_out[...] = held[3, 0], held[3, 1]
    for i in range(MEMBERS):
        up[:, i * D : (i + 1) * D] = held[i, 2]


def outputs(me, pieces):
    return pl.pallas_call(
        outputs_kernel,
        name="outputs",
        in_specs=[SMEM] + [VMEM] * 4,
        out_shape=(
            SHAPE((3, 6, D), F32),
            SHAPE((6, D), F32),
            SHAPE((3, 6, D), F32),
            SHAPE((6, D), F32),
            SHAPE((6, FF), F32),
        ),
        out_specs=(VMEM,) * 5,
        scratch_shapes=[pltpu.VMEM((MEMBERS, 3, 6, D), F32)],
        compiler_params=params(),
        cost_estimate=cost(10**6, 10**6),
    )(me, *pieces)


def take(value, index, dim):
    return lax.squeeze(lax.dynamic_slice_in_dim(value, index, 1, dim), (dim,))


def member():
    return (lax.axis_index("x") % 2) * 2 + lax.axis_index("c")


def trade(pieces):
    came = [pieces[0]]
    for flip in range(1, 4):
        pairs = [(i, (i // 4) * 4 + ((i % 4) ^ flip)) for i in range(8)]
        came.append(lax.ppermute(pieces[flip], ("x", "c"), pairs))
    return came


def exchange(blocks):
    me = member()
    parts = trade([take(blocks, me ^ flip, 0) for flip in range(4)])
    odd, high = (me & 1) == 1, (me & 2) == 2
    pairs = [jnp.where(odd, parts[i ^ 1], parts[i]) for i in range(4)]
    return [jnp.where(high, pairs[i ^ 2], pairs[i]) for i in range(4)]


def swap(value):
    return lax.ppermute(value, "c", [(0, 1), (1, 0)])


def scatter_chip_rows(shares):
    return lax.psum_scatter(shares, ("x", "c"), scatter_dimension=0, tiled=False)


STAGES = (("y", "z"), ("z", "y"), ("x", "x"))
TABLE_STAGES = (("x", "x"), ("y", "y"), ("z", "z"))
STRIDES = {"y": 32, "z": 8, "x": 2}


def place_on(axes):
    here = jnp.where(lax.axis_index("c") == 0, lax.axis_index(axes[0]), lax.axis_index(axes[1]))
    return here.astype(jnp.int32)[None]


def deliver(pieces, axes):
    came = [pieces[0]]
    for hop in range(1, 4):
        pairs = []
        for dev in range(DEVICES):
            stride = STRIDES[axes[dev % 2]]
            at = dev // stride % 4
            pairs.append((dev, dev + ((at + hop) % 4 - at) * stride))
        came.append(lax.ppermute(pieces[hop], AXES, pairs))
    return came


def gather(norm_gain, norm_bias, row_qkv, row_out, row_bias, col_qkv, col_out, col_bias,
           ffn_up, up_bias, ffn_down, down_bias, pos_tables):
    row = jnp.concatenate([row_qkv, row_out[None]], axis=0)
    col = jnp.concatenate([col_qkv, col_out[None]], axis=0)
    up = ffn_up.reshape(6, MEMBERS, D).transpose(1, 0, 2)
    slabs = jnp.stack(exchange(jnp.stack([row, col, up], axis=1)), axis=1)
    packed = jnp.concatenate(
        [slabs.reshape(3 * SLAB, D), ffn_down, pos_tables[0], pos_tables[1]], axis=0
    )
    gathered = lax.all_gather(packed, AXES, axis=0, tiled=False)
    sixes = jnp.concatenate([norm_gain, norm_bias, row_bias, col_bias, down_bias[None]], axis=0)
    line = jnp.pad(jnp.concatenate([sixes.reshape(-1), up_bias]), (0, 26))
    lines = lax.all_gather(line, AXES, axis=0, tiled=False).astype(F32)
    small = lines[:, :78].reshape(DEVICES, 13, 6).transpose(1, 0, 2).reshape(13, D)
    small = jnp.pad(small, ((0, 3), (0, 0)))
    return gathered.reshape(GROUPS, MEMBERS, PACK, D), small, lines[:, 78:102].reshape(4, D)


def on_device(tokens, cotangent, lengths, row_offset, col_offset, *weights):
    gathered, small, up_bias = gather(*weights)
    core = lax.axis_index("c").astype(jnp.int32)
    ints = jnp.concatenate([lengths, row_offset, col_offset, core[None]])
    act, g2, saved, hidden, ffn_shares, ffn_sums = forward_call(
        ints, tokens.reshape(TOKENS, D), cotangent.reshape(TOKENS, D), small, up_bias, gathered
    )
    barrier = lax.optimization_barrier
    ffn = scatter_chip_rows(ffn_shares)
    col_heads = heads_call(True, ints, g2, gathered, saved)
    g1, own, other, col_sums = column_call(ints, g2, small, gathered, saved, hidden, col_heads)
    row_heads = heads_call(False, ints, g1, gathered, saved)
    places = [place_on(axes) for axes in STAGES]
    other, row_heads = barrier((swap(other), row_heads))
    pieces, row_heads = barrier((split((own, other), places[0]), row_heads))
    col = deliver(pieces, STAGES[0])
    g0, table_own, table_other = row_input_call(
        ints, g1, small, col_sums, ffn_sums, gathered, hidden, row_heads
    )
    own, other = row_weights_call(ints, g1, saved, row_heads)
    table_other, col = barrier((table_other, col))
    other, table_other, ffn = barrier((other, swap(table_other), ffn))
    ffn = lax.psum_scatter(ffn.reshape(4, 4, 2 * SLAB, D), "y", scatter_dimension=0, tiled=False)
    y_place, z_place = place_on(TABLE_STAGES[1]), place_on(TABLE_STAGES[2])
    table, other = barrier((split((table_own, table_other), places[2]), swap(other)))
    table = deliver(table, TABLE_STAGES[0])
    row = deliver(split((own, other), places[0]), STAGES[0])
    table = deliver(split(table, y_place), TABLE_STAGES[1])
    rows = deliver(second_split(row, col, places[1]), STAGES[1])
    pieces = third_split(rows, table, ffn, jnp.concatenate([places[2], z_place]))
    rows, rest = deliver(pieces[:4], STAGES[2]), deliver(pieces[4:], TABLE_STAGES[2])
    return (act.reshape(tokens.shape), g0.reshape(tokens.shape)) + owned(rows, rest)


def owned(rows, rest):
    me = member().astype(jnp.int32)[None]
    down, tables, line, *pieces = last_split(me, rows, rest)
    row_qkv, row_out, col_qkv, col_out, up = outputs(me, trade(pieces))
    sixes = line[0, :96].reshape(6, 16).T
    row_sums, col_sums, ffn_sums = sixes[0:5], sixes[5:10], sixes[10:13]
    gain = jnp.stack([row_sums[0], col_sums[0], ffn_sums[1]])
    shift_grad = jnp.stack([row_sums[1], col_sums[1], ffn_sums[2]])
    return (
        gain,
        shift_grad,
        row_qkv,
        row_out,
        row_sums[2:5],
        col_qkv,
        col_out,
        col_sums[2:5],
        up,
        line[0, 96:120],
        down,
        ffn_sums[0],
        tables,
    )


def solution(mesh):
    mesh = Mesh(mesh.devices.reshape(4, 4, 4, 2), AXES)
    first, second = P(AXES), P(None, AXES)
    weights = (second, second, second, first, second, second, first, second) + (first,) * 4 + (second,)
    return jax.shard_map(
        on_device,
        mesh=mesh,
        in_specs=(first,) * 5 + weights,
        out_specs=(first, first) + weights,
        check_vma=False,
    )
```

```python
import math

import jax
import jax.numpy as jnp
from jax import lax
from jax.experimental import pallas as pl
from jax.experimental.pallas import tpu as pltpu
from jax.sharding import Mesh, PartitionSpec as P

AXES = ("y", "z", "x", "c")
DEVICES = 128
GROUPS = 32
MEMBERS = 4
D = 768
FF = 3072
HEAD_DIM = 64
POSITIONS = 1024
ROWS = 8
COLS = 64
TOKENS = ROWS * COLS
SLAB = 24
WIDE = D + 128
PACK = 112
PAIRS = 6
EPS = 1e-05
MASKED = -1e30
ROW_SCALE = 1.0 / math.sqrt(HEAD_DIM * ROWS)
COL_SCALE = 1.0 / math.sqrt(HEAD_DIM)
BF16 = jnp.bfloat16
F32 = jnp.float32
GAIN, SHIFT, ROW_BIAS, COL_BIAS, DOWN_BIAS = 0, 3, 6, 9, 12
A1, Q1, K1, V1, M1, A2, Q2, K2, V2, M2 = range(10)


def dot(left, right):
    return jnp.dot(left, right, preferred_element_type=F32)


def dot_nt(left, right):
    return lax.dot_general(left, right, (((1,), (1,)), ((), ())), preferred_element_type=F32)


def dot_tn(left, right):
    return lax.dot_general(left, right, (((0,), (0,)), ((), ())), preferred_element_type=F32)


def chunk(index, size):
    return pl.ds(pl.multiple_of(index * size, size), size)


def loop(count, body, unroll=1):
    def step(index, carry):
        body(index)
        return carry

    lax.fori_loop(0, count, step, 0, unroll=unroll)


def unit_of(hidden):
    centred = hidden - jnp.mean(hidden, axis=-1, keepdims=True)
    inverse = lax.rsqrt(jnp.mean(centred * centred, axis=-1, keepdims=True) + EPS)
    return centred * inverse, inverse


def norm(hidden, small, which):
    unit, _ = unit_of(hidden)
    gain, shift = small[GAIN + which : GAIN + which + 1, :], small[SHIFT + which : SHIFT + which + 1, :]
    return (unit * gain + shift).astype(BF16)


def norm_back(grad, hidden, gain):
    unit, inverse = unit_of(hidden)
    inner = grad * gain
    mean = jnp.mean(inner, axis=-1, keepdims=True)
    cross = jnp.mean(inner * unit, axis=-1, keepdims=True)
    return inverse * (inner - mean - unit * cross), grad * unit


def total(value):
    return jnp.sum(value, axis=0, keepdims=True)


def first_head(shape):
    return (lax.broadcasted_iota(jnp.int32, shape, 1) & 127) < HEAD_DIM


def stack_heads(value):
    keep = jnp.where(first_head(value.shape), 1.0, 0.0)
    return jnp.concatenate([value * keep.astype(BF16), value * (1.0 - keep).astype(BF16)], axis=0)


def merge_heads(value):
    half = value.shape[0] // 2
    return jnp.where(first_head((half, value.shape[1])), value[:half], value[half:])


def softmax(scores):
    top = jnp.max(scores, axis=-1, keepdims=True)
    raised = jnp.exp(scores - top)
    return raised / jnp.sum(raised, axis=-1, keepdims=True)


class RowHeads:
    scale = ROW_SCALE
    steps = 2

    def __init__(self, length):
        self.length = length

    def blocks(self, step):
        return [chunk(3 * step + i, 128) for i in range(3)]

    def load(self, ref, plane, lanes):
        return jnp.concatenate(
            [ref[plane, r * COLS : (r + 1) * COLS, lanes] for r in range(ROWS)], axis=1
        )

    def store(self, ref, plane, lanes, value):
        for r in range(ROWS):
            ref[plane, r * COLS : (r + 1) * COLS, lanes] = value[:, r * 128 : (r + 1) * 128]

    def mask(self):
        shape = (2 * COLS, COLS)
        return lax.broadcasted_iota(jnp.int32, shape, 1) < self.length


class ColHeads:
    scale = COL_SCALE
    steps = PAIRS

    def blocks(self, step):
        return [(i * 16, chunk(step, 128)) for i in range(4)]

    def load(self, ref, plane, block):
        start, lanes = block
        return jnp.concatenate(
            [ref[plane, r * COLS + start : r * COLS + start + 16, lanes] for r in range(ROWS)], axis=0
        )

    def store(self, ref, plane, block, value):
        start, lanes = block
        for r in range(ROWS):
            ref[plane, r * COLS + start : r * COLS + start + 16, lanes] = value[16 * r : 16 * r + 16]

    def mask(self):
        row = lax.broadcasted_iota(jnp.int32, (256, 128), 0) & 15
        return row == (lax.broadcasted_iota(jnp.int32, (256, 128), 1) & 15)


def each(function, *lists):
    return [function(*values) for values in zip(*lists)]


def weights_of(heads, queries, keys):
    mask = heads.mask()
    scores = each(dot_nt, queries, keys)
    return each(lambda s: softmax(jnp.where(mask, s * heads.scale, MASKED)), scores)


def attend(heads, ref, q, k, v, m):
    def body(step):
        blocks = heads.blocks(step)
        queries, keys, values = (
            [heads.load(ref, plane, block) for block in blocks] for plane in (q, k, v)
        )
        probs = weights_of(heads, each(stack_heads, queries), keys)
        mixed = each(lambda p, value: dot(p.astype(BF16), value), probs, values)
        for block, value in zip(blocks, mixed):
            heads.store(ref, m, block, merge_heads(value).astype(BF16))

    loop(heads.steps, body)


def attend_back(heads, ref, q, k, v, dm):
    def body(step):
        blocks = heads.blocks(step)
        queries, keys, values, mixed = (
            [heads.load(ref, plane, block) for block in blocks] for plane in (q, k, v, dm)
        )
        queries, mixed = each(stack_heads, queries), each(stack_heads, mixed)
        probs = weights_of(heads, queries, keys)
        grad = each(dot_nt, mixed, values)
        grad_values = each(lambda p, value: dot_tn(p.astype(BF16), value), probs, mixed)
        inner = each(
            lambda p, g: (p * (g - jnp.sum(g * p, axis=-1, keepdims=True))).astype(BF16), probs, grad
        )
        grad_queries = each(lambda i, key: merge_heads(dot(i, key)) * heads.scale, inner, keys)
        grad_keys = each(lambda i, query: dot_tn(i, query) * heads.scale, inner, queries)
        for i, block in enumerate(blocks):
            heads.store(ref, q, block, grad_queries[i].astype(BF16))
            heads.store(ref, k, block, grad_keys[i].astype(BF16))
            heads.store(ref, v, block, grad_values[i].astype(BF16))

    loop(heads.steps, body)


def whole(ref, index):
    return ref[index].reshape(D, D)


def project(ref, source, planes, weights, first, small, bias_row):
    def body(index):
        rows = chunk(index, 256)
        normed = ref[source, rows, :]
        for i, plane in enumerate(planes):
            value = dot(normed, whole(weights, first + i))
            if i != 1:
                row = bias_row + (0 if i == 0 else 1)
                value = value + small[row : row + 1, :]
            ref[plane, rows, :] = value.astype(BF16)

    loop(2, body)


class Copies:
    def __init__(self, sems):
        self.sems, self.used = sems, 0

    def start(self, source, target):
        copy = pltpu.make_async_copy(source, target, self.sems.at[self.used])
        self.used += 1
        copy.start()
        return copy

    def send(self, core, parity, source, own, other):
        sem = self.sems.at[self.used]
        self.used += 1
        here = pltpu.make_async_copy(source, own, sem)
        there = pltpu.make_async_copy(source, other, sem)
        pl.when(core == parity)(here.start)
        pl.when(core != parity)(there.start)
        return here


def position_rows(window, offset, count):
    shape = (count, window.shape[0])
    pick = lax.broadcasted_iota(jnp.int32, shape, 1) == (
        lax.broadcasted_iota(jnp.int32, shape, 0) + offset % 8
    )
    return dot(jnp.where(pick, 1.0, 0.0).astype(BF16), window)


def forward_kernel(
    ints, tokens, cotangent, small, up_bias, gathered,
    act_out, g2_out, saved_out, hidden_out, shares, sums,
    weights, down, window, act, hidden, h2, a3, gy, wide, y, da, sems,
):
    grads = weights
    length, row_offset, col_offset = ints[0], ints[1], ints[2]
    copies = Copies(sems)
    near = []
    for i in range(2):
        dev = jnp.minimum(row_offset // 8 + i, DEVICES - 1)
        near.append(
            copies.start(gathered.at[dev // 4, dev % 4, 96:104, :], window.at[8 * i : 8 * i + 8, :])
        )
    for i in range(9):
        dev = jnp.minimum(col_offset // 8 + i, DEVICES - 1)
        near.append(
            copies.start(
                gathered.at[dev // 4, dev % 4, 104:112, :], window.at[16 + 8 * i : 24 + 8 * i, :]
            )
        )
    loads = [
        copies.start(gathered.at[:, i % 4, 24 * (i // 4) : 24 * (i // 4) + 24, :], weights.at[i])
        for i in range(12)
    ]
    loads += [
        copies.start(gathered.at[8 * f : 8 * f + 8, :, 72:96, :], down.at[f]) for f in range(4)
    ]
    for copy in near:
        copy.wait()
    row_pos = position_rows(window[0:16, :], row_offset, ROWS)
    col_pos = position_rows(window[16:88, :], col_offset, COLS)
    for r in range(ROWS):
        rows = slice(r * COLS, (r + 1) * COLS)
        value = tokens[rows, :].astype(F32) + row_pos[r : r + 1, :] + col_pos
        hidden[0, rows, :] = value
        act[A1, rows, :] = norm(value, small, 0)
    stores = [copies.start(hidden.at[0], hidden_out.at[0]), copies.start(act.at[A1], saved_out.at[A1])]

    def branch(first, source, planes, heads, bias, target, which, last):
        for i in range(3):
            loads[first + i].wait()
        project(act, source, planes[:3], weights, first, small, bias)
        for plane in planes[:3]:
            stores.append(copies.start(act.at[plane], saved_out.at[plane]))
        attend(heads, act, *planes)
        stores.append(copies.start(act.at[planes[3]], saved_out.at[planes[3]]))
        loads[first + 3].wait()

        def body(index):
            rows = chunk(index, 256)
            branch_out = dot(act[planes[3], rows, :], whole(weights, first + 3))
            before = hidden[which - 1, rows, :]
            after = before + (branch_out + small[bias + 2 : bias + 3, :])
            if last:
                h2[rows, :] = after
                a3[rows, :] = norm(after, small, which)
            else:
                hidden[which, rows, :] = after
                act[target, rows, :] = norm(after, small, which)

        loop(2, body)

    branch(0, A1, (Q1, K1, V1, M1), RowHeads(length), ROW_BIAS, A2, 1, False)
    stores.append(copies.start(hidden.at[1], hidden_out.at[1]))
    stores.append(copies.start(act.at[A2], saved_out.at[A2]))
    branch(4, A2, (Q2, K2, V2, M2), ColHeads(), COL_BIAS, None, 2, True)

    in_use = lax.broadcasted_iota(jnp.int32, (COLS, D), 0) < length
    for r in range(ROWS):
        rows = slice(r * COLS, (r + 1) * COLS)
        gy[rows, :] = jnp.where(in_use, cotangent[rows, :].astype(F32), 0.0).astype(BF16)
    for copy in loads[8:]:
        copy.wait()

    def ffn(f):
        up, low = whole(weights, 8 + f), down[f].reshape(D, D)
        bias = up_bias[pl.ds(f, 1), :]

        def body(index):
            rows = chunk(index, 512)
            z = dot(a3[rows, :], up) + bias
            cdf = 0.5 * (1.0 + lax.erf(z * math.sqrt(0.5)))
            slope = cdf + z * (jnp.exp(-0.5 * z * z) * (1.0 / math.sqrt(2.0 * math.pi)))
            u = (z * cdf).astype(BF16)
            wide[0, rows, :] = u
            du = dot_nt(gy[rows, :], low).astype(BF16).astype(F32)
            dz = (du * slope).astype(BF16)
            wide[1, rows, :] = dz
            more, more_da = dot(u, low), dot_nt(dz, up)

            @pl.when(f == 0)
            def _():
                y[rows, :] = more
                da[rows, :] = more_da

            @pl.when(f != 0)
            def _():
                y[rows, :] += more
                da[rows, :] += more_da

        loop(1, body)
        sums[pl.ds(f, 1), :] = total(wide[1].astype(F32))

        value = dot_tn(wide[0], gy[...]).astype(BF16).reshape(4, 8, SLAB, D)
        for k in range(8):
            grads[4 + f, 4 * k : 4 * k + 4] = value[:, k]
        value = dot_tn(a3[...], wide[1]).astype(BF16).reshape(16, 2, SLAB, D)
        for half in range(2):
            grads[f, 16 * half : 16 * half + 16] = value[:, half]
        for copy in ffn_sends(f):
            copy.start()

    first_sem = copies.used

    def ffn_sends(f):
        sends = []
        for half in range(2):
            place = (4 * half + f, slice(None), slice(0, SLAB))
            sends.append((grads.at[f, 16 * half : 16 * half + 16], shares.at[place]))
        for k in range(8):
            place = (k, pl.ds(4 * f, 4), slice(SLAB, 2 * SLAB))
            sends.append((grads.at[4 + f, 4 * k : 4 * k + 4], shares.at[place]))
        return [
            pltpu.make_async_copy(source, target, sems.at[first_sem + 10 * f + i])
            for i, (source, target) in enumerate(sends)
        ]

    loop(4, ffn)
    gain = small[GAIN + 2 : GAIN + 3, :]

    def finish(index, carry):
        rows = chunk(index, 64)
        late = h2[rows, :]
        act_out[rows, :] = (late + (y[rows, :] + small[DOWN_BIAS : DOWN_BIAS + 1, :])).astype(BF16)
        grad = da[rows, :]
        inner, unit = norm_back(grad, late, gain)
        cot = gy[rows, :].astype(F32)
        g2_out[rows, :] = cot + inner
        return carry[0] + total(unit), carry[1] + total(grad), carry[2] + total(cot)

    zero = jnp.zeros((1, D), F32)
    gain_sum, shift_sum, down_sum = lax.fori_loop(0, 8, finish, (zero, zero, zero))
    sums[4:5, :] = down_sum
    sums[5:6, :] = gain_sum
    sums[6:7, :] = shift_sum
    sums[7:8, :] = zero
    for copy in stores + [copy for f in range(4) for copy in ffn_sends(f)]:
        copy.wait()


def row_heads_kernel(ints, grad_in, gathered, saved, grads_out, weight, act, sems):
    copies = Copies(sems)
    load = copies.start(gathered.at[:, 3, 0:SLAB, :], weight.at[0])
    act_loads = [copies.start(saved.at[plane], act.at[i]) for i, plane in enumerate((Q1, K1, V1))]
    load.wait()

    def mixed_back(index):
        rows = chunk(index, 256)
        act[3, rows, :] = dot_nt(grad_in[rows, :].astype(BF16), whole(weight, 0)).astype(BF16)

    loop(2, mixed_back)
    for copy in act_loads:
        copy.wait()
    attend_back(RowHeads(ints[0]), act, 0, 1, 2, 3)
    stores = [copies.start(act.at[i], grads_out.at[i]) for i in range(3)]
    for copy in stores:
        copy.wait()


class Shares:
    def __init__(self, core, copies, own, other):
        self.core, self.copies, self.own, self.other, self.sent = core, copies, own, other, []

    def send(self, grads, member):
        every, parity = slice(None), member % 2
        for half in range(2):
            x = 2 * half + member // 2
            if parity == 0:
                places = [(grads.at[member, half], (every, every, x))]
            else:
                places = [(grads.at[member, half, y], (every, y, x)) for y in range(4)]
            for source, place in places:
                self.sent.append(
                    self.copies.send(self.core, parity, source, self.own.at[place], self.other.at[place])
                )

    def wait(self):
        for copy in self.sent:
            copy.wait()


def keep(grads, which, value):
    value = value.astype(BF16).reshape(4, 4, 2, SLAB, D)
    for half in range(2):
        grads[which, half] = value[:, :, half]


def weight_grads(loads, act_loads, grad_in, act, out_grad, normed, mixed, grads, shares):
    def low(index):
        rows = chunk(index, 128)
        out_grad[rows, :] = grad_in[rows, :].astype(BF16)

    loop(4, low)
    loads["mixed"].wait()

    keep(grads, 3, dot_tn(mixed[...], out_grad[...]))
    shares.send(grads, 3)
    for copy in [loads["normed"]] + act_loads:
        copy.wait()

    def weight_back(which):
        keep(grads, which, dot_tn(normed[...], act[which]))

    loop(3, weight_back)
    for member in range(3):
        shares.send(grads, member)


def input_grads(loads, grad_in, gain, act, weights, hidden, da, grad_out, sums, lines=None):
    for i in range(3):
        for copy in loads["inputs"][i]:
            copy.wait()

        def input_back(index):
            rows = chunk(index, 256)
            value = dot_nt(act[i, rows, :], whole(weights, i))
            da[rows, :] = value if i == 0 else da[rows, :] + value

        loop(2, input_back)
    loads["hidden"].wait()

    def finish(index, carry):
        rows = chunk(index, 64)
        grad, before = da[rows, :], grad_in[rows, :]
        inner, unit = norm_back(grad, hidden[rows, :], gain)
        value = before + inner
        grad_out[rows, :] = value
        added = [unit, grad, act[0, rows, :], act[2, rows, :], before.astype(BF16)]
        added = [total(extra.astype(F32)) for extra in added]
        if lines is not None:
            lines[pl.ds(index, 1), :] = total(value)
            added.append(value)
        return tuple(a + b for a, b in zip(carry, added))

    carry = (jnp.zeros((1, D), F32),) * 5
    if lines is not None:
        carry = carry + (jnp.zeros((COLS, D), F32),)
    carry = lax.fori_loop(0, 8, finish, carry)
    for i in range(5):
        sums[i : i + 1, :] = carry[i]
    sums[5:8, :] = jnp.zeros((3, D), F32)
    return carry[-1]


def column_kernel(
    ints, grad_in, small, gathered, saved, hidden_saved,
    grad_out, own, other, sums,
    weights, act, out_grad, normed, mixed, hidden, da, grads, sems,
):
    copies = Copies(sems)
    shares = Shares(ints[3], copies, own, other)
    slabs = [gathered.at[:, i, SLAB : 2 * SLAB, :] for i in range(4)]
    out_load = copies.start(slabs[3], weights.at[3])
    act_loads = [copies.start(saved.at[plane], act.at[i]) for i, plane in enumerate((Q2, K2, V2))]
    loads = {"mixed": copies.start(saved.at[M2], mixed), "normed": copies.start(saved.at[A2], normed)}
    loads["inputs"] = [[copies.start(slabs[i], weights.at[i])] for i in range(3)]
    loads["hidden"] = copies.start(hidden_saved.at[1], hidden)
    out_load.wait()

    def mixed_back(index):
        rows = chunk(index, 256)
        act[3, rows, :] = dot_nt(grad_in[rows, :].astype(BF16), whole(weights, 3)).astype(BF16)

    loop(2, mixed_back)
    for copy in act_loads:
        copy.wait()
    attend_back(ColHeads(), act, 0, 1, 2, 3)
    weight_grads(loads, [], grad_in, act, out_grad, normed, mixed, grads, shares)
    input_grads(loads, grad_in, small[GAIN + 1 : GAIN + 2, :], act, weights, hidden, da, grad_out, sums)
    shares.wait()


def row_weights_kernel(
    ints, grad_in, saved, grads_in, own, other, act, out_grad, normed, mixed, grads, sems
):
    copies = Copies(sems)
    shares = Shares(ints[3], copies, own, other)
    loads = {"mixed": copies.start(saved.at[M1], mixed), "normed": copies.start(saved.at[A1], normed)}
    act_loads = [copies.start(grads_in.at[i], act.at[i]) for i in range(3)]
    weight_grads(loads, act_loads, grad_in, act, out_grad, normed, mixed, grads, shares)
    shares.wait()


def small_lines(sums, sums_col, sums_ffn):
    lines = jnp.concatenate([sums[0:5, :], sums_col[0:5, :], sums_ffn[4:7, :], sums[5:8, :]], axis=0)
    shape = (DEVICES, D)
    dev, lane = (lax.broadcasted_iota(jnp.int32, shape, axis) for axis in (0, 1))
    packed = jnp.zeros((DEVICES, 128), F32)
    for j in range(6):
        pick = jnp.where(lane == 6 * dev + j, 1.0, 0.0).astype(BF16)
        blank = [jnp.zeros((16, D), F32)] * 8
        blank[j] = lines
        packed = packed + dot_nt(pick, jnp.concatenate(blank, axis=0).astype(BF16))
    up = jnp.concatenate(
        [jnp.broadcast_to(sums_ffn[f : f + 1, :], (32, D)) for f in range(4)], axis=0
    )
    first = 24 * (dev & 31)
    up = jnp.where((lane >= first) & (lane < first + 24), up, 0.0).astype(BF16)
    shape = (128, D)
    to, lane = (lax.broadcasted_iota(jnp.int32, shape, axis) for axis in (0, 1))
    fold = jnp.where(to - 96 == lane % 24, 1.0, 0.0).astype(BF16)
    return (packed + dot_nt(up, fold)).astype(BF16)


def row_input_kernel(
    ints, grad_in, small, sums_col, sums_ffn, gathered, hidden_saved, grads_in,
    grad_out, own, other,
    weights, act, hidden, da, zeros, table, lines, sums, owned_lines, sems,
):
    copies = Copies(sems)
    loads = {"inputs": []}
    for i in range(3):
        slab = gathered.at[:, i, 0:SLAB, :]
        loads["inputs"].append(
            [copies.start(grads_in.at[i], act.at[i]), copies.start(slab, weights.at[i])]
        )
    loads["hidden"] = copies.start(hidden_saved.at[0], hidden)
    zeros[...] = jnp.zeros_like(zeros)
    fills = [copies.start(zeros, out.at[:, :, :, :, 0:D]) for out in (own, other)]
    gain = small[GAIN : GAIN + 1, :]
    col_lines = input_grads(loads, grad_in, gain, act, weights, hidden, da, grad_out, sums, lines)
    packed = small_lines(sums, sums_col, sums_ffn).astype(F32).reshape(4, 4, 4, 2, 1, 128)
    owned_lines[...] = jnp.broadcast_to(packed, owned_lines.shape).astype(BF16)
    for copy in fills:
        copy.wait()
    sent = []
    for parity in range(2):
        for x in range(4):
            source, place = owned_lines.at[:, :, x, parity], (x, slice(None), slice(None), slice(0, 16), slice(D, WIDE))
            sent.append(copies.send(ints[3], parity, source, own.at[place], other.at[place]))
    send_tables(ints, copies, lines[...], col_lines, table, own, other)
    for copy in sent:
        copy.wait()


def send_tables(ints, copies, row_lines, col_lines, table, own, other):
    core = ints[3]

    def placed(values, offset, count):
        shape = (count, values.shape[0])
        here = lax.broadcasted_iota(jnp.int32, shape, 0) == (
            lax.broadcasted_iota(jnp.int32, shape, 1) + offset % 8
        )
        return dot(jnp.where(here, 1.0, 0.0).astype(BF16), values.astype(BF16)).astype(BF16)

    spots = []
    for first, count, values, offset, start in (
        (0, 2, row_lines, ints[1], 0),
        (2, 9, col_lines, ints[2], 8),
    ):
        table[first : first + count] = placed(values, offset, 8 * count).reshape(count, 8, D)
        spots += [(first + i, offset // 8 + i, start) for i in range(count)]
    waits = []
    for slot, owner, start in spots:
        real, dev = owner < DEVICES, jnp.minimum(owner, DEVICES - 1)
        x, y, z = (dev // 2) % 4, dev // 32, (dev // 8) % 4
        place = (x, y, z, slice(start, start + 8), slice(0, D))
        sem = copies.sems.at[copies.used]
        copies.used += 1
        here = pltpu.make_async_copy(table.at[slot], own.at[place], sem)
        there = pltpu.make_async_copy(table.at[slot], other.at[place], sem)
        pl.when(real & (dev % 2 == core))(here.start)
        pl.when(real & (dev % 2 != core))(there.start)
        waits.append((real, here))
    for real, copy in waits:
        pl.when(real)(copy.wait)


VMEM = pl.BlockSpec(memory_space=pltpu.VMEM)
ANY = pl.BlockSpec(memory_space=pl.ANY)
SMEM = pl.BlockSpec(memory_space=pltpu.SMEM)
SHAPE = jax.ShapeDtypeStruct


def params():
    return pltpu.CompilerParams(vmem_limit_bytes=62 * 1024 * 1024)


def cost(flops, traffic):
    return pl.CostEstimate(flops=flops, transcendentals=0, bytes_accessed=traffic)


def forward_call(ints, tokens, cotangent, small, up_bias, gathered):
    plane = (TOKENS, D)
    return pl.pallas_call(
        forward_kernel,
        name="forward",
        in_specs=[SMEM, VMEM, VMEM, VMEM, VMEM, ANY],
        out_shape=(
            SHAPE(plane, BF16),
            SHAPE(plane, F32),
            SHAPE((10,) + plane, BF16),
            SHAPE((2,) + plane, F32),
            SHAPE((8, 16, 2 * SLAB, D), BF16),
            SHAPE((8, D), F32),
        ),
        out_specs=(VMEM, VMEM, ANY, ANY, ANY, VMEM),
        scratch_shapes=[
            pltpu.VMEM((12, GROUPS, SLAB, D), BF16),
            pltpu.VMEM((4, 8, MEMBERS, SLAB, D), BF16),
            pltpu.VMEM((88, D), BF16),
            pltpu.VMEM((10,) + plane, BF16),
            pltpu.VMEM((2,) + plane, F32),
            pltpu.VMEM(plane, F32),
            pltpu.VMEM(plane, BF16),
            pltpu.VMEM(plane, BF16),
            pltpu.VMEM((2,) + plane, BF16),
            pltpu.VMEM(plane, F32),
            pltpu.VMEM(plane, F32),
            pltpu.SemaphoreType.DMA((96,)),
        ],
        compiler_params=params(),
        cost_estimate=cost(24 * 10**9, 50 * 10**6),
    )(ints, tokens, cotangent, small, up_bias, gathered)


def row_heads_call(ints, grad, gathered, saved):
    plane = (TOKENS, D)
    return pl.pallas_call(
        row_heads_kernel,
        name="row_heads",
        in_specs=[SMEM, VMEM, ANY, ANY],
        out_shape=SHAPE((3,) + plane, BF16),
        out_specs=ANY,
        scratch_shapes=[
            pltpu.VMEM((1, GROUPS, SLAB, D), BF16),
            pltpu.VMEM((4,) + plane, BF16),
            pltpu.SemaphoreType.DMA((8,)),
        ],
        compiler_params=params(),
        cost_estimate=cost(10**10, 10**7),
    )(ints, grad, gathered, saved)


PLANE = (TOKENS, D)


def share_of(rows):
    return SHAPE((4, 4, 4, rows, D), BF16)


def column_call(ints, grad, small, gathered, saved, hidden):
    return pl.pallas_call(
        column_kernel,
        name="column_back",
        in_specs=[SMEM, VMEM, VMEM, ANY, ANY, ANY],
        out_shape=(SHAPE(PLANE, F32), share_of(SLAB), share_of(SLAB), SHAPE((8, D), F32)),
        out_specs=(VMEM, ANY, ANY, VMEM),
        scratch_shapes=[
            pltpu.VMEM((4, GROUPS, SLAB, D), BF16),
            pltpu.VMEM((4,) + PLANE, BF16),
            pltpu.VMEM(PLANE, BF16),
            pltpu.VMEM(PLANE, BF16),
            pltpu.VMEM(PLANE, BF16),
            pltpu.VMEM(PLANE, F32),
            pltpu.VMEM(PLANE, F32),
            pltpu.VMEM((4, 2, 4, 4, SLAB, D), BF16),
            pltpu.SemaphoreType.DMA((48,)),
        ],
        compiler_params=params(),
        cost_estimate=cost(10**10, 10**7),
    )(ints, grad, small, gathered, saved, hidden)


def row_weights_call(ints, grad, saved, grads):
    return pl.pallas_call(
        row_weights_kernel,
        name="row_weights",
        in_specs=[SMEM, VMEM, ANY, ANY],
        out_shape=(share_of(SLAB), share_of(SLAB)),
        out_specs=(ANY, ANY),
        scratch_shapes=[
            pltpu.VMEM((3,) + PLANE, BF16),
            pltpu.VMEM(PLANE, BF16),
            pltpu.VMEM(PLANE, BF16),
            pltpu.VMEM(PLANE, BF16),
            pltpu.VMEM((4, 2, 4, 4, SLAB, D), BF16),
            pltpu.SemaphoreType.DMA((32,)),
        ],
        compiler_params=params(),
        cost_estimate=cost(10**6, 10**5),
    )(ints, grad, saved, grads)


def row_input_call(ints, grad, small, sums_col, sums_ffn, gathered, hidden, grads):
    return pl.pallas_call(
        row_input_kernel,
        name="row_input",
        in_specs=[SMEM, VMEM, VMEM, VMEM, VMEM, ANY, ANY, ANY],
        out_shape=(SHAPE(PLANE, F32),) + (SHAPE((4, 4, 4, 16, WIDE), BF16),) * 2,
        out_specs=(VMEM, ANY, ANY),
        scratch_shapes=[
            pltpu.VMEM((3, GROUPS, SLAB, D), BF16),
            pltpu.VMEM((3,) + PLANE, BF16),
            pltpu.VMEM(PLANE, F32),
            pltpu.VMEM(PLANE, F32),
            pltpu.VMEM((4, 4, 4, 16, D), BF16),
            pltpu.VMEM((11, 8, D), BF16),
            pltpu.VMEM((ROWS, D), F32),
            pltpu.VMEM((8, D), F32),
            pltpu.VMEM((4, 4, 4, 2, 16, 128), BF16),
            pltpu.SemaphoreType.DMA((48,)),
        ],
        compiler_params=params(),
        cost_estimate=cost(2 * 10**10, 10**7),
    )(ints, grad, small, sums_col, sums_ffn, gathered, hidden, grads)


def sum_of(pieces, *index):
    value = pieces[0][index].astype(F32)
    for piece in pieces[1:]:
        value = value + piece[index].astype(F32)
    return value


def split_kernel(place, *refs):
    for hop in range(4):
        refs[-4 + hop][0] = sum_of(refs[:-4], (place[0] + hop) & 3, 0).astype(BF16)


def split(inputs, place):
    shape = inputs[0].shape
    rest = (0,) * (len(shape) - 2)
    return pl.pallas_call(
        split_kernel,
        name="split_shares",
        grid=(4,),
        in_specs=[SMEM]
        + [pl.BlockSpec((4, 1) + shape[2:], lambda j: (0, j) + rest)] * len(inputs),
        out_shape=(SHAPE(shape[1:], BF16),) * 4,
        out_specs=(pl.BlockSpec((1,) + shape[2:], lambda j: (j,) + rest),) * 4,
        compiler_params=params(),
        cost_estimate=cost(10**6, 10**6),
    )(place, *inputs)


def second_kernel(place, *refs):
    for hop in range(4):
        to = (place[0] + hop) & 3
        for g in range(2):
            value = sum_of(refs[4 * g : 4 * g + 4], to, 0)
            refs[8 + hop][0, g * SLAB : (g + 1) * SLAB, :] = value.astype(BF16)


def second_split(row, col, place):
    return pl.pallas_call(
        second_kernel,
        name="second_split",
        grid=(4,),
        in_specs=[SMEM] + [pl.BlockSpec((4, 1, SLAB, D), lambda j: (0, j, 0, 0))] * 8,
        out_shape=(SHAPE((4, 2 * SLAB, D), BF16),) * 4,
        out_specs=(pl.BlockSpec((1, 2 * SLAB, D), lambda j: (j, 0, 0)),) * 4,
        compiler_params=params(),
        cost_estimate=cost(10**6, 10**6),
    )(place, *row, *col)


def third_kernel(place, ffn, *refs):
    rows, table, pieces = refs[:4], refs[4:8], refs[8:]
    for hop in range(4):
        pieces[hop][...] = sum_of(rows, (place[0] + hop) & 3).astype(BF16)
        to = (place[1] + hop) & 3
        value = sum_of(table, to).astype(BF16)
        pieces[4 + hop][0:16, :] = value[:, 0:D]
        pieces[4 + hop][16:24, :] = jnp.zeros((8, D), BF16)
        pieces[4 + hop][16:24, 0:128] = value[0:8, D:WIDE]
        pieces[4 + hop][SLAB : 3 * SLAB, :] = ffn[to]


def third_split(rows, table, ffn, place):
    return pl.pallas_call(
        third_kernel,
        name="third_split",
        in_specs=[SMEM] + [VMEM] * 9,
        out_shape=(SHAPE((2 * SLAB, D), BF16),) * 4 + (SHAPE((3 * SLAB, D), BF16),) * 4,
        out_specs=(VMEM,) * 8,
        compiler_params=params(),
        cost_estimate=cost(10**6, 10**6),
    )(place, ffn, *rows, *table)


def last_kernel(me, *refs):
    rows, rest, (down, tables), small, pieces, held = refs[:4], refs[4:8], refs[8:10], refs[10:16], refs[16:20], refs[20]
    down[...] = sum_of(rest, slice(2 * SLAB, 3 * SLAB))
    for i in range(2):
        tables[i] = sum_of(rest, slice(8 * i, 8 * i + 8))
    line = sum_of(rest, slice(16, 24), slice(0, 128))[0:1]
    gain, shift, row_bias, col_bias, up_bias, down_bias = small
    up_bias[...] = line[:, 96:120]
    lines = jnp.broadcast_to(line, (16, 128))
    value, lane = (lax.broadcasted_iota(jnp.int32, lines.shape, axis) for axis in (0, 1))
    for j in range(6):
        column = jnp.sum(jnp.where(lane == 16 * j + value, lines, 0.0), axis=1, keepdims=True)
        at = slice(j, j + 1)
        for i, first in enumerate((0, 5, 11)):
            gain[i : i + 1, at] = column[first : first + 1]
            shift[i : i + 1, at] = column[first + 1 : first + 2]
        row_bias[:, at], col_bias[:, at] = column[2:5], column[7:10]
        down_bias[:, at] = column[10:11]
    for kind, (source, start) in enumerate(((rows, 0), (rows, SLAB), (rest, SLAB))):
        value = sum_of(source, slice(start, start + SLAB))
        for member in range(MEMBERS):
            held[member, kind] = value[6 * member : 6 * member + 6, :]
    for flip in range(4):
        pieces[flip][...] = held[me[0] ^ flip].astype(BF16)


def last_split(me, rows, rest):
    return pl.pallas_call(
        last_kernel,
        name="last_split",
        in_specs=[SMEM] + [VMEM] * 8,
        out_shape=(
            SHAPE((SLAB, D), F32),
            SHAPE((2, 8, D), F32),
        )
        + (SHAPE((3, 6), F32),) * 4
        + (SHAPE((1, SLAB), F32), SHAPE((1, 6), F32))
        + (SHAPE((3, 6, D), BF16),) * 4,
        out_specs=(VMEM,) * 12,
        scratch_shapes=[pltpu.VMEM((MEMBERS, 3, 6, D), F32)],
        compiler_params=params(),
        cost_estimate=cost(10**6, 10**6),
    )(me, *rows, *rest)


def outputs_kernel(me, one, two, three, four, row_qkv, row_out, col_qkv, col_out, up, held):
    for flip, piece in enumerate((one, two, three, four)):
        held[me[0] ^ flip] = piece[...].astype(F32)
    for i in range(3):
        row_qkv[i], col_qkv[i] = held[i, 0], held[i, 1]
    row_out[...], col_out[...] = held[3, 0], held[3, 1]
    for i in range(MEMBERS):
        up[:, i * D : (i + 1) * D] = held[i, 2]


def outputs(me, pieces):
    return pl.pallas_call(
        outputs_kernel,
        name="outputs",
        in_specs=[SMEM] + [VMEM] * 4,
        out_shape=(
            SHAPE((3, 6, D), F32),
            SHAPE((6, D), F32),
            SHAPE((3, 6, D), F32),
            SHAPE((6, D), F32),
            SHAPE((6, FF), F32),
        ),
        out_specs=(VMEM,) * 5,
        scratch_shapes=[pltpu.VMEM((MEMBERS, 3, 6, D), F32)],
        compiler_params=params(),
        cost_estimate=cost(10**6, 10**6),
    )(me, *pieces)


def take(value, index, dim):
    return lax.squeeze(lax.dynamic_slice_in_dim(value, index, 1, dim), (dim,))


def member():
    return (lax.axis_index("x") % 2) * 2 + lax.axis_index("c")


def trade(pieces):
    came = [pieces[0]]
    for flip in range(1, 4):
        pairs = [(i, (i // 4) * 4 + ((i % 4) ^ flip)) for i in range(8)]
        came.append(lax.ppermute(pieces[flip], ("x", "c"), pairs))
    return came


def exchange(blocks):
    me = member()
    parts = trade([take(blocks, me ^ flip, 0) for flip in range(4)])
    odd, high = (me & 1) == 1, (me & 2) == 2
    pairs = [jnp.where(odd, parts[i ^ 1], parts[i]) for i in range(4)]
    return [jnp.where(high, pairs[i ^ 2], pairs[i]) for i in range(4)]


def swap(value):
    return lax.ppermute(value, "c", [(0, 1), (1, 0)])


def scatter_chip_rows(shares):
    return lax.psum_scatter(shares, ("x", "c"), scatter_dimension=0, tiled=False)


STAGES = (("y", "z"), ("z", "y"), ("x", "x"))
TABLE_STAGES = (("x", "x"), ("y", "y"), ("z", "z"))
STRIDES = {"y": 32, "z": 8, "x": 2}


def place_on(axes):
    here = jnp.where(lax.axis_index("c") == 0, lax.axis_index(axes[0]), lax.axis_index(axes[1]))
    return here.astype(jnp.int32)[None]


def deliver(pieces, axes):
    came = [pieces[0]]
    for hop in range(1, 4):
        pairs = []
        for dev in range(DEVICES):
            stride = STRIDES[axes[dev % 2]]
            at = dev // stride % 4
            pairs.append((dev, dev + ((at + hop) % 4 - at) * stride))
        came.append(lax.ppermute(pieces[hop], AXES, pairs))
    return came


def gather(norm_gain, norm_bias, row_qkv, row_out, row_bias, col_qkv, col_out, col_bias,
           ffn_up, up_bias, ffn_down, down_bias, pos_tables):
    row = jnp.concatenate([row_qkv, row_out[None]], axis=0)
    col = jnp.concatenate([col_qkv, col_out[None]], axis=0)
    up = ffn_up.reshape(6, MEMBERS, D).transpose(1, 0, 2)
    slabs = jnp.stack(exchange(jnp.stack([row, col, up], axis=1)), axis=1)
    packed = jnp.concatenate(
        [slabs.reshape(3 * SLAB, D), ffn_down, pos_tables[0], pos_tables[1]], axis=0
    )
    gathered = lax.all_gather(packed, AXES, axis=0, tiled=False)
    sixes = jnp.concatenate([norm_gain, norm_bias, row_bias, col_bias, down_bias[None]], axis=0)
    line = jnp.pad(jnp.concatenate([sixes.reshape(-1), up_bias]), (0, 26))
    lines = lax.all_gather(line, AXES, axis=0, tiled=False).astype(F32)
    small = lines[:, :78].reshape(DEVICES, 13, 6).transpose(1, 0, 2).reshape(13, D)
    small = jnp.pad(small, ((0, 3), (0, 0)))
    return gathered.reshape(GROUPS, MEMBERS, PACK, D), small, lines[:, 78:102].reshape(4, D)


def on_device(tokens, cotangent, lengths, row_offset, col_offset, *weights):
    gathered, small, up_bias = gather(*weights)
    core = lax.axis_index("c").astype(jnp.int32)
    ints = jnp.concatenate([lengths, row_offset, col_offset, core[None]])
    act, g2, saved, hidden, ffn_shares, ffn_sums = forward_call(
        ints, tokens.reshape(TOKENS, D), cotangent.reshape(TOKENS, D), small, up_bias, gathered
    )
    barrier = lax.optimization_barrier
    ffn = scatter_chip_rows(ffn_shares)
    g1, own, other, col_sums = column_call(ints, g2, small, gathered, saved, hidden)
    row_heads = row_heads_call(ints, g1, gathered, saved)
    places = [place_on(axes) for axes in STAGES]
    other, row_heads = barrier((swap(other), row_heads))
    pieces, row_heads = barrier((split((own, other), places[0]), row_heads))
    col = deliver(pieces, STAGES[0])
    g0, table_own, table_other = row_input_call(
        ints, g1, small, col_sums, ffn_sums, gathered, hidden, row_heads
    )
    own, other = row_weights_call(ints, g1, saved, row_heads)
    table_other, col, ffn = barrier((table_other, col, ffn))
    other, table_other = barrier((other, swap(table_other)))
    ffn = lax.psum_scatter(ffn.reshape(4, 4, 2 * SLAB, D), "y", scatter_dimension=0, tiled=False)
    y_place, z_place = place_on(TABLE_STAGES[1]), place_on(TABLE_STAGES[2])
    table, other = barrier((split((table_own, table_other), places[2]), swap(other)))
    table = deliver(table, TABLE_STAGES[0])
    row = deliver(split((own, other), places[0]), STAGES[0])
    table = deliver(split(table, y_place), TABLE_STAGES[1])
    rows = deliver(second_split(row, col, places[1]), STAGES[1])
    pieces = third_split(rows, table, ffn, jnp.concatenate([places[2], z_place]))
    rows, rest = deliver(pieces[:4], STAGES[2]), deliver(pieces[4:], TABLE_STAGES[2])
    return (act.reshape(tokens.shape), g0.reshape(tokens.shape)) + owned(rows, rest)


def owned(rows, rest):
    me = member().astype(jnp.int32)[None]
    down, tables, gain, shift, row_bias, col_bias, up_bias, down_bias, *pieces = last_split(me, rows, rest)
    row_qkv, row_out, col_qkv, col_out, up = outputs(me, trade(pieces))
    return (
        gain,
        shift,
        row_qkv,
        row_out,
        row_bias,
        col_qkv,
        col_out,
        col_bias,
        up,
        up_bias[0],
        down,
        down_bias[0],
        tables,
    )


def solution(mesh):
    mesh = Mesh(mesh.devices.reshape(4, 4, 4, 2), AXES)
    first, second = P(AXES), P(None, AXES)
    weights = (second, second, second, first, second, second, first, second) + (first,) * 4 + (second,)
    return jax.shard_map(
        on_device,
        mesh=mesh,
        in_specs=(first,) * 5 + weights,
        out_specs=(first, first) + weights,
        check_vma=False,
    )
```

```python
import math

import jax
import jax.numpy as jnp
from jax import lax
from jax.experimental import pallas as pl
from jax.experimental.pallas import tpu as pltpu
from jax.sharding import Mesh, PartitionSpec as P

AXES = ("y", "z", "x", "c")
DEVICES = 128
GROUPS = 32
MEMBERS = 4
D = 768
FF = 3072
HEAD_DIM = 64
POSITIONS = 1024
ROWS = 8
COLS = 64
TOKENS = ROWS * COLS
SLAB = 24
WIDE = D + 128
PACK = 112
PAIRS = 6
EPS = 1e-05
MASKED = -1e30
ROW_SCALE = 1.0 / math.sqrt(HEAD_DIM * ROWS)
COL_SCALE = 1.0 / math.sqrt(HEAD_DIM)
BF16 = jnp.bfloat16
F32 = jnp.float32
GAIN, SHIFT, ROW_BIAS, COL_BIAS, DOWN_BIAS = 0, 3, 6, 9, 12
A1, Q1, K1, V1, M1, A2, Q2, K2, V2, M2 = range(10)


def dot(left, right):
    return jnp.dot(left, right, preferred_element_type=F32)


def dot_nt(left, right):
    return lax.dot_general(left, right, (((1,), (1,)), ((), ())), preferred_element_type=F32)


def dot_tn(left, right):
    return lax.dot_general(left, right, (((0,), (0,)), ((), ())), preferred_element_type=F32)


def chunk(index, size):
    return pl.ds(pl.multiple_of(index * size, size), size)


def loop(count, body, unroll=1):
    def step(index, carry):
        body(index)
        return carry

    lax.fori_loop(0, count, step, 0, unroll=unroll)


def unit_of(hidden):
    centred = hidden - jnp.mean(hidden, axis=-1, keepdims=True)
    inverse = lax.rsqrt(jnp.mean(centred * centred, axis=-1, keepdims=True) + EPS)
    return centred * inverse, inverse


def norm(hidden, small, which):
    unit, _ = unit_of(hidden)
    gain, shift = small[GAIN + which : GAIN + which + 1, :], small[SHIFT + which : SHIFT + which + 1, :]
    return (unit * gain + shift).astype(BF16)


def norm_back(grad, hidden, gain):
    unit, inverse = unit_of(hidden)
    inner = grad * gain
    mean = jnp.mean(inner, axis=-1, keepdims=True)
    cross = jnp.mean(inner * unit, axis=-1, keepdims=True)
    return inverse * (inner - mean - unit * cross), grad * unit


def total(value):
    return jnp.sum(value, axis=0, keepdims=True)


def first_head(shape):
    return (lax.broadcasted_iota(jnp.int32, shape, 1) & 127) < HEAD_DIM


def stack_heads(value):
    keep = jnp.where(first_head(value.shape), 1.0, 0.0)
    return jnp.concatenate([value * keep.astype(BF16), value * (1.0 - keep).astype(BF16)], axis=0)


def merge_heads(value):
    half = value.shape[0] // 2
    return jnp.where(first_head((half, value.shape[1])), value[:half], value[half:])


def softmax(scores):
    top = jnp.max(scores, axis=-1, keepdims=True)
    raised = jnp.exp(scores - top)
    return raised / jnp.sum(raised, axis=-1, keepdims=True)


class RowHeads:
    scale = ROW_SCALE
    steps = 2

    def __init__(self, length):
        self.length = length

    def blocks(self, step):
        return [chunk(3 * step + i, 128) for i in range(3)]

    def load(self, ref, plane, lanes):
        return jnp.concatenate(
            [ref[plane, r * COLS : (r + 1) * COLS, lanes] for r in range(ROWS)], axis=1
        )

    def store(self, ref, plane, lanes, value):
        for r in range(ROWS):
            ref[plane, r * COLS : (r + 1) * COLS, lanes] = value[:, r * 128 : (r + 1) * 128]

    def mask(self):
        shape = (2 * COLS, COLS)
        return lax.broadcasted_iota(jnp.int32, shape, 1) < self.length


class ColHeads:
    scale = COL_SCALE
    steps = PAIRS

    def blocks(self, step):
        return [(i * 16, chunk(step, 128)) for i in range(4)]

    def load(self, ref, plane, block):
        start, lanes = block
        return jnp.concatenate(
            [ref[plane, r * COLS + start : r * COLS + start + 16, lanes] for r in range(ROWS)], axis=0
        )

    def store(self, ref, plane, block, value):
        start, lanes = block
        for r in range(ROWS):
            ref[plane, r * COLS + start : r * COLS + start + 16, lanes] = value[16 * r : 16 * r + 16]

    def mask(self):
        row = lax.broadcasted_iota(jnp.int32, (256, 128), 0) & 15
        return row == (lax.broadcasted_iota(jnp.int32, (256, 128), 1) & 15)


def each(function, *lists):
    return [function(*values) for values in zip(*lists)]


def weights_of(heads, queries, keys):
    mask = heads.mask()
    scores = each(dot_nt, queries, keys)
    return each(lambda s: softmax(jnp.where(mask, s * heads.scale, MASKED)), scores)


def attend(heads, ref, q, k, v, m):
    def body(step):
        blocks = heads.blocks(step)
        queries, keys, values = (
            [heads.load(ref, plane, block) for block in blocks] for plane in (q, k, v)
        )
        probs = weights_of(heads, each(stack_heads, queries), keys)
        mixed = each(lambda p, value: dot(p.astype(BF16), value), probs, values)
        for block, value in zip(blocks, mixed):
            heads.store(ref, m, block, merge_heads(value).astype(BF16))

    loop(heads.steps, body)


def attend_back(heads, ref, q, k, v, dm):
    def body(step):
        blocks = heads.blocks(step)
        queries, keys, values, mixed = (
            [heads.load(ref, plane, block) for block in blocks] for plane in (q, k, v, dm)
        )
        queries, mixed = each(stack_heads, queries), each(stack_heads, mixed)
        probs = weights_of(heads, queries, keys)
        grad = each(dot_nt, mixed, values)
        grad_values = each(lambda p, value: dot_tn(p.astype(BF16), value), probs, mixed)
        inner = each(
            lambda p, g: (p * (g - jnp.sum(g * p, axis=-1, keepdims=True))).astype(BF16), probs, grad
        )
        grad_queries = each(lambda i, key: merge_heads(dot(i, key)) * heads.scale, inner, keys)
        grad_keys = each(lambda i, query: dot_tn(i, query) * heads.scale, inner, queries)
        for i, block in enumerate(blocks):
            heads.store(ref, q, block, grad_queries[i].astype(BF16))
            heads.store(ref, k, block, grad_keys[i].astype(BF16))
            heads.store(ref, v, block, grad_values[i].astype(BF16))

    loop(heads.steps, body)


def whole(ref, index):
    return ref[index].reshape(D, D)


def project(ref, source, planes, weights, first, small, bias_row):
    def body(index):
        rows = chunk(index, 256)
        normed = ref[source, rows, :]
        for i, plane in enumerate(planes):
            value = dot(normed, whole(weights, first + i))
            if i != 1:
                row = bias_row + (0 if i == 0 else 1)
                value = value + small[row : row + 1, :]
            ref[plane, rows, :] = value.astype(BF16)

    loop(2, body)


class Copies:
    def __init__(self, sems):
        self.sems, self.used = sems, 0

    def start(self, source, target):
        copy = pltpu.make_async_copy(source, target, self.sems.at[self.used])
        self.used += 1
        copy.start()
        return copy

    def send(self, core, parity, source, own, other):
        sem = self.sems.at[self.used]
        self.used += 1
        here = pltpu.make_async_copy(source, own, sem)
        there = pltpu.make_async_copy(source, other, sem)
        pl.when(core == parity)(here.start)
        pl.when(core != parity)(there.start)
        return here


def position_rows(window, offset, count):
    shape = (count, window.shape[0])
    pick = lax.broadcasted_iota(jnp.int32, shape, 1) == (
        lax.broadcasted_iota(jnp.int32, shape, 0) + offset % 8
    )
    return dot(jnp.where(pick, 1.0, 0.0).astype(BF16), window)


def forward_kernel(
    ints, tokens, cotangent, small, up_bias, gathered,
    act_out, g2_out, saved_out, hidden_out, shares, sums,
    weights, down, window, act, hidden, h2, a3, gy, wide, y, da, sems,
):
    grads = weights
    length, row_offset, col_offset = ints[0], ints[1], ints[2]
    copies = Copies(sems)
    near = []
    for i in range(2):
        dev = jnp.minimum(row_offset // 8 + i, DEVICES - 1)
        near.append(
            copies.start(gathered.at[dev // 4, dev % 4, 96:104, :], window.at[8 * i : 8 * i + 8, :])
        )
    for i in range(9):
        dev = jnp.minimum(col_offset // 8 + i, DEVICES - 1)
        near.append(
            copies.start(
                gathered.at[dev // 4, dev % 4, 104:112, :], window.at[16 + 8 * i : 24 + 8 * i, :]
            )
        )
    loads = [
        copies.start(gathered.at[:, i % 4, 24 * (i // 4) : 24 * (i // 4) + 24, :], weights.at[i])
        for i in range(12)
    ]
    loads += [
        copies.start(gathered.at[8 * f : 8 * f + 8, :, 72:96, :], down.at[f]) for f in range(4)
    ]
    for copy in near:
        copy.wait()
    row_pos = position_rows(window[0:16, :], row_offset, ROWS)
    col_pos = position_rows(window[16:88, :], col_offset, COLS)
    for r in range(ROWS):
        rows = slice(r * COLS, (r + 1) * COLS)
        value = tokens[rows, :].astype(F32) + row_pos[r : r + 1, :] + col_pos
        hidden[0, rows, :] = value
        act[A1, rows, :] = norm(value, small, 0)
    stores = [copies.start(hidden.at[0], hidden_out.at[0]), copies.start(act.at[A1], saved_out.at[A1])]

    def branch(first, source, planes, heads, bias, target, which, last):
        for i in range(3):
            loads[first + i].wait()
        project(act, source, planes[:3], weights, first, small, bias)
        for plane in planes[:3]:
            stores.append(copies.start(act.at[plane], saved_out.at[plane]))
        attend(heads, act, *planes)
        stores.append(copies.start(act.at[planes[3]], saved_out.at[planes[3]]))
        loads[first + 3].wait()

        def body(index):
            rows = chunk(index, 256)
            branch_out = dot(act[planes[3], rows, :], whole(weights, first + 3))
            before = hidden[which - 1, rows, :]
            after = before + (branch_out + small[bias + 2 : bias + 3, :])
            if last:
                h2[rows, :] = after
                a3[rows, :] = norm(after, small, which)
            else:
                hidden[which, rows, :] = after
                act[target, rows, :] = norm(after, small, which)

        loop(2, body)

    branch(0, A1, (Q1, K1, V1, M1), RowHeads(length), ROW_BIAS, A2, 1, False)
    stores.append(copies.start(hidden.at[1], hidden_out.at[1]))
    stores.append(copies.start(act.at[A2], saved_out.at[A2]))
    branch(4, A2, (Q2, K2, V2, M2), ColHeads(), COL_BIAS, None, 2, True)

    in_use = lax.broadcasted_iota(jnp.int32, (COLS, D), 0) < length
    for r in range(ROWS):
        rows = slice(r * COLS, (r + 1) * COLS)
        gy[rows, :] = jnp.where(in_use, cotangent[rows, :].astype(F32), 0.0).astype(BF16)
    for copy in loads[8:]:
        copy.wait()

    def ffn(f):
        up, low = whole(weights, 8 + f), down[f].reshape(D, D)
        bias = up_bias[pl.ds(f, 1), :]

        def body(index):
            rows = chunk(index, 512)
            z = dot(a3[rows, :], up) + bias
            cdf = 0.5 * (1.0 + lax.erf(z * math.sqrt(0.5)))
            slope = cdf + z * (jnp.exp(-0.5 * z * z) * (1.0 / math.sqrt(2.0 * math.pi)))
            u = (z * cdf).astype(BF16)
            wide[0, rows, :] = u
            du = dot_nt(gy[rows, :], low).astype(BF16).astype(F32)
            dz = (du * slope).astype(BF16)
            wide[1, rows, :] = dz
            more, more_da = dot(u, low), dot_nt(dz, up)

            @pl.when(f == 0)
            def _():
                y[rows, :] = more
                da[rows, :] = more_da

            @pl.when(f != 0)
            def _():
                y[rows, :] += more
                da[rows, :] += more_da

        loop(1, body)
        sums[pl.ds(f, 1), :] = total(wide[1].astype(F32))

        value = dot_tn(wide[0], gy[...]).astype(BF16).reshape(4, 8, SLAB, D)
        for k in range(8):
            grads[4 + f, 4 * k : 4 * k + 4] = value[:, k]
        value = dot_tn(a3[...], wide[1]).astype(BF16).reshape(16, 2, SLAB, D)
        for half in range(2):
            grads[f, 16 * half : 16 * half + 16] = value[:, half]
        for copy in ffn_sends(f):
            copy.start()

    first_sem = copies.used

    def ffn_sends(f):
        sends = []
        for half in range(2):
            place = (4 * half + f, slice(None), slice(0, SLAB))
            sends.append((grads.at[f, 16 * half : 16 * half + 16], shares.at[place]))
        for k in range(8):
            place = (k, pl.ds(4 * f, 4), slice(SLAB, 2 * SLAB))
            sends.append((grads.at[4 + f, 4 * k : 4 * k + 4], shares.at[place]))
        return [
            pltpu.make_async_copy(source, target, sems.at[first_sem + 10 * f + i])
            for i, (source, target) in enumerate(sends)
        ]

    loop(4, ffn)
    gain = small[GAIN + 2 : GAIN + 3, :]

    def finish(index, carry):
        rows = chunk(index, 64)
        late = h2[rows, :]
        act_out[rows, :] = (late + (y[rows, :] + small[DOWN_BIAS : DOWN_BIAS + 1, :])).astype(BF16)
        grad = da[rows, :]
        inner, unit = norm_back(grad, late, gain)
        cot = gy[rows, :].astype(F32)
        g2_out[rows, :] = cot + inner
        return carry[0] + total(unit), carry[1] + total(grad), carry[2] + total(cot)

    zero = jnp.zeros((1, D), F32)
    gain_sum, shift_sum, down_sum = lax.fori_loop(0, 8, finish, (zero, zero, zero))
    sums[4:5, :] = down_sum
    sums[5:6, :] = gain_sum
    sums[6:7, :] = shift_sum
    sums[7:8, :] = zero
    for copy in stores + [copy for f in range(4) for copy in ffn_sends(f)]:
        copy.wait()


def row_heads_kernel(ints, grad_in, gathered, saved, grads_out, weight, act, sems):
    copies = Copies(sems)
    load = copies.start(gathered.at[:, 3, 0:SLAB, :], weight.at[0])
    act_loads = [copies.start(saved.at[plane], act.at[i]) for i, plane in enumerate((Q1, K1, V1))]
    load.wait()

    def mixed_back(index):
        rows = chunk(index, 256)
        act[3, rows, :] = dot_nt(grad_in[rows, :].astype(BF16), whole(weight, 0)).astype(BF16)

    loop(2, mixed_back)
    for copy in act_loads:
        copy.wait()
    attend_back(RowHeads(ints[0]), act, 0, 1, 2, 3)
    stores = [copies.start(act.at[i], grads_out.at[i]) for i in range(3)]
    for copy in stores:
        copy.wait()


class Shares:
    def __init__(self, core, copies, own, other):
        self.core, self.copies, self.own, self.other, self.sent = core, copies, own, other, []

    def send(self, grads, member):
        every, parity = slice(None), member % 2
        for half in range(2):
            x = 2 * half + member // 2
            if parity == 0:
                places = [(grads.at[member, half], (every, every, x))]
            else:
                places = [(grads.at[member, half, y], (every, y, x)) for y in range(4)]
            for source, place in places:
                self.sent.append(
                    self.copies.send(self.core, parity, source, self.own.at[place], self.other.at[place])
                )

    def wait(self):
        for copy in self.sent:
            copy.wait()


def keep(grads, which, value):
    value = value.astype(BF16).reshape(4, 4, 2, SLAB, D)
    for half in range(2):
        grads[which, half] = value[:, :, half]


def weight_grads(loads, act_loads, grad_in, act, out_grad, normed, mixed, grads, shares):
    def low(index):
        rows = chunk(index, 128)
        out_grad[rows, :] = grad_in[rows, :].astype(BF16)

    loop(4, low)
    loads["mixed"].wait()

    keep(grads, 3, dot_tn(mixed[...], out_grad[...]))
    shares.send(grads, 3)
    for copy in [loads["normed"]] + act_loads:
        copy.wait()

    def weight_back(which):
        keep(grads, which, dot_tn(normed[...], act[which]))

    loop(3, weight_back)
    for member in range(3):
        shares.send(grads, member)


def input_grads(loads, grad_in, gain, act, weights, hidden, da, grad_out, sums, lines=None, loaded=None):
    for i in range(3):
        for copy in loads["inputs"][i]:
            copy.wait()

        def input_back(index):
            rows = chunk(index, 256)
            value = dot_nt(act[i, rows, :], whole(weights, i))
            da[rows, :] = value if i == 0 else da[rows, :] + value

        if i == 2 and loaded is not None:
            loaded()
        loop(2, input_back)
    loads["hidden"].wait()

    def finish(index, carry):
        rows = chunk(index, 64)
        grad, before = da[rows, :], grad_in[rows, :]
        inner, unit = norm_back(grad, hidden[rows, :], gain)
        value = before + inner
        grad_out[rows, :] = value
        added = [unit, grad, act[0, rows, :], act[2, rows, :], before.astype(BF16)]
        added = [total(extra.astype(F32)) for extra in added]
        if lines is not None:
            lines[pl.ds(index, 1), :] = total(value)
            added.append(value)
        return tuple(a + b for a, b in zip(carry, added))

    carry = (jnp.zeros((1, D), F32),) * 5
    if lines is not None:
        carry = carry + (jnp.zeros((COLS, D), F32),)
    carry = lax.fori_loop(0, 8, finish, carry)
    for i in range(5):
        sums[i : i + 1, :] = carry[i]
    sums[5:8, :] = jnp.zeros((3, D), F32)
    return carry[-1]


def column_kernel(
    ints, grad_in, small, gathered, saved, hidden_saved,
    grad_out, own, other, sums,
    weights, act, out_grad, normed, mixed, hidden, da, grads, sems,
):
    copies = Copies(sems)
    shares = Shares(ints[3], copies, own, other)
    slabs = [gathered.at[:, i, SLAB : 2 * SLAB, :] for i in range(4)]
    out_load = copies.start(slabs[3], weights.at[3])
    act_loads = [copies.start(saved.at[plane], act.at[i]) for i, plane in enumerate((Q2, K2, V2))]
    loads = {"mixed": copies.start(saved.at[M2], mixed), "normed": copies.start(saved.at[A2], normed)}
    loads["inputs"] = [[copies.start(slabs[i], weights.at[i])] for i in range(3)]
    loads["hidden"] = copies.start(hidden_saved.at[1], hidden)
    out_load.wait()

    def mixed_back(index):
        rows = chunk(index, 256)
        act[3, rows, :] = dot_nt(grad_in[rows, :].astype(BF16), whole(weights, 3)).astype(BF16)

    loop(2, mixed_back)
    for copy in act_loads:
        copy.wait()
    attend_back(ColHeads(), act, 0, 1, 2, 3)
    weight_grads(loads, [], grad_in, act, out_grad, normed, mixed, grads, shares)
    input_grads(loads, grad_in, small[GAIN + 1 : GAIN + 2, :], act, weights, hidden, da, grad_out, sums)
    shares.wait()


def row_weights_kernel(
    ints, grad_in, saved, grads_in, own, other, act, out_grad, normed, mixed, grads, sems
):
    copies = Copies(sems)
    shares = Shares(ints[3], copies, own, other)
    loads = {"mixed": copies.start(saved.at[M1], mixed), "normed": copies.start(saved.at[A1], normed)}
    act_loads = [copies.start(grads_in.at[i], act.at[i]) for i in range(3)]
    weight_grads(loads, act_loads, grad_in, act, out_grad, normed, mixed, grads, shares)
    shares.wait()


def small_lines(sums, sums_col, sums_ffn):
    lines = jnp.concatenate([sums[0:5, :], sums_col[0:5, :], sums_ffn[4:7, :], sums[5:8, :]], axis=0)
    shape = (DEVICES, D)
    dev, lane = (lax.broadcasted_iota(jnp.int32, shape, axis) for axis in (0, 1))
    packed = jnp.zeros((DEVICES, 128), F32)
    for j in range(6):
        pick = jnp.where(lane == 6 * dev + j, 1.0, 0.0).astype(BF16)
        blank = [jnp.zeros((16, D), F32)] * 8
        blank[j] = lines
        packed = packed + dot_nt(pick, jnp.concatenate(blank, axis=0).astype(BF16))
    up = jnp.concatenate(
        [jnp.broadcast_to(sums_ffn[f : f + 1, :], (32, D)) for f in range(4)], axis=0
    )
    first = 24 * (dev & 31)
    up = jnp.where((lane >= first) & (lane < first + 24), up, 0.0).astype(BF16)
    shape = (128, D)
    to, lane = (lax.broadcasted_iota(jnp.int32, shape, axis) for axis in (0, 1))
    fold = jnp.where(to - 96 == lane % 24, 1.0, 0.0).astype(BF16)
    return (packed + dot_nt(up, fold)).astype(BF16)


def row_input_kernel(
    ints, grad_in, small, sums_col, sums_ffn, gathered, hidden_saved, grads_in,
    grad_out, own, other,
    weights, act, hidden, da, zeros, table, lines, sums, owned_lines, sems,
):
    copies = Copies(sems)
    loads = {"inputs": []}
    for i in range(3):
        slab = gathered.at[:, i, 0:SLAB, :]
        loads["inputs"].append(
            [copies.start(grads_in.at[i], act.at[i]), copies.start(slab, weights.at[i])]
        )
    loads["hidden"] = copies.start(hidden_saved.at[0], hidden)
    zeros[...] = jnp.zeros_like(zeros)
    fills = []

    def fill():
        fills.extend(copies.start(zeros, out.at[:, :, :, :, 0:D]) for out in (own, other))

    gain = small[GAIN : GAIN + 1, :]
    col_lines = input_grads(
        loads, grad_in, gain, act, weights, hidden, da, grad_out, sums, lines, fill
    )
    packed = small_lines(sums, sums_col, sums_ffn).astype(F32).reshape(4, 4, 4, 2, 1, 128)
    owned_lines[...] = jnp.broadcast_to(packed, owned_lines.shape).astype(BF16)
    for copy in fills:
        copy.wait()
    sent = []
    for parity in range(2):
        for x in range(4):
            source, place = owned_lines.at[:, :, x, parity], (x, slice(None), slice(None), slice(0, 16), slice(D, WIDE))
            sent.append(copies.send(ints[3], parity, source, own.at[place], other.at[place]))
    send_tables(ints, copies, lines[...], col_lines, table, own, other)
    for copy in sent:
        copy.wait()


def send_tables(ints, copies, row_lines, col_lines, table, own, other):
    core = ints[3]

    def placed(values, offset, count):
        shape = (count, values.shape[0])
        here = lax.broadcasted_iota(jnp.int32, shape, 0) == (
            lax.broadcasted_iota(jnp.int32, shape, 1) + offset % 8
        )
        return dot(jnp.where(here, 1.0, 0.0).astype(BF16), values.astype(BF16)).astype(BF16)

    spots = []
    for first, count, values, offset, start in (
        (0, 2, row_lines, ints[1], 0),
        (2, 9, col_lines, ints[2], 8),
    ):
        table[first : first + count] = placed(values, offset, 8 * count).reshape(count, 8, D)
        spots += [(first + i, offset // 8 + i, start) for i in range(count)]
    waits = []
    for slot, owner, start in spots:
        real, dev = owner < DEVICES, jnp.minimum(owner, DEVICES - 1)
        x, y, z = (dev // 2) % 4, dev // 32, (dev // 8) % 4
        place = (x, y, z, slice(start, start + 8), slice(0, D))
        sem = copies.sems.at[copies.used]
        copies.used += 1
        here = pltpu.make_async_copy(table.at[slot], own.at[place], sem)
        there = pltpu.make_async_copy(table.at[slot], other.at[place], sem)
        pl.when(real & (dev % 2 == core))(here.start)
        pl.when(real & (dev % 2 != core))(there.start)
        waits.append((real, here))
    for real, copy in waits:
        pl.when(real)(copy.wait)


VMEM = pl.BlockSpec(memory_space=pltpu.VMEM)
ANY = pl.BlockSpec(memory_space=pl.ANY)
SMEM = pl.BlockSpec(memory_space=pltpu.SMEM)
SHAPE = jax.ShapeDtypeStruct


def params():
    return pltpu.CompilerParams(vmem_limit_bytes=62 * 1024 * 1024)


def cost(flops, traffic):
    return pl.CostEstimate(flops=flops, transcendentals=0, bytes_accessed=traffic)


def forward_call(ints, tokens, cotangent, small, up_bias, gathered):
    plane = (TOKENS, D)
    return pl.pallas_call(
        forward_kernel,
        name="forward",
        in_specs=[SMEM, VMEM, VMEM, VMEM, VMEM, ANY],
        out_shape=(
            SHAPE(plane, BF16),
            SHAPE(plane, F32),
            SHAPE((10,) + plane, BF16),
            SHAPE((2,) + plane, F32),
            SHAPE((8, 16, 2 * SLAB, D), BF16),
            SHAPE((8, D), F32),
        ),
        out_specs=(VMEM, VMEM, ANY, ANY, ANY, VMEM),
        scratch_shapes=[
            pltpu.VMEM((12, GROUPS, SLAB, D), BF16),
            pltpu.VMEM((4, 8, MEMBERS, SLAB, D), BF16),
            pltpu.VMEM((88, D), BF16),
            pltpu.VMEM((10,) + plane, BF16),
            pltpu.VMEM((2,) + plane, F32),
            pltpu.VMEM(plane, F32),
            pltpu.VMEM(plane, BF16),
            pltpu.VMEM(plane, BF16),
            pltpu.VMEM((2,) + plane, BF16),
            pltpu.VMEM(plane, F32),
            pltpu.VMEM(plane, F32),
            pltpu.SemaphoreType.DMA((96,)),
        ],
        compiler_params=params(),
        cost_estimate=cost(24 * 10**9, 50 * 10**6),
    )(ints, tokens, cotangent, small, up_bias, gathered)


def row_heads_call(ints, grad, gathered, saved):
    plane = (TOKENS, D)
    return pl.pallas_call(
        row_heads_kernel,
        name="row_heads",
        in_specs=[SMEM, VMEM, ANY, ANY],
        out_shape=SHAPE((3,) + plane, BF16),
        out_specs=ANY,
        scratch_shapes=[
            pltpu.VMEM((1, GROUPS, SLAB, D), BF16),
            pltpu.VMEM((4,) + plane, BF16),
            pltpu.SemaphoreType.DMA((8,)),
        ],
        compiler_params=params(),
        cost_estimate=cost(10**10, 10**7),
    )(ints, grad, gathered, saved)


PLANE = (TOKENS, D)


def share_of(rows):
    return SHAPE((4, 4, 4, rows, D), BF16)


def column_call(ints, grad, small, gathered, saved, hidden):
    return pl.pallas_call(
        column_kernel,
        name="column_back",
        in_specs=[SMEM, VMEM, VMEM, ANY, ANY, ANY],
        out_shape=(SHAPE(PLANE, F32), share_of(SLAB), share_of(SLAB), SHAPE((8, D), F32)),
        out_specs=(VMEM, ANY, ANY, VMEM),
        scratch_shapes=[
            pltpu.VMEM((4, GROUPS, SLAB, D), BF16),
            pltpu.VMEM((4,) + PLANE, BF16),
            pltpu.VMEM(PLANE, BF16),
            pltpu.VMEM(PLANE, BF16),
            pltpu.VMEM(PLANE, BF16),
            pltpu.VMEM(PLANE, F32),
            pltpu.VMEM(PLANE, F32),
            pltpu.VMEM((4, 2, 4, 4, SLAB, D), BF16),
            pltpu.SemaphoreType.DMA((48,)),
        ],
        compiler_params=params(),
        cost_estimate=cost(10**10, 10**7),
    )(ints, grad, small, gathered, saved, hidden)


def row_weights_call(ints, grad, saved, grads):
    return pl.pallas_call(
        row_weights_kernel,
        name="row_weights",
        in_specs=[SMEM, VMEM, ANY, ANY],
        out_shape=(share_of(SLAB), share_of(SLAB)),
        out_specs=(ANY, ANY),
        scratch_shapes=[
            pltpu.VMEM((3,) + PLANE, BF16),
            pltpu.VMEM(PLANE, BF16),
            pltpu.VMEM(PLANE, BF16),
            pltpu.VMEM(PLANE, BF16),
            pltpu.VMEM((4, 2, 4, 4, SLAB, D), BF16),
            pltpu.SemaphoreType.DMA((32,)),
        ],
        compiler_params=params(),
        cost_estimate=cost(10**6, 10**5),
    )(ints, grad, saved, grads)


def row_input_call(ints, grad, small, sums_col, sums_ffn, gathered, hidden, grads):
    return pl.pallas_call(
        row_input_kernel,
        name="row_input",
        in_specs=[SMEM, VMEM, VMEM, VMEM, VMEM, ANY, ANY, ANY],
        out_shape=(SHAPE(PLANE, F32),) + (SHAPE((4, 4, 4, 16, WIDE), BF16),) * 2,
        out_specs=(VMEM, ANY, ANY),
        scratch_shapes=[
            pltpu.VMEM((3, GROUPS, SLAB, D), BF16),
            pltpu.VMEM((3,) + PLANE, BF16),
            pltpu.VMEM(PLANE, F32),
            pltpu.VMEM(PLANE, F32),
            pltpu.VMEM((4, 4, 4, 16, D), BF16),
            pltpu.VMEM((11, 8, D), BF16),
            pltpu.VMEM((ROWS, D), F32),
            pltpu.VMEM((8, D), F32),
            pltpu.VMEM((4, 4, 4, 2, 16, 128), BF16),
            pltpu.SemaphoreType.DMA((48,)),
        ],
        compiler_params=params(),
        cost_estimate=cost(2 * 10**10, 10**7),
    )(ints, grad, small, sums_col, sums_ffn, gathered, hidden, grads)


def sum_of(pieces, *index):
    value = pieces[0][index].astype(F32)
    for piece in pieces[1:]:
        value = value + piece[index].astype(F32)
    return value


def split_kernel(place, *refs):
    for hop in range(4):
        refs[-4 + hop][0] = sum_of(refs[:-4], (place[0] + hop) & 3, 0).astype(BF16)


def split(inputs, place):
    shape = inputs[0].shape
    rest = (0,) * (len(shape) - 2)
    return pl.pallas_call(
        split_kernel,
        name="split_shares",
        grid=(4,),
        in_specs=[SMEM]
        + [pl.BlockSpec((4, 1) + shape[2:], lambda j: (0, j) + rest)] * len(inputs),
        out_shape=(SHAPE(shape[1:], BF16),) * 4,
        out_specs=(pl.BlockSpec((1,) + shape[2:], lambda j: (j,) + rest),) * 4,
        compiler_params=params(),
        cost_estimate=cost(10**6, 10**6),
    )(place, *inputs)


def second_kernel(place, *refs):
    for hop in range(4):
        to = (place[0] + hop) & 3
        for g in range(2):
            value = sum_of(refs[4 * g : 4 * g + 4], to, 0)
            refs[8 + hop][0, g * SLAB : (g + 1) * SLAB, :] = value.astype(BF16)


def second_split(row, col, place):
    return pl.pallas_call(
        second_kernel,
        name="second_split",
        grid=(4,),
        in_specs=[SMEM] + [pl.BlockSpec((4, 1, SLAB, D), lambda j: (0, j, 0, 0))] * 8,
        out_shape=(SHAPE((4, 2 * SLAB, D), BF16),) * 4,
        out_specs=(pl.BlockSpec((1, 2 * SLAB, D), lambda j: (j, 0, 0)),) * 4,
        compiler_params=params(),
        cost_estimate=cost(10**6, 10**6),
    )(place, *row, *col)


def third_kernel(place, table_place, ffn, *refs):
    rows, table, pieces = refs[:4], refs[4:8], refs[8:]
    for hop in range(4):
        pieces[hop][...] = sum_of(rows, (place[0] + hop) & 3).astype(BF16)
        to = (table_place[0] + hop) & 3
        value = sum_of(table, to).astype(BF16)
        pieces[4 + hop][0:16, :] = value[:, 0:D]
        pieces[4 + hop][16:24, :] = jnp.zeros((8, D), BF16)
        pieces[4 + hop][16:24, 0:128] = value[0:8, D:WIDE]
        pieces[4 + hop][SLAB : 3 * SLAB, :] = ffn[to]


def third_split(rows, table, ffn, place, table_place):
    return pl.pallas_call(
        third_kernel,
        name="third_split",
        in_specs=[SMEM] * 2 + [VMEM] * 9,
        out_shape=(SHAPE((2 * SLAB, D), BF16),) * 4 + (SHAPE((3 * SLAB, D), BF16),) * 4,
        out_specs=(VMEM,) * 8,
        compiler_params=params(),
        cost_estimate=cost(10**6, 10**6),
    )(place, table_place, ffn, *rows, *table)


def last_kernel(me, *refs):
    rows, rest, (down, tables), small, pieces, held = refs[:4], refs[4:8], refs[8:10], refs[10:16], refs[16:20], refs[20]
    down[...] = sum_of(rest, slice(2 * SLAB, 3 * SLAB))
    for i in range(2):
        tables[i] = sum_of(rest, slice(8 * i, 8 * i + 8))
    line = sum_of(rest, slice(16, 24), slice(0, 128))[0:1]
    gain, shift, row_bias, col_bias, up_bias, down_bias = small
    up_bias[...] = line[:, 96:120]
    lines = jnp.broadcast_to(line, (16, 128))
    value, lane = (lax.broadcasted_iota(jnp.int32, lines.shape, axis) for axis in (0, 1))
    for j in range(6):
        column = jnp.sum(jnp.where(lane == 16 * j + value, lines, 0.0), axis=1, keepdims=True)
        at = slice(j, j + 1)
        for i, first in enumerate((0, 5, 11)):
            gain[i : i + 1, at] = column[first : first + 1]
            shift[i : i + 1, at] = column[first + 1 : first + 2]
        row_bias[:, at], col_bias[:, at] = column[2:5], column[7:10]
        down_bias[:, at] = column[10:11]
    for kind, (source, start) in enumerate(((rows, 0), (rows, SLAB), (rest, SLAB))):
        value = sum_of(source, slice(start, start + SLAB))
        for member in range(MEMBERS):
            held[member, kind] = value[6 * member : 6 * member + 6, :]
    for flip in range(4):
        pieces[flip][...] = held[me[0] ^ flip].astype(BF16)


def last_split(me, rows, rest):
    return pl.pallas_call(
        last_kernel,
        name="last_split",
        in_specs=[SMEM] + [VMEM] * 8,
        out_shape=(
            SHAPE((SLAB, D), F32),
            SHAPE((2, 8, D), F32),
        )
        + (SHAPE((3, 6), F32),) * 4
        + (SHAPE((1, SLAB), F32), SHAPE((1, 6), F32))
        + (SHAPE((3, 6, D), BF16),) * 4,
        out_specs=(VMEM,) * 12,
        scratch_shapes=[pltpu.VMEM((MEMBERS, 3, 6, D), F32)],
        compiler_params=params(),
        cost_estimate=cost(10**6, 10**6),
    )(me, *rows, *rest)


def outputs_kernel(me, one, two, three, four, row_qkv, row_out, col_qkv, col_out, up, held):
    for flip, piece in enumerate((one, two, three, four)):
        held[me[0] ^ flip] = piece[...].astype(F32)
    for i in range(3):
        row_qkv[i], col_qkv[i] = held[i, 0], held[i, 1]
    row_out[...], col_out[...] = held[3, 0], held[3, 1]
    for i in range(MEMBERS):
        up[:, i * D : (i + 1) * D] = held[i, 2]


def outputs(me, pieces):
    return pl.pallas_call(
        outputs_kernel,
        name="outputs",
        in_specs=[SMEM] + [VMEM] * 4,
        out_shape=(
            SHAPE((3, 6, D), F32),
            SHAPE((6, D), F32),
            SHAPE((3, 6, D), F32),
            SHAPE((6, D), F32),
            SHAPE((6, FF), F32),
        ),
        out_specs=(VMEM,) * 5,
        scratch_shapes=[pltpu.VMEM((MEMBERS, 3, 6, D), F32)],
        compiler_params=params(),
        cost_estimate=cost(10**6, 10**6),
    )(me, *pieces)


def take(value, index, dim):
    return lax.squeeze(lax.dynamic_slice_in_dim(value, index, 1, dim), (dim,))


def member():
    return (lax.axis_index("x") % 2) * 2 + lax.axis_index("c")


def trade(pieces):
    came = [pieces[0]]
    for flip in range(1, 4):
        pairs = [(i, (i // 4) * 4 + ((i % 4) ^ flip)) for i in range(8)]
        came.append(lax.ppermute(pieces[flip], ("x", "c"), pairs))
    return came


def exchange(blocks):
    me = member()
    parts = trade([take(blocks, me ^ flip, 0) for flip in range(4)])
    odd, high = (me & 1) == 1, (me & 2) == 2
    pairs = [jnp.where(odd, parts[i ^ 1], parts[i]) for i in range(4)]
    return [jnp.where(high, pairs[i ^ 2], pairs[i]) for i in range(4)]


def swap(value):
    return lax.ppermute(value, "c", [(0, 1), (1, 0)])


def scatter_chip_rows(shares):
    return lax.psum_scatter(shares, ("x", "c"), scatter_dimension=0, tiled=False)


STAGES = (("y", "z"), ("z", "y"), ("x", "x"))
TABLE_STAGES = (("x", "x"), ("y", "y"), ("z", "z"))
STRIDES = {"y": 32, "z": 8, "x": 2}


def place_on(axes):
    here = jnp.where(lax.axis_index("c") == 0, lax.axis_index(axes[0]), lax.axis_index(axes[1]))
    return here.astype(jnp.int32)[None]


def deliver(pieces, axes):
    came = [pieces[0]]
    for hop in range(1, 4):
        pairs = []
        for dev in range(DEVICES):
            stride = STRIDES[axes[dev % 2]]
            at = dev // stride % 4
            pairs.append((dev, dev + ((at + hop) % 4 - at) * stride))
        came.append(lax.ppermute(pieces[hop], AXES, pairs))
    return came


def gather(norm_gain, norm_bias, row_qkv, row_out, row_bias, col_qkv, col_out, col_bias,
           ffn_up, up_bias, ffn_down, down_bias, pos_tables):
    row = jnp.concatenate([row_qkv, row_out[None]], axis=0)
    col = jnp.concatenate([col_qkv, col_out[None]], axis=0)
    up = ffn_up.reshape(6, MEMBERS, D).transpose(1, 0, 2)
    slabs = jnp.stack(exchange(jnp.stack([row, col, up], axis=1)), axis=1)
    packed = jnp.concatenate(
        [slabs.reshape(3 * SLAB, D), ffn_down, pos_tables[0], pos_tables[1]], axis=0
    )
    gathered = lax.all_gather(packed, AXES, axis=0, tiled=False)
    sixes = jnp.concatenate([norm_gain, norm_bias, row_bias, col_bias, down_bias[None]], axis=0)
    line = jnp.pad(jnp.concatenate([sixes.reshape(-1), up_bias]), (0, 26))
    lines = lax.all_gather(line, AXES, axis=0, tiled=False).astype(F32)
    small = lines[:, :78].reshape(DEVICES, 13, 6).transpose(1, 0, 2).reshape(13, D)
    small = jnp.pad(small, ((0, 3), (0, 0)))
    return gathered.reshape(GROUPS, MEMBERS, PACK, D), small, lines[:, 78:102].reshape(4, D)


def on_device(tokens, cotangent, lengths, row_offset, col_offset, *weights):
    gathered, small, up_bias = gather(*weights)
    core = lax.axis_index("c").astype(jnp.int32)
    ints = jnp.concatenate([lengths, row_offset, col_offset, core[None]])
    act, g2, saved, hidden, ffn_shares, ffn_sums = forward_call(
        ints, tokens.reshape(TOKENS, D), cotangent.reshape(TOKENS, D), small, up_bias, gathered
    )
    barrier = lax.optimization_barrier
    ffn = scatter_chip_rows(ffn_shares)
    g1, own, other, col_sums = column_call(ints, g2, small, gathered, saved, hidden)
    row_heads = row_heads_call(ints, g1, gathered, saved)
    places = [place_on(axes) for axes in STAGES]
    other, row_heads = barrier((swap(other), row_heads))
    pieces, row_heads = barrier((split((own, other), places[0]), row_heads))
    col = deliver(pieces, STAGES[0])
    g0, table_own, table_other = row_input_call(
        ints, g1, small, col_sums, ffn_sums, gathered, hidden, row_heads
    )
    own, other = row_weights_call(ints, g1, saved, row_heads)
    table_other, col = barrier((table_other, col))
    other, table_other, ffn = barrier((other, swap(table_other), ffn))
    ffn = lax.psum_scatter(ffn.reshape(4, 4, 2 * SLAB, D), "y", scatter_dimension=0, tiled=False)
    y_place, z_place = place_on(TABLE_STAGES[1]), place_on(TABLE_STAGES[2])
    table, other = barrier((split((table_own, table_other), places[2]), swap(other)))
    table = deliver(table, TABLE_STAGES[0])
    row = deliver(split((own, other), places[0]), STAGES[0])
    table = deliver(split(table, y_place), TABLE_STAGES[1])
    rows = deliver(second_split(row, col, places[1]), STAGES[1])
    pieces = third_split(rows, table, ffn, places[2], z_place)
    rows, rest = deliver(pieces[:4], STAGES[2]), deliver(pieces[4:], TABLE_STAGES[2])
    return (act.reshape(tokens.shape), g0.reshape(tokens.shape)) + owned(rows, rest)


def owned(rows, rest):
    me = member().astype(jnp.int32)[None]
    down, tables, gain, shift, row_bias, col_bias, up_bias, down_bias, *pieces = last_split(me, rows, rest)
    row_qkv, row_out, col_qkv, col_out, up = outputs(me, trade(pieces))
    return (
        gain,
        shift,
        row_qkv,
        row_out,
        row_bias,
        col_qkv,
        col_out,
        col_bias,
        up,
        up_bias[0],
        down,
        down_bias[0],
        tables,
    )


def solution(mesh):
    mesh = Mesh(mesh.devices.reshape(4, 4, 4, 2), AXES)
    first, second = P(AXES), P(None, AXES)
    weights = (second, second, second, first, second, second, first, second) + (first,) * 4 + (second,)
    return jax.shard_map(
        on_device,
        mesh=mesh,
        in_specs=(first,) * 5 + weights,
        out_specs=(first, first) + weights,
        check_vma=False,
    )
```

```python
import math

import jax
import jax.numpy as jnp
from jax import lax
from jax.experimental import pallas as pl
from jax.experimental.pallas import tpu as pltpu
from jax.sharding import Mesh, PartitionSpec as P

AXES = ("y", "z", "x", "c")
DEVICES = 128
GROUPS = 32
MEMBERS = 4
D = 768
FF = 3072
HEAD_DIM = 64
POSITIONS = 1024
ROWS = 8
COLS = 64
TOKENS = ROWS * COLS
SLAB = 24
WIDE = D + 128
PACK = 112
PAIRS = 6
EPS = 1e-05
MASKED = -1e30
ROW_SCALE = 1.0 / math.sqrt(HEAD_DIM * ROWS)
COL_SCALE = 1.0 / math.sqrt(HEAD_DIM)
BF16 = jnp.bfloat16
F32 = jnp.float32
GAIN, SHIFT, ROW_BIAS, COL_BIAS, DOWN_BIAS = 0, 3, 6, 9, 12
A1, Q1, K1, V1, M1, A2, Q2, K2, V2, M2 = range(10)


def dot(left, right):
    return jnp.dot(left, right, preferred_element_type=F32)


def dot_nt(left, right):
    return lax.dot_general(left, right, (((1,), (1,)), ((), ())), preferred_element_type=F32)


def dot_tn(left, right):
    return lax.dot_general(left, right, (((0,), (0,)), ((), ())), preferred_element_type=F32)


def chunk(index, size):
    return pl.ds(pl.multiple_of(index * size, size), size)


def loop(count, body, unroll=1):
    def step(index, carry):
        body(index)
        return carry

    lax.fori_loop(0, count, step, 0, unroll=unroll)


def unit_of(hidden):
    centred = hidden - jnp.mean(hidden, axis=-1, keepdims=True)
    inverse = lax.rsqrt(jnp.mean(centred * centred, axis=-1, keepdims=True) + EPS)
    return centred * inverse, inverse


def norm(hidden, small, which):
    unit, _ = unit_of(hidden)
    gain, shift = small[GAIN + which : GAIN + which + 1, :], small[SHIFT + which : SHIFT + which + 1, :]
    return (unit * gain + shift).astype(BF16)


def norm_back(grad, hidden, gain):
    unit, inverse = unit_of(hidden)
    inner = grad * gain
    mean = jnp.mean(inner, axis=-1, keepdims=True)
    cross = jnp.mean(inner * unit, axis=-1, keepdims=True)
    return inverse * (inner - mean - unit * cross), grad * unit


def total(value):
    return jnp.sum(value, axis=0, keepdims=True)


def first_head(shape):
    return (lax.broadcasted_iota(jnp.int32, shape, 1) & 127) < HEAD_DIM


def stack_heads(value):
    keep = jnp.where(first_head(value.shape), 1.0, 0.0)
    return jnp.concatenate([value * keep.astype(BF16), value * (1.0 - keep).astype(BF16)], axis=0)


def merge_heads(value):
    half = value.shape[0] // 2
    return jnp.where(first_head((half, value.shape[1])), value[:half], value[half:])


def softmax(scores):
    top = jnp.max(scores, axis=-1, keepdims=True)
    raised = jnp.exp(scores - top)
    return raised / jnp.sum(raised, axis=-1, keepdims=True)


class RowHeads:
    scale = ROW_SCALE
    steps = 2

    def __init__(self, length):
        self.length = length

    def blocks(self, step):
        return [chunk(3 * step + i, 128) for i in range(3)]

    def load(self, ref, plane, lanes):
        return jnp.concatenate(
            [ref[plane, r * COLS : (r + 1) * COLS, lanes] for r in range(ROWS)], axis=1
        )

    def store(self, ref, plane, lanes, value):
        for r in range(ROWS):
            ref[plane, r * COLS : (r + 1) * COLS, lanes] = value[:, r * 128 : (r + 1) * 128]

    def mask(self):
        shape = (2 * COLS, COLS)
        return lax.broadcasted_iota(jnp.int32, shape, 1) < self.length


class ColHeads:
    scale = COL_SCALE
    steps = PAIRS

    def blocks(self, step):
        return [(i * 16, chunk(step, 128)) for i in range(4)]

    def load(self, ref, plane, block):
        start, lanes = block
        return jnp.concatenate(
            [ref[plane, r * COLS + start : r * COLS + start + 16, lanes] for r in range(ROWS)], axis=0
        )

    def store(self, ref, plane, block, value):
        start, lanes = block
        for r in range(ROWS):
            ref[plane, r * COLS + start : r * COLS + start + 16, lanes] = value[16 * r : 16 * r + 16]

    def mask(self):
        row = lax.broadcasted_iota(jnp.int32, (256, 128), 0) & 15
        return row == (lax.broadcasted_iota(jnp.int32, (256, 128), 1) & 15)


def each(function, *lists):
    return [function(*values) for values in zip(*lists)]


def weights_of(heads, queries, keys):
    mask = heads.mask()
    scores = each(dot_nt, queries, keys)
    return each(lambda s: softmax(jnp.where(mask, s * heads.scale, MASKED)), scores)


def attend(heads, ref, q, k, v, m):
    def body(step):
        blocks = heads.blocks(step)
        queries, keys, values = (
            [heads.load(ref, plane, block) for block in blocks] for plane in (q, k, v)
        )
        probs = weights_of(heads, each(stack_heads, queries), keys)
        mixed = each(lambda p, value: dot(p.astype(BF16), value), probs, values)
        for block, value in zip(blocks, mixed):
            heads.store(ref, m, block, merge_heads(value).astype(BF16))

    loop(heads.steps, body)


def attend_back(heads, ref, q, k, v, dm):
    def body(step):
        blocks = heads.blocks(step)
        queries, keys, values, mixed = (
            [heads.load(ref, plane, block) for block in blocks] for plane in (q, k, v, dm)
        )
        queries, mixed = each(stack_heads, queries), each(stack_heads, mixed)
        probs = weights_of(heads, queries, keys)
        grad = each(dot_nt, mixed, values)
        grad_values = each(lambda p, value: dot_tn(p.astype(BF16), value), probs, mixed)
        inner = each(
            lambda p, g: (p * (g - jnp.sum(g * p, axis=-1, keepdims=True))).astype(BF16), probs, grad
        )
        grad_queries = each(lambda i, key: merge_heads(dot(i, key)) * heads.scale, inner, keys)
        grad_keys = each(lambda i, query: dot_tn(i, query) * heads.scale, inner, queries)
        for i, block in enumerate(blocks):
            heads.store(ref, q, block, grad_queries[i].astype(BF16))
            heads.store(ref, k, block, grad_keys[i].astype(BF16))
            heads.store(ref, v, block, grad_values[i].astype(BF16))

    loop(heads.steps, body)


def whole(ref, index):
    return ref[index].reshape(D, D)


def project(ref, source, planes, weights, first, small, bias_row):
    def body(index):
        rows = chunk(index, 256)
        normed = ref[source, rows, :]
        for i, plane in enumerate(planes):
            value = dot(normed, whole(weights, first + i))
            if i != 1:
                row = bias_row + (0 if i == 0 else 1)
                value = value + small[row : row + 1, :]
            ref[plane, rows, :] = value.astype(BF16)

    loop(2, body)


class Copies:
    def __init__(self, sems):
        self.sems, self.used = sems, 0

    def start(self, source, target):
        copy = pltpu.make_async_copy(source, target, self.sems.at[self.used])
        self.used += 1
        copy.start()
        return copy

    def send(self, core, parity, source, own, other):
        sem = self.sems.at[self.used]
        self.used += 1
        here = pltpu.make_async_copy(source, own, sem)
        there = pltpu.make_async_copy(source, other, sem)
        pl.when(core == parity)(here.start)
        pl.when(core != parity)(there.start)
        return here


def position_rows(window, offset, count):
    shape = (count, window.shape[0])
    pick = lax.broadcasted_iota(jnp.int32, shape, 1) == (
        lax.broadcasted_iota(jnp.int32, shape, 0) + offset % 8
    )
    return dot(jnp.where(pick, 1.0, 0.0).astype(BF16), window)


def forward_kernel(
    ints, tokens, cotangent, small, up_bias, gathered,
    act_out, g2_out, saved_out, hidden_out, shares, sums,
    weights, down, window, act, hidden, h2, a3, gy, wide, y, da, sems,
):
    grads = weights
    length, row_offset, col_offset = ints[0], ints[1], ints[2]
    copies = Copies(sems)
    near = []
    for i in range(2):
        dev = jnp.minimum(row_offset // 8 + i, DEVICES - 1)
        near.append(
            copies.start(gathered.at[dev // 4, dev % 4, 96:104, :], window.at[8 * i : 8 * i + 8, :])
        )
    for i in range(9):
        dev = jnp.minimum(col_offset // 8 + i, DEVICES - 1)
        near.append(
            copies.start(
                gathered.at[dev // 4, dev % 4, 104:112, :], window.at[16 + 8 * i : 24 + 8 * i, :]
            )
        )
    loads = [
        copies.start(gathered.at[:, i % 4, 24 * (i // 4) : 24 * (i // 4) + 24, :], weights.at[i])
        for i in range(12)
    ]
    loads += [
        copies.start(gathered.at[8 * f : 8 * f + 8, :, 72:96, :], down.at[f]) for f in range(4)
    ]
    for copy in near:
        copy.wait()
    row_pos = position_rows(window[0:16, :], row_offset, ROWS)
    col_pos = position_rows(window[16:88, :], col_offset, COLS)
    for r in range(ROWS):
        rows = slice(r * COLS, (r + 1) * COLS)
        value = tokens[rows, :].astype(F32) + row_pos[r : r + 1, :] + col_pos
        hidden[0, rows, :] = value
        act[A1, rows, :] = norm(value, small, 0)
    stores = [copies.start(hidden.at[0], hidden_out.at[0]), copies.start(act.at[A1], saved_out.at[A1])]

    def branch(first, source, planes, heads, bias, target, which, last):
        for i in range(3):
            loads[first + i].wait()
        project(act, source, planes[:3], weights, first, small, bias)
        for plane in planes[:3]:
            stores.append(copies.start(act.at[plane], saved_out.at[plane]))
        attend(heads, act, *planes)
        stores.append(copies.start(act.at[planes[3]], saved_out.at[planes[3]]))
        loads[first + 3].wait()

        def body(index):
            rows = chunk(index, 256)
            branch_out = dot(act[planes[3], rows, :], whole(weights, first + 3))
            before = hidden[which - 1, rows, :]
            after = before + (branch_out + small[bias + 2 : bias + 3, :])
            if last:
                h2[rows, :] = after
                a3[rows, :] = norm(after, small, which)
            else:
                hidden[which, rows, :] = after
                act[target, rows, :] = norm(after, small, which)

        loop(2, body)

    branch(0, A1, (Q1, K1, V1, M1), RowHeads(length), ROW_BIAS, A2, 1, False)
    stores.append(copies.start(hidden.at[1], hidden_out.at[1]))
    stores.append(copies.start(act.at[A2], saved_out.at[A2]))
    branch(4, A2, (Q2, K2, V2, M2), ColHeads(), COL_BIAS, None, 2, True)

    in_use = lax.broadcasted_iota(jnp.int32, (COLS, D), 0) < length
    for r in range(ROWS):
        rows = slice(r * COLS, (r + 1) * COLS)
        gy[rows, :] = jnp.where(in_use, cotangent[rows, :].astype(F32), 0.0).astype(BF16)
    for copy in loads[8:]:
        copy.wait()

    def ffn(f):
        up, low = whole(weights, 8 + f), down[f].reshape(D, D)
        bias = up_bias[pl.ds(f, 1), :]

        def body(index):
            rows = chunk(index, 512)
            z = dot(a3[rows, :], up) + bias
            cdf = 0.5 * (1.0 + lax.erf(z * math.sqrt(0.5)))
            slope = cdf + z * (jnp.exp(-0.5 * z * z) * (1.0 / math.sqrt(2.0 * math.pi)))
            u = (z * cdf).astype(BF16)
            wide[0, rows, :] = u
            du = dot_nt(gy[rows, :], low).astype(BF16).astype(F32)
            dz = (du * slope).astype(BF16)
            wide[1, rows, :] = dz
            more, more_da = dot(u, low), dot_nt(dz, up)

            @pl.when(f == 0)
            def _():
                y[rows, :] = more
                da[rows, :] = more_da

            @pl.when(f != 0)
            def _():
                y[rows, :] += more
                da[rows, :] += more_da

        loop(1, body)
        sums[pl.ds(f, 1), :] = total(wide[1].astype(F32))

        value = dot_tn(wide[0], gy[...]).astype(BF16).reshape(4, 8, SLAB, D)
        for k in range(8):
            grads[4 + f, 4 * k : 4 * k + 4] = value[:, k]
        value = dot_tn(a3[...], wide[1]).astype(BF16).reshape(16, 2, SLAB, D)
        for half in range(2):
            grads[f, 16 * half : 16 * half + 16] = value[:, half]
        for copy in ffn_sends(f):
            copy.start()

    first_sem = copies.used

    def ffn_sends(f):
        sends = []
        for half in range(2):
            place = (4 * half + f, slice(None), slice(0, SLAB))
            sends.append((grads.at[f, 16 * half : 16 * half + 16], shares.at[place]))
        for k in range(8):
            place = (k, pl.ds(4 * f, 4), slice(SLAB, 2 * SLAB))
            sends.append((grads.at[4 + f, 4 * k : 4 * k + 4], shares.at[place]))
        return [
            pltpu.make_async_copy(source, target, sems.at[first_sem + 10 * f + i])
            for i, (source, target) in enumerate(sends)
        ]

    loop(4, ffn)
    gain = small[GAIN + 2 : GAIN + 3, :]

    def finish(index, carry):
        rows = chunk(index, 64)
        late = h2[rows, :]
        act_out[rows, :] = (late + (y[rows, :] + small[DOWN_BIAS : DOWN_BIAS + 1, :])).astype(BF16)
        grad = da[rows, :]
        inner, unit = norm_back(grad, late, gain)
        cot = gy[rows, :].astype(F32)
        g2_out[rows, :] = cot + inner
        return carry[0] + total(unit), carry[1] + total(grad), carry[2] + total(cot)

    zero = jnp.zeros((1, D), F32)
    gain_sum, shift_sum, down_sum = lax.fori_loop(0, 8, finish, (zero, zero, zero))
    sums[4:5, :] = down_sum
    sums[5:6, :] = gain_sum
    sums[6:7, :] = shift_sum
    sums[7:8, :] = zero
    for copy in stores + [copy for f in range(4) for copy in ffn_sends(f)]:
        copy.wait()


def row_heads_kernel(ints, grad_in, gathered, saved, grads_out, weight, act, sems):
    copies = Copies(sems)
    load = copies.start(gathered.at[:, 3, 0:SLAB, :], weight.at[0])
    act_loads = [copies.start(saved.at[plane], act.at[i]) for i, plane in enumerate((Q1, K1, V1))]
    load.wait()

    def mixed_back(index):
        rows = chunk(index, 256)
        act[3, rows, :] = dot_nt(grad_in[rows, :].astype(BF16), whole(weight, 0)).astype(BF16)

    loop(2, mixed_back)
    for copy in act_loads:
        copy.wait()
    attend_back(RowHeads(ints[0]), act, 0, 1, 2, 3)
    stores = [copies.start(act.at[i], grads_out.at[i]) for i in range(3)]
    for copy in stores:
        copy.wait()


class Shares:
    def __init__(self, core, copies, own, other):
        self.core, self.copies, self.own, self.other, self.sent = core, copies, own, other, []

    def send(self, grads, member):
        every, parity = slice(None), member % 2
        for half in range(2):
            x = 2 * half + member // 2
            if parity == 0:
                places = [(grads.at[member, half], (every, every, x))]
            else:
                places = [(grads.at[member, half, y], (every, y, x)) for y in range(4)]
            for source, place in places:
                self.sent.append(
                    self.copies.send(self.core, parity, source, self.own.at[place], self.other.at[place])
                )

    def wait(self):
        for copy in self.sent:
            copy.wait()


def keep(grads, which, value):
    value = value.astype(BF16).reshape(4, 4, 2, SLAB, D)
    for half in range(2):
        grads[which, half] = value[:, :, half]


def weight_grads(loads, act_loads, grad_in, act, out_grad, normed, mixed, grads, shares):
    def low(index):
        rows = chunk(index, 128)
        out_grad[rows, :] = grad_in[rows, :].astype(BF16)

    loop(4, low)
    loads["mixed"].wait()

    keep(grads, 3, dot_tn(mixed[...], out_grad[...]))
    shares.send(grads, 3)
    for copy in [loads["normed"]] + act_loads:
        copy.wait()

    def weight_back(which):
        keep(grads, which, dot_tn(normed[...], act[which]))

    loop(3, weight_back)
    for member in range(3):
        shares.send(grads, member)


def input_grads(loads, grad_in, gain, act, weights, hidden, da, grad_out, sums, lines=None, loaded=None):
    for i in range(3):
        for copy in loads["inputs"][i]:
            copy.wait()

        def input_back(index):
            rows = chunk(index, 256)
            value = dot_nt(act[i, rows, :], whole(weights, i))
            da[rows, :] = value if i == 0 else da[rows, :] + value

        if i == 2 and loaded is not None:
            loaded()
        loop(2, input_back)
    loads["hidden"].wait()

    def finish(index, carry):
        rows = chunk(index, 64)
        grad, before = da[rows, :], grad_in[rows, :]
        inner, unit = norm_back(grad, hidden[rows, :], gain)
        value = before + inner
        grad_out[rows, :] = value
        added = [unit, grad, act[0, rows, :], act[2, rows, :], before.astype(BF16)]
        added = [total(extra.astype(F32)) for extra in added]
        if lines is not None:
            lines[pl.ds(index, 1), :] = total(value)
            added.append(value)
        return tuple(a + b for a, b in zip(carry, added))

    carry = (jnp.zeros((1, D), F32),) * 5
    if lines is not None:
        carry = carry + (jnp.zeros((COLS, D), F32),)
    carry = lax.fori_loop(0, 8, finish, carry)
    for i in range(5):
        sums[i : i + 1, :] = carry[i]
    sums[5:8, :] = jnp.zeros((3, D), F32)
    return carry[-1]


def column_kernel(
    ints, grad_in, small, gathered, saved, hidden_saved,
    grad_out, own, other, sums,
    weights, act, out_grad, normed, mixed, hidden, da, grads, sems,
):
    copies = Copies(sems)
    shares = Shares(ints[3], copies, own, other)
    slabs = [gathered.at[:, i, SLAB : 2 * SLAB, :] for i in range(4)]
    out_load = copies.start(slabs[3], weights.at[3])
    act_loads = [copies.start(saved.at[plane], act.at[i]) for i, plane in enumerate((Q2, K2, V2))]
    loads = {"mixed": copies.start(saved.at[M2], mixed), "normed": copies.start(saved.at[A2], normed)}
    loads["inputs"] = [[copies.start(slabs[i], weights.at[i])] for i in range(3)]
    loads["hidden"] = copies.start(hidden_saved.at[1], hidden)
    out_load.wait()

    def mixed_back(index):
        rows = chunk(index, 256)
        act[3, rows, :] = dot_nt(grad_in[rows, :].astype(BF16), whole(weights, 3)).astype(BF16)

    loop(2, mixed_back)
    for copy in act_loads:
        copy.wait()
    attend_back(ColHeads(), act, 0, 1, 2, 3)
    weight_grads(loads, [], grad_in, act, out_grad, normed, mixed, grads, shares)
    input_grads(loads, grad_in, small[GAIN + 1 : GAIN + 2, :], act, weights, hidden, da, grad_out, sums)
    shares.wait()


def row_weights_kernel(
    ints, grad_in, saved, grads_in, own, other, act, out_grad, normed, mixed, grads, sems
):
    copies = Copies(sems)
    shares = Shares(ints[3], copies, own, other)
    loads = {"mixed": copies.start(saved.at[M1], mixed), "normed": copies.start(saved.at[A1], normed)}
    act_loads = [copies.start(grads_in.at[i], act.at[i]) for i in range(3)]
    weight_grads(loads, act_loads, grad_in, act, out_grad, normed, mixed, grads, shares)
    shares.wait()


def small_lines(sums, sums_col, sums_ffn):
    lines = jnp.concatenate([sums[0:5, :], sums_col[0:5, :], sums_ffn[4:7, :], sums[5:8, :]], axis=0)
    shape = (DEVICES, D)
    dev, lane = (lax.broadcasted_iota(jnp.int32, shape, axis) for axis in (0, 1))
    packed = jnp.zeros((DEVICES, 128), F32)
    for j in range(6):
        pick = jnp.where(lane == 6 * dev + j, 1.0, 0.0).astype(BF16)
        blank = [jnp.zeros((16, D), F32)] * 8
        blank[j] = lines
        packed = packed + dot_nt(pick, jnp.concatenate(blank, axis=0).astype(BF16))
    up = jnp.concatenate(
        [jnp.broadcast_to(sums_ffn[f : f + 1, :], (32, D)) for f in range(4)], axis=0
    )
    first = 24 * (dev & 31)
    up = jnp.where((lane >= first) & (lane < first + 24), up, 0.0).astype(BF16)
    shape = (128, D)
    to, lane = (lax.broadcasted_iota(jnp.int32, shape, axis) for axis in (0, 1))
    fold = jnp.where(to - 96 == lane % 24, 1.0, 0.0).astype(BF16)
    return (packed + dot_nt(up, fold)).astype(BF16)


def row_input_kernel(
    ints, grad_in, small, sums_col, sums_ffn, gathered, hidden_saved, grads_in,
    grad_out, own, other,
    weights, act, hidden, da, zeros, table, lines, sums, owned_lines, sems,
):
    copies = Copies(sems)
    loads = {"inputs": []}
    for i in range(3):
        slab = gathered.at[:, i, 0:SLAB, :]
        loads["inputs"].append(
            [copies.start(grads_in.at[i], act.at[i]), copies.start(slab, weights.at[i])]
        )
    loads["hidden"] = copies.start(hidden_saved.at[0], hidden)
    zeros[...] = jnp.zeros_like(zeros)
    fills = []

    def fill():
        fills.extend(copies.start(zeros, out.at[:, :, :, :, 0:D]) for out in (own, other))

    gain = small[GAIN : GAIN + 1, :]
    col_lines = input_grads(
        loads, grad_in, gain, act, weights, hidden, da, grad_out, sums, lines, fill
    )
    packed = small_lines(sums, sums_col, sums_ffn).astype(F32).reshape(4, 4, 4, 2, 1, 128)
    owned_lines[...] = jnp.broadcast_to(packed, owned_lines.shape).astype(BF16)
    for copy in fills:
        copy.wait()
    sent = []
    for parity in range(2):
        for x in range(4):
            source, place = owned_lines.at[:, :, x, parity], (x, slice(None), slice(None), slice(0, 16), slice(D, WIDE))
            sent.append(copies.send(ints[3], parity, source, own.at[place], other.at[place]))
    send_tables(ints, copies, lines[...], col_lines, table, own, other)
    for copy in sent:
        copy.wait()


def send_tables(ints, copies, row_lines, col_lines, table, own, other):
    core = ints[3]

    def placed(values, offset, count):
        shape = (count, values.shape[0])
        here = lax.broadcasted_iota(jnp.int32, shape, 0) == (
            lax.broadcasted_iota(jnp.int32, shape, 1) + offset % 8
        )
        return dot(jnp.where(here, 1.0, 0.0).astype(BF16), values.astype(BF16)).astype(BF16)

    spots = []
    for first, count, values, offset, start in (
        (0, 2, row_lines, ints[1], 0),
        (2, 9, col_lines, ints[2], 8),
    ):
        table[first : first + count] = placed(values, offset, 8 * count).reshape(count, 8, D)
        spots += [(first + i, offset // 8 + i, start) for i in range(count)]
    waits = []
    for slot, owner, start in spots:
        real, dev = owner < DEVICES, jnp.minimum(owner, DEVICES - 1)
        x, y, z = (dev // 2) % 4, dev // 32, (dev // 8) % 4
        place = (x, y, z, slice(start, start + 8), slice(0, D))
        sem = copies.sems.at[copies.used]
        copies.used += 1
        here = pltpu.make_async_copy(table.at[slot], own.at[place], sem)
        there = pltpu.make_async_copy(table.at[slot], other.at[place], sem)
        pl.when(real & (dev % 2 == core))(here.start)
        pl.when(real & (dev % 2 != core))(there.start)
        waits.append((real, here))
    for real, copy in waits:
        pl.when(real)(copy.wait)


VMEM = pl.BlockSpec(memory_space=pltpu.VMEM)
ANY = pl.BlockSpec(memory_space=pl.ANY)
SMEM = pl.BlockSpec(memory_space=pltpu.SMEM)
SHAPE = jax.ShapeDtypeStruct


def params(mebibytes=62):
    return pltpu.CompilerParams(vmem_limit_bytes=mebibytes * 1024 * 1024)


def cost(flops, traffic):
    return pl.CostEstimate(flops=flops, transcendentals=0, bytes_accessed=traffic)


def forward_call(ints, tokens, cotangent, small, up_bias, gathered):
    plane = (TOKENS, D)
    return pl.pallas_call(
        forward_kernel,
        name="forward",
        in_specs=[SMEM, VMEM, VMEM, VMEM, VMEM, ANY],
        out_shape=(
            SHAPE(plane, BF16),
            SHAPE(plane, F32),
            SHAPE((10,) + plane, BF16),
            SHAPE((2,) + plane, F32),
            SHAPE((8, 16, 2 * SLAB, D), BF16),
            SHAPE((8, D), F32),
        ),
        out_specs=(VMEM, VMEM, ANY, ANY, ANY, VMEM),
        scratch_shapes=[
            pltpu.VMEM((12, GROUPS, SLAB, D), BF16),
            pltpu.VMEM((4, 8, MEMBERS, SLAB, D), BF16),
            pltpu.VMEM((88, D), BF16),
            pltpu.VMEM((10,) + plane, BF16),
            pltpu.VMEM((2,) + plane, F32),
            pltpu.VMEM(plane, F32),
            pltpu.VMEM(plane, BF16),
            pltpu.VMEM(plane, BF16),
            pltpu.VMEM((2,) + plane, BF16),
            pltpu.VMEM(plane, F32),
            pltpu.VMEM(plane, F32),
            pltpu.SemaphoreType.DMA((96,)),
        ],
        compiler_params=params(),
        cost_estimate=cost(24 * 10**9, 50 * 10**6),
    )(ints, tokens, cotangent, small, up_bias, gathered)


def row_heads_call(ints, grad, gathered, saved):
    plane = (TOKENS, D)
    return pl.pallas_call(
        row_heads_kernel,
        name="row_heads",
        in_specs=[SMEM, VMEM, ANY, ANY],
        out_shape=SHAPE((3,) + plane, BF16),
        out_specs=ANY,
        scratch_shapes=[
            pltpu.VMEM((1, GROUPS, SLAB, D), BF16),
            pltpu.VMEM((4,) + plane, BF16),
            pltpu.SemaphoreType.DMA((8,)),
        ],
        compiler_params=params(),
        cost_estimate=cost(10**10, 10**7),
    )(ints, grad, gathered, saved)


PLANE = (TOKENS, D)


def share_of(rows):
    return SHAPE((4, 4, 4, rows, D), BF16)


def column_call(ints, grad, small, gathered, saved, hidden):
    return pl.pallas_call(
        column_kernel,
        name="column_back",
        in_specs=[SMEM, VMEM, VMEM, ANY, ANY, ANY],
        out_shape=(SHAPE(PLANE, F32), share_of(SLAB), share_of(SLAB), SHAPE((8, D), F32)),
        out_specs=(VMEM, ANY, ANY, VMEM),
        scratch_shapes=[
            pltpu.VMEM((4, GROUPS, SLAB, D), BF16),
            pltpu.VMEM((4,) + PLANE, BF16),
            pltpu.VMEM(PLANE, BF16),
            pltpu.VMEM(PLANE, BF16),
            pltpu.VMEM(PLANE, BF16),
            pltpu.VMEM(PLANE, F32),
            pltpu.VMEM(PLANE, F32),
            pltpu.VMEM((4, 2, 4, 4, SLAB, D), BF16),
            pltpu.SemaphoreType.DMA((48,)),
        ],
        compiler_params=params(),
        cost_estimate=cost(10**10, 10**7),
    )(ints, grad, small, gathered, saved, hidden)


def row_weights_call(ints, grad, saved, grads):
    return pl.pallas_call(
        row_weights_kernel,
        name="row_weights",
        in_specs=[SMEM, VMEM, ANY, ANY],
        out_shape=(share_of(SLAB), share_of(SLAB)),
        out_specs=(ANY, ANY),
        scratch_shapes=[
            pltpu.VMEM((3,) + PLANE, BF16),
            pltpu.VMEM(PLANE, BF16),
            pltpu.VMEM(PLANE, BF16),
            pltpu.VMEM(PLANE, BF16),
            pltpu.VMEM((4, 2, 4, 4, SLAB, D), BF16),
            pltpu.SemaphoreType.DMA((32,)),
        ],
        compiler_params=params(),
        cost_estimate=cost(10**6, 10**5),
    )(ints, grad, saved, grads)


def row_input_call(ints, grad, small, sums_col, sums_ffn, gathered, hidden, grads):
    return pl.pallas_call(
        row_input_kernel,
        name="row_input",
        in_specs=[SMEM, VMEM, VMEM, VMEM, VMEM, ANY, ANY, ANY],
        out_shape=(SHAPE(PLANE, F32),) + (SHAPE((4, 4, 4, 16, WIDE), BF16),) * 2,
        out_specs=(VMEM, ANY, ANY),
        scratch_shapes=[
            pltpu.VMEM((3, GROUPS, SLAB, D), BF16),
            pltpu.VMEM((3,) + PLANE, BF16),
            pltpu.VMEM(PLANE, F32),
            pltpu.VMEM(PLANE, F32),
            pltpu.VMEM((4, 4, 4, 16, D), BF16),
            pltpu.VMEM((11, 8, D), BF16),
            pltpu.VMEM((ROWS, D), F32),
            pltpu.VMEM((8, D), F32),
            pltpu.VMEM((4, 4, 4, 2, 16, 128), BF16),
            pltpu.SemaphoreType.DMA((48,)),
        ],
        compiler_params=params(),
        cost_estimate=cost(2 * 10**10, 10**7),
    )(ints, grad, small, sums_col, sums_ffn, gathered, hidden, grads)


def sum_of(pieces, *index):
    value = pieces[0][index].astype(F32)
    for piece in pieces[1:]:
        value = value + piece[index].astype(F32)
    return value


def split_kernel(place, *refs):
    for hop in range(4):
        to = (place[0] + hop) & 3
        for j in range(refs[-1].shape[0]):
            refs[-4 + hop][j] = sum_of(refs[:-4], to, j).astype(BF16)


def split(inputs, place):
    shape = inputs[0].shape
    rest = (0,) * (len(shape) - 2)
    large = len(shape) == 5
    in_block = pl.BlockSpec((4, 1) + shape[2:], lambda j: (0, j) + rest) if large else VMEM
    out_block = pl.BlockSpec((1,) + shape[2:], lambda j: (j,) + rest) if large else VMEM
    return pl.pallas_call(
        split_kernel,
        name="split_shares",
        grid=(4,) if large else (),
        in_specs=[SMEM] + [in_block] * len(inputs),
        out_shape=(SHAPE(shape[1:], BF16),) * 4,
        out_specs=(out_block,) * 4,
        compiler_params=params(62 if large else 6),
        cost_estimate=cost(10**6, 10**6),
    )(place, *inputs)


def second_kernel(place, *refs):
    for hop in range(4):
        to = (place[0] + hop) & 3

        def body(j):
            for g in range(2):
                value = sum_of(refs[4 * g : 4 * g + 4], to, j)
                refs[8 + hop][j, g * SLAB : (g + 1) * SLAB, :] = value.astype(BF16)

        loop(4, body)


def second_split(row, col, place):
    return pl.pallas_call(
        second_kernel,
        name="second_split",
        in_specs=[SMEM] + [VMEM] * 8,
        out_shape=(SHAPE((4, 2 * SLAB, D), BF16),) * 4,
        out_specs=(VMEM,) * 4,
        compiler_params=params(10),
        cost_estimate=cost(10**6, 10**6),
    )(place, *row, *col)


def third_kernel(place, table_place, ffn, *refs):
    rows, table, pieces = refs[:4], refs[4:8], refs[8:]
    for hop in range(4):
        pieces[hop][...] = sum_of(rows, (place[0] + hop) & 3).astype(BF16)
        to = (table_place[0] + hop) & 3
        value = sum_of(table, to).astype(BF16)
        pieces[4 + hop][0:16, :] = value[:, 0:D]
        pieces[4 + hop][16:24, :] = jnp.zeros((8, D), BF16)
        pieces[4 + hop][16:24, 0:128] = value[0:8, D:WIDE]
        pieces[4 + hop][SLAB : 3 * SLAB, :] = ffn[to]


def third_split(rows, table, ffn, place, table_place):
    return pl.pallas_call(
        third_kernel,
        name="third_split",
        in_specs=[SMEM] * 2 + [VMEM] * 9,
        out_shape=(SHAPE((2 * SLAB, D), BF16),) * 4 + (SHAPE((3 * SLAB, D), BF16),) * 4,
        out_specs=(VMEM,) * 8,
        compiler_params=params(6),
        cost_estimate=cost(10**6, 10**6),
    )(place, table_place, ffn, *rows, *table)


def last_kernel(me, *refs):
    rows, rest, (down, tables), small, pieces, held = refs[:4], refs[4:8], refs[8:10], refs[10:16], refs[16:20], refs[20]
    down[...] = sum_of(rest, slice(2 * SLAB, 3 * SLAB))
    for i in range(2):
        tables[i] = sum_of(rest, slice(8 * i, 8 * i + 8))
    line = sum_of(rest, slice(16, 24), slice(0, 128))[0:1]
    gain, shift, row_bias, col_bias, up_bias, down_bias = small
    up_bias[...] = line[:, 96:120]
    lines = jnp.broadcast_to(line, (16, 128))
    value, lane = (lax.broadcasted_iota(jnp.int32, lines.shape, axis) for axis in (0, 1))
    for j in range(6):
        column = jnp.sum(jnp.where(lane == 16 * j + value, lines, 0.0), axis=1, keepdims=True)
        at = slice(j, j + 1)
        for i, first in enumerate((0, 5, 11)):
            gain[i : i + 1, at] = column[first : first + 1]
            shift[i : i + 1, at] = column[first + 1 : first + 2]
        row_bias[:, at], col_bias[:, at] = column[2:5], column[7:10]
        down_bias[:, at] = column[10:11]
    for kind, (source, start) in enumerate(((rows, 0), (rows, SLAB), (rest, SLAB))):
        value = sum_of(source, slice(start, start + SLAB))
        for member in range(MEMBERS):
            held[member, kind] = value[6 * member : 6 * member + 6, :]
    for flip in range(4):
        pieces[flip][...] = held[me[0] ^ flip].astype(BF16)


def last_split(me, rows, rest):
    return pl.pallas_call(
        last_kernel,
        name="last_split",
        in_specs=[SMEM] + [VMEM] * 8,
        out_shape=(
            SHAPE((SLAB, D), F32),
            SHAPE((2, 8, D), F32),
        )
        + (SHAPE((3, 6), F32),) * 4
        + (SHAPE((1, SLAB), F32), SHAPE((1, 6), F32))
        + (SHAPE((3, 6, D), BF16),) * 4,
        out_specs=(VMEM,) * 12,
        scratch_shapes=[pltpu.VMEM((MEMBERS, 3, 6, D), F32)],
        compiler_params=params(6),
        cost_estimate=cost(10**6, 10**6),
    )(me, *rows, *rest)


def outputs_kernel(me, one, two, three, four, row_qkv, row_out, col_qkv, col_out, up, held):
    for flip, piece in enumerate((one, two, three, four)):
        held[me[0] ^ flip] = piece[...].astype(F32)
    for i in range(3):
        row_qkv[i], col_qkv[i] = held[i, 0], held[i, 1]
    row_out[...], col_out[...] = held[3, 0], held[3, 1]
    for i in range(MEMBERS):
        up[:, i * D : (i + 1) * D] = held[i, 2]


def outputs(me, pieces):
    return pl.pallas_call(
        outputs_kernel,
        name="outputs",
        in_specs=[SMEM] + [VMEM] * 4,
        out_shape=(
            SHAPE((3, 6, D), F32),
            SHAPE((6, D), F32),
            SHAPE((3, 6, D), F32),
            SHAPE((6, D), F32),
            SHAPE((6, FF), F32),
        ),
        out_specs=(VMEM,) * 5,
        scratch_shapes=[pltpu.VMEM((MEMBERS, 3, 6, D), F32)],
        compiler_params=params(6),
        cost_estimate=cost(10**6, 10**6),
    )(me, *pieces)


def take(value, index, dim):
    return lax.squeeze(lax.dynamic_slice_in_dim(value, index, 1, dim), (dim,))


def member():
    return (lax.axis_index("x") % 2) * 2 + lax.axis_index("c")


def trade(pieces):
    came = [pieces[0]]
    for flip in range(1, 4):
        pairs = [(i, (i // 4) * 4 + ((i % 4) ^ flip)) for i in range(8)]
        came.append(lax.ppermute(pieces[flip], ("x", "c"), pairs))
    return came


def exchange(blocks):
    me = member()
    parts = trade([take(blocks, me ^ flip, 0) for flip in range(4)])
    odd, high = (me & 1) == 1, (me & 2) == 2
    pairs = [jnp.where(odd, parts[i ^ 1], parts[i]) for i in range(4)]
    return [jnp.where(high, pairs[i ^ 2], pairs[i]) for i in range(4)]


def swap(value):
    return lax.ppermute(value, "c", [(0, 1), (1, 0)])


def scatter_chip_rows(shares):
    return lax.psum_scatter(shares, ("x", "c"), scatter_dimension=0, tiled=False)


STAGES = (("y", "z"), ("z", "y"), ("x", "x"))
TABLE_STAGES = (("x", "x"), ("y", "y"), ("z", "z"))
STRIDES = {"y": 32, "z": 8, "x": 2}


def place_on(axes):
    here = jnp.where(lax.axis_index("c") == 0, lax.axis_index(axes[0]), lax.axis_index(axes[1]))
    return here.astype(jnp.int32)[None]


def deliver(pieces, axes):
    came = [pieces[0]]
    for hop in range(1, 4):
        pairs = []
        for dev in range(DEVICES):
            stride = STRIDES[axes[dev % 2]]
            at = dev // stride % 4
            pairs.append((dev, dev + ((at + hop) % 4 - at) * stride))
        came.append(lax.ppermute(pieces[hop], AXES, pairs))
    return came


def gather(norm_gain, norm_bias, row_qkv, row_out, row_bias, col_qkv, col_out, col_bias,
           ffn_up, up_bias, ffn_down, down_bias, pos_tables):
    row = jnp.concatenate([row_qkv, row_out[None]], axis=0)
    col = jnp.concatenate([col_qkv, col_out[None]], axis=0)
    up = ffn_up.reshape(6, MEMBERS, D).transpose(1, 0, 2)
    slabs = jnp.stack(exchange(jnp.stack([row, col, up], axis=1)), axis=1)
    packed = jnp.concatenate(
        [slabs.reshape(3 * SLAB, D), ffn_down, pos_tables[0], pos_tables[1]], axis=0
    )
    gathered = lax.all_gather(packed, AXES, axis=0, tiled=False)
    sixes = jnp.concatenate([norm_gain, norm_bias, row_bias, col_bias, down_bias[None]], axis=0)
    line = jnp.pad(jnp.concatenate([sixes.reshape(-1), up_bias]), (0, 26))
    lines = lax.all_gather(line, AXES, axis=0, tiled=False).astype(F32)
    small = lines[:, :78].reshape(DEVICES, 13, 6).transpose(1, 0, 2).reshape(13, D)
    small = jnp.pad(small, ((0, 3), (0, 0)))
    return gathered.reshape(GROUPS, MEMBERS, PACK, D), small, lines[:, 78:102].reshape(4, D)


def on_device(tokens, cotangent, lengths, row_offset, col_offset, *weights):
    gathered, small, up_bias = gather(*weights)
    core = lax.axis_index("c").astype(jnp.int32)
    ints = jnp.concatenate([lengths, row_offset, col_offset, core[None]])
    act, g2, saved, hidden, ffn_shares, ffn_sums = forward_call(
        ints, tokens.reshape(TOKENS, D), cotangent.reshape(TOKENS, D), small, up_bias, gathered
    )
    barrier = lax.optimization_barrier
    ffn = scatter_chip_rows(ffn_shares)
    g1, own, other, col_sums = column_call(ints, g2, small, gathered, saved, hidden)
    row_heads = row_heads_call(ints, g1, gathered, saved)
    places = [place_on(axes) for axes in STAGES]
    other, row_heads = barrier((swap(other), row_heads))
    pieces, row_heads = barrier((split((own, other), places[0]), row_heads))
    col = deliver(pieces, STAGES[0])
    g0, table_own, table_other = row_input_call(
        ints, g1, small, col_sums, ffn_sums, gathered, hidden, row_heads
    )
    own, other = row_weights_call(ints, g1, saved, row_heads)
    table_other, col = barrier((table_other, col))
    other, table_other, ffn = barrier((other, swap(table_other), ffn))
    ffn = lax.psum_scatter(ffn.reshape(4, 4, 2 * SLAB, D), "y", scatter_dimension=0, tiled=False)
    y_place, z_place = place_on(TABLE_STAGES[1]), place_on(TABLE_STAGES[2])
    table, other = barrier((split((table_own, table_other), places[2]), swap(other)))
    table = deliver(table, TABLE_STAGES[0])
    row = deliver(split((own, other), places[0]), STAGES[0])
    table = deliver(split(table, y_place), TABLE_STAGES[1])
    rows = deliver(second_split(row, col, places[1]), STAGES[1])
    pieces = third_split(rows, table, ffn, places[2], z_place)
    rows, rest = deliver(pieces[:4], STAGES[2]), deliver(pieces[4:], TABLE_STAGES[2])
    return (act.reshape(tokens.shape), g0.reshape(tokens.shape)) + owned(rows, rest)


def owned(rows, rest):
    me = member().astype(jnp.int32)[None]
    down, tables, gain, shift, row_bias, col_bias, up_bias, down_bias, *pieces = last_split(me, rows, rest)
    row_qkv, row_out, col_qkv, col_out, up = outputs(me, trade(pieces))
    return (
        gain,
        shift,
        row_qkv,
        row_out,
        row_bias,
        col_qkv,
        col_out,
        col_bias,
        up,
        up_bias[0],
        down,
        down_bias[0],
        tables,
    )


def solution(mesh):
    mesh = Mesh(mesh.devices.reshape(4, 4, 4, 2), AXES)
    first, second = P(AXES), P(None, AXES)
    weights = (second, second, second, first, second, second, first, second) + (first,) * 4 + (second,)
    return jax.shard_map(
        on_device,
        mesh=mesh,
        in_specs=(first,) * 5 + weights,
        out_specs=(first, first) + weights,
        check_vma=False,
    )
```

```python
import math

import jax
import jax.numpy as jnp
from jax import lax
from jax.experimental import pallas as pl
from jax.experimental.pallas import tpu as pltpu
from jax.sharding import Mesh, PartitionSpec as P

AXES = ("y", "z", "x", "c")
DEVICES = 128
GROUPS = 32
MEMBERS = 4
D = 768
FF = 3072
HEAD_DIM = 64
POSITIONS = 1024
ROWS = 8
COLS = 64
TOKENS = ROWS * COLS
SLAB = 24
WIDE = D + 128
PACK = 112
PAIRS = 6
EPS = 1e-05
MASKED = -1e30
ROW_SCALE = 1.0 / math.sqrt(HEAD_DIM * ROWS)
COL_SCALE = 1.0 / math.sqrt(HEAD_DIM)
BF16 = jnp.bfloat16
F32 = jnp.float32
GAIN, SHIFT, ROW_BIAS, COL_BIAS, DOWN_BIAS = 0, 3, 6, 9, 12
A1, Q1, K1, V1, M1, A2, Q2, K2, V2, M2 = range(10)


def dot(left, right):
    return jnp.dot(left, right, preferred_element_type=F32)


def dot_nt(left, right):
    return lax.dot_general(left, right, (((1,), (1,)), ((), ())), preferred_element_type=F32)


def dot_tn(left, right):
    return lax.dot_general(left, right, (((0,), (0,)), ((), ())), preferred_element_type=F32)


def chunk(index, size):
    return pl.ds(pl.multiple_of(index * size, size), size)


def loop(count, body, unroll=1):
    def step(index, carry):
        body(index)
        return carry

    lax.fori_loop(0, count, step, 0, unroll=unroll)


def unit_of(hidden):
    centred = hidden - jnp.mean(hidden, axis=-1, keepdims=True)
    inverse = lax.rsqrt(jnp.mean(centred * centred, axis=-1, keepdims=True) + EPS)
    return centred * inverse, inverse


def norm(hidden, small, which):
    unit, _ = unit_of(hidden)
    gain, shift = small[GAIN + which : GAIN + which + 1, :], small[SHIFT + which : SHIFT + which + 1, :]
    return (unit * gain + shift).astype(BF16)


def norm_back(grad, hidden, gain):
    unit, inverse = unit_of(hidden)
    inner = grad * gain
    mean = jnp.mean(inner, axis=-1, keepdims=True)
    cross = jnp.mean(inner * unit, axis=-1, keepdims=True)
    return inverse * (inner - mean - unit * cross), grad * unit


def total(value):
    return jnp.sum(value, axis=0, keepdims=True)


def first_head(shape):
    return (lax.broadcasted_iota(jnp.int32, shape, 1) & 127) < HEAD_DIM


def stack_heads(value):
    keep = jnp.where(first_head(value.shape), 1.0, 0.0)
    return jnp.concatenate([value * keep.astype(BF16), value * (1.0 - keep).astype(BF16)], axis=0)


def merge_heads(value):
    half = value.shape[0] // 2
    return jnp.where(first_head((half, value.shape[1])), value[:half], value[half:])


def softmax(scores):
    top = jnp.max(scores, axis=-1, keepdims=True)
    raised = jnp.exp(scores - top)
    return raised / jnp.sum(raised, axis=-1, keepdims=True)


class RowHeads:
    scale = ROW_SCALE
    steps = 2

    def __init__(self, length):
        self.length = length

    def blocks(self, step):
        return [chunk(3 * step + i, 128) for i in range(3)]

    def load(self, ref, plane, lanes):
        return jnp.concatenate(
            [ref[plane, r * COLS : (r + 1) * COLS, lanes] for r in range(ROWS)], axis=1
        )

    def store(self, ref, plane, lanes, value):
        for r in range(ROWS):
            ref[plane, r * COLS : (r + 1) * COLS, lanes] = value[:, r * 128 : (r + 1) * 128]

    def mask(self):
        shape = (2 * COLS, COLS)
        return lax.broadcasted_iota(jnp.int32, shape, 1) < self.length


class ColHeads:
    scale = COL_SCALE
    steps = PAIRS

    def blocks(self, step):
        return [(i * 16, chunk(step, 128)) for i in range(4)]

    def load(self, ref, plane, block):
        start, lanes = block
        return jnp.concatenate(
            [ref[plane, r * COLS + start : r * COLS + start + 16, lanes] for r in range(ROWS)], axis=0
        )

    def store(self, ref, plane, block, value):
        start, lanes = block
        for r in range(ROWS):
            ref[plane, r * COLS + start : r * COLS + start + 16, lanes] = value[16 * r : 16 * r + 16]

    def mask(self):
        row = lax.broadcasted_iota(jnp.int32, (256, 128), 0) & 15
        return row == (lax.broadcasted_iota(jnp.int32, (256, 128), 1) & 15)


def each(function, *lists):
    return [function(*values) for values in zip(*lists)]


def weights_of(heads, queries, keys):
    mask = heads.mask()
    scores = each(dot_nt, queries, keys)
    return each(lambda s: softmax(jnp.where(mask, s * heads.scale, MASKED)), scores)


def attend(heads, ref, q, k, v, m):
    def body(step):
        blocks = heads.blocks(step)
        queries, keys, values = (
            [heads.load(ref, plane, block) for block in blocks] for plane in (q, k, v)
        )
        probs = weights_of(heads, each(stack_heads, queries), keys)
        mixed = each(lambda p, value: dot(p.astype(BF16), value), probs, values)
        for block, value in zip(blocks, mixed):
            heads.store(ref, m, block, merge_heads(value).astype(BF16))

    loop(heads.steps, body)


def attend_back(heads, ref, q, k, v, dm):
    def body(step):
        blocks = heads.blocks(step)
        queries, keys, values, mixed = (
            [heads.load(ref, plane, block) for block in blocks] for plane in (q, k, v, dm)
        )
        queries, mixed = each(stack_heads, queries), each(stack_heads, mixed)
        probs = weights_of(heads, queries, keys)
        grad = each(dot_nt, mixed, values)
        grad_values = each(lambda p, value: dot_tn(p.astype(BF16), value), probs, mixed)
        inner = each(
            lambda p, g: (p * (g - jnp.sum(g * p, axis=-1, keepdims=True))).astype(BF16), probs, grad
        )
        grad_queries = each(lambda i, key: merge_heads(dot(i, key)) * heads.scale, inner, keys)
        grad_keys = each(lambda i, query: dot_tn(i, query) * heads.scale, inner, queries)
        for i, block in enumerate(blocks):
            heads.store(ref, q, block, grad_queries[i].astype(BF16))
            heads.store(ref, k, block, grad_keys[i].astype(BF16))
            heads.store(ref, v, block, grad_values[i].astype(BF16))

    loop(heads.steps, body)


def whole(ref, index):
    return ref[index].reshape(D, D)


def project(ref, source, planes, weights, first, small, bias_row):
    def body(index):
        rows = chunk(index, 256)
        normed = ref[source, rows, :]
        for i, plane in enumerate(planes):
            value = dot(normed, whole(weights, first + i))
            if i != 1:
                row = bias_row + (0 if i == 0 else 1)
                value = value + small[row : row + 1, :]
            ref[plane, rows, :] = value.astype(BF16)

    loop(2, body)


class Copies:
    def __init__(self, sems):
        self.sems, self.used = sems, 0

    def start(self, source, target):
        copy = pltpu.make_async_copy(source, target, self.sems.at[self.used])
        self.used += 1
        copy.start()
        return copy

    def send(self, core, parity, source, own, other):
        sem = self.sems.at[self.used]
        self.used += 1
        here = pltpu.make_async_copy(source, own, sem)
        there = pltpu.make_async_copy(source, other, sem)
        pl.when(core == parity)(here.start)
        pl.when(core != parity)(there.start)
        return here


def position_rows(window, offset, count):
    shape = (count, window.shape[0])
    pick = lax.broadcasted_iota(jnp.int32, shape, 1) == (
        lax.broadcasted_iota(jnp.int32, shape, 0) + offset % 8
    )
    return dot(jnp.where(pick, 1.0, 0.0).astype(BF16), window)


def forward_kernel(
    ints, tokens, cotangent, small, up_bias, gathered,
    act_out, g2_out, saved_out, hidden_out, shares, sums,
    weights, down, window, act, hidden, h2, a3, gy, wide, y, da, sems,
):
    grads = weights
    length, row_offset, col_offset = ints[0], ints[1], ints[2]
    copies = Copies(sems)
    near = []
    for i in range(2):
        dev = jnp.minimum(row_offset // 8 + i, DEVICES - 1)
        near.append(
            copies.start(gathered.at[dev // 4, dev % 4, 96:104, :], window.at[8 * i : 8 * i + 8, :])
        )
    for i in range(9):
        dev = jnp.minimum(col_offset // 8 + i, DEVICES - 1)
        near.append(
            copies.start(
                gathered.at[dev // 4, dev % 4, 104:112, :], window.at[16 + 8 * i : 24 + 8 * i, :]
            )
        )
    loads = [
        copies.start(gathered.at[:, i % 4, 24 * (i // 4) : 24 * (i // 4) + 24, :], weights.at[i])
        for i in range(12)
    ]
    loads += [
        copies.start(gathered.at[8 * f : 8 * f + 8, :, 72:96, :], down.at[f]) for f in range(4)
    ]
    for copy in near:
        copy.wait()
    row_pos = position_rows(window[0:16, :], row_offset, ROWS)
    col_pos = position_rows(window[16:88, :], col_offset, COLS)
    for r in range(ROWS):
        rows = slice(r * COLS, (r + 1) * COLS)
        value = tokens[rows, :].astype(F32) + row_pos[r : r + 1, :] + col_pos
        hidden[0, rows, :] = value
        act[A1, rows, :] = norm(value, small, 0)
    stores = [copies.start(hidden.at[0], hidden_out.at[0]), copies.start(act.at[A1], saved_out.at[A1])]

    def branch(first, source, planes, heads, bias, target, which, last):
        for i in range(3):
            loads[first + i].wait()
        project(act, source, planes[:3], weights, first, small, bias)
        for plane in planes[:3]:
            stores.append(copies.start(act.at[plane], saved_out.at[plane]))
        attend(heads, act, *planes)
        stores.append(copies.start(act.at[planes[3]], saved_out.at[planes[3]]))
        loads[first + 3].wait()

        def body(index):
            rows = chunk(index, 256)
            branch_out = dot(act[planes[3], rows, :], whole(weights, first + 3))
            before = hidden[which - 1, rows, :]
            after = before + (branch_out + small[bias + 2 : bias + 3, :])
            if last:
                h2[rows, :] = after
                a3[rows, :] = norm(after, small, which)
            else:
                hidden[which, rows, :] = after
                act[target, rows, :] = norm(after, small, which)

        loop(2, body)

    branch(0, A1, (Q1, K1, V1, M1), RowHeads(length), ROW_BIAS, A2, 1, False)
    stores.append(copies.start(hidden.at[1], hidden_out.at[1]))
    stores.append(copies.start(act.at[A2], saved_out.at[A2]))
    branch(4, A2, (Q2, K2, V2, M2), ColHeads(), COL_BIAS, None, 2, True)

    in_use = lax.broadcasted_iota(jnp.int32, (COLS, D), 0) < length
    for r in range(ROWS):
        rows = slice(r * COLS, (r + 1) * COLS)
        gy[rows, :] = jnp.where(in_use, cotangent[rows, :].astype(F32), 0.0).astype(BF16)
    for copy in loads[8:]:
        copy.wait()

    def ffn(f):
        up, low = whole(weights, 8 + f), down[f].reshape(D, D)
        bias = up_bias[pl.ds(f, 1), :]

        def body(index):
            rows = chunk(index, 512)
            z = dot(a3[rows, :], up) + bias
            cdf = 0.5 * (1.0 + lax.erf(z * math.sqrt(0.5)))
            slope = cdf + z * (jnp.exp(-0.5 * z * z) * (1.0 / math.sqrt(2.0 * math.pi)))
            u = (z * cdf).astype(BF16)
            wide[0, rows, :] = u
            du = dot_nt(gy[rows, :], low).astype(BF16).astype(F32)
            dz = (du * slope).astype(BF16)
            wide[1, rows, :] = dz
            more, more_da = dot(u, low), dot_nt(dz, up)

            @pl.when(f == 0)
            def _():
                y[rows, :] = more
                da[rows, :] = more_da

            @pl.when(f != 0)
            def _():
                y[rows, :] += more
                da[rows, :] += more_da

        loop(1, body)
        sums[pl.ds(f, 1), :] = total(wide[1].astype(F32))

        value = dot_tn(wide[0], gy[...]).astype(BF16).reshape(4, 8, SLAB, D)
        for k in range(8):
            grads[4 + f, 4 * k : 4 * k + 4] = value[:, k]
        value = dot_tn(a3[...], wide[1]).astype(BF16).reshape(16, 2, SLAB, D)
        for half in range(2):
            grads[f, 16 * half : 16 * half + 16] = value[:, half]
        for copy in ffn_sends(f):
            copy.start()

    first_sem = copies.used

    def ffn_sends(f):
        sends = []
        for half in range(2):
            place = (4 * half + f, slice(None), slice(0, SLAB))
            sends.append((grads.at[f, 16 * half : 16 * half + 16], shares.at[place]))
        for k in range(8):
            place = (k, pl.ds(4 * f, 4), slice(SLAB, 2 * SLAB))
            sends.append((grads.at[4 + f, 4 * k : 4 * k + 4], shares.at[place]))
        return [
            pltpu.make_async_copy(source, target, sems.at[first_sem + 10 * f + i])
            for i, (source, target) in enumerate(sends)
        ]

    loop(4, ffn)
    gain = small[GAIN + 2 : GAIN + 3, :]

    def finish(index, carry):
        rows = chunk(index, 64)
        late = h2[rows, :]
        act_out[rows, :] = (late + (y[rows, :] + small[DOWN_BIAS : DOWN_BIAS + 1, :])).astype(BF16)
        grad = da[rows, :]
        inner, unit = norm_back(grad, late, gain)
        cot = gy[rows, :].astype(F32)
        g2_out[rows, :] = cot + inner
        return carry[0] + total(unit), carry[1] + total(grad), carry[2] + total(cot)

    zero = jnp.zeros((1, D), F32)
    gain_sum, shift_sum, down_sum = lax.fori_loop(0, 8, finish, (zero, zero, zero))
    sums[4:5, :] = down_sum
    sums[5:6, :] = gain_sum
    sums[6:7, :] = shift_sum
    sums[7:8, :] = zero
    for copy in stores + [copy for f in range(4) for copy in ffn_sends(f)]:
        copy.wait()


def row_heads_kernel(ints, grad_in, gathered, saved, grads_out, weight, act, sems):
    copies = Copies(sems)
    load = copies.start(gathered.at[:, 3, 0:SLAB, :], weight.at[0])
    act_loads = [copies.start(saved.at[plane], act.at[i]) for i, plane in enumerate((Q1, K1, V1))]
    load.wait()

    def mixed_back(index):
        rows = chunk(index, 256)
        act[3, rows, :] = dot_nt(grad_in[rows, :].astype(BF16), whole(weight, 0)).astype(BF16)

    loop(2, mixed_back)
    for copy in act_loads:
        copy.wait()
    attend_back(RowHeads(ints[0]), act, 0, 1, 2, 3)
    stores = [copies.start(act.at[i], grads_out.at[i]) for i in range(3)]
    for copy in stores:
        copy.wait()


class Shares:
    def __init__(self, core, copies, own, other):
        self.core, self.copies, self.own, self.other, self.sent = core, copies, own, other, []

    def send(self, grads, member):
        every, parity = slice(None), member % 2
        for half in range(2):
            x = 2 * half + member // 2
            if parity == 0:
                places = [(grads.at[member, half], (every, every, x))]
            else:
                places = [(grads.at[member, half, y], (every, y, x)) for y in range(4)]
            for source, place in places:
                self.sent.append(
                    self.copies.send(self.core, parity, source, self.own.at[place], self.other.at[place])
                )

    def wait(self):
        for copy in self.sent:
            copy.wait()


def keep(grads, which, value):
    value = value.astype(BF16).reshape(4, 4, 2, SLAB, D)
    for half in range(2):
        grads[which, half] = value[:, :, half]


def weight_grads(loads, act_loads, grad_in, act, out_grad, normed, mixed, grads, shares):
    def low(index):
        rows = chunk(index, 128)
        out_grad[rows, :] = grad_in[rows, :].astype(BF16)

    loop(4, low)
    loads["mixed"].wait()

    keep(grads, 3, dot_tn(mixed[...], out_grad[...]))
    shares.send(grads, 3)
    for copy in [loads["normed"]] + act_loads:
        copy.wait()

    def weight_back(which):
        keep(grads, which, dot_tn(normed[...], act[which]))

    loop(3, weight_back)
    for member in range(3):
        shares.send(grads, member)


def input_grads(loads, grad_in, gain, act, weights, hidden, da, grad_out, sums, lines=None, loaded=None):
    for i in range(3):
        for copy in loads["inputs"][i]:
            copy.wait()

        def input_back(index):
            rows = chunk(index, 256)
            value = dot_nt(act[i, rows, :], whole(weights, i))
            da[rows, :] = value if i == 0 else da[rows, :] + value

        if i == 2 and loaded is not None:
            loaded()
        loop(2, input_back)
    loads["hidden"].wait()

    def finish(index, carry):
        rows = chunk(index, 64)
        grad, before = da[rows, :], grad_in[rows, :]
        inner, unit = norm_back(grad, hidden[rows, :], gain)
        value = before + inner
        grad_out[rows, :] = value
        added = [unit, grad, act[0, rows, :], act[2, rows, :], before.astype(BF16)]
        added = [total(extra.astype(F32)) for extra in added]
        if lines is not None:
            lines[pl.ds(index, 1), :] = total(value)
            added.append(value)
        return tuple(a + b for a, b in zip(carry, added))

    carry = (jnp.zeros((1, D), F32),) * 5
    if lines is not None:
        carry = carry + (jnp.zeros((COLS, D), F32),)
    carry = lax.fori_loop(0, 8, finish, carry)
    for i in range(5):
        sums[i : i + 1, :] = carry[i]
    sums[5:8, :] = jnp.zeros((3, D), F32)
    return carry[-1]


def column_kernel(
    ints, grad_in, small, gathered, saved, hidden_saved,
    grad_out, own, other, sums,
    weights, act, out_grad, normed, mixed, hidden, da, grads, sems,
):
    copies = Copies(sems)
    shares = Shares(ints[3], copies, own, other)
    slabs = [gathered.at[:, i, SLAB : 2 * SLAB, :] for i in range(4)]
    out_load = copies.start(slabs[3], weights.at[3])
    act_loads = [copies.start(saved.at[plane], act.at[i]) for i, plane in enumerate((Q2, K2, V2))]
    loads = {"mixed": copies.start(saved.at[M2], mixed), "normed": copies.start(saved.at[A2], normed)}
    loads["inputs"] = [[copies.start(slabs[i], weights.at[i])] for i in range(3)]
    loads["hidden"] = copies.start(hidden_saved.at[1], hidden)
    out_load.wait()

    def mixed_back(index):
        rows = chunk(index, 256)
        act[3, rows, :] = dot_nt(grad_in[rows, :].astype(BF16), whole(weights, 3)).astype(BF16)

    loop(2, mixed_back)
    for copy in act_loads:
        copy.wait()
    attend_back(ColHeads(), act, 0, 1, 2, 3)
    weight_grads(loads, [], grad_in, act, out_grad, normed, mixed, grads, shares)
    input_grads(loads, grad_in, small[GAIN + 1 : GAIN + 2, :], act, weights, hidden, da, grad_out, sums)
    shares.wait()


def row_weights_kernel(
    ints, grad_in, saved, grads_in, own, other, act, out_grad, normed, mixed, grads, sems
):
    copies = Copies(sems)
    shares = Shares(ints[3], copies, own, other)
    loads = {"mixed": copies.start(saved.at[M1], mixed), "normed": copies.start(saved.at[A1], normed)}
    act_loads = [copies.start(grads_in.at[i], act.at[i]) for i in range(3)]
    weight_grads(loads, act_loads, grad_in, act, out_grad, normed, mixed, grads, shares)
    shares.wait()


def small_lines(sums, sums_col, sums_ffn):
    lines = jnp.concatenate([sums[0:5, :], sums_col[0:5, :], sums_ffn[4:7, :], sums[5:8, :]], axis=0)
    shape = (DEVICES, D)
    dev, lane = (lax.broadcasted_iota(jnp.int32, shape, axis) for axis in (0, 1))
    packed = jnp.zeros((DEVICES, 128), F32)
    for j in range(6):
        pick = jnp.where(lane == 6 * dev + j, 1.0, 0.0).astype(BF16)
        blank = [jnp.zeros((16, D), F32)] * 8
        blank[j] = lines
        packed = packed + dot_nt(pick, jnp.concatenate(blank, axis=0).astype(BF16))
    up = jnp.concatenate(
        [jnp.broadcast_to(sums_ffn[f : f + 1, :], (32, D)) for f in range(4)], axis=0
    )
    first = 24 * (dev & 31)
    up = jnp.where((lane >= first) & (lane < first + 24), up, 0.0).astype(BF16)
    shape = (128, D)
    to, lane = (lax.broadcasted_iota(jnp.int32, shape, axis) for axis in (0, 1))
    fold = jnp.where(to - 96 == lane % 24, 1.0, 0.0).astype(BF16)
    return (packed + dot_nt(up, fold)).astype(BF16)


def row_input_kernel(
    ints, grad_in, small, sums_col, sums_ffn, gathered, hidden_saved, grads_in,
    grad_out, own, other,
    weights, act, hidden, da, zeros, table, lines, sums, owned_lines, sems,
):
    copies = Copies(sems)
    loads = {"inputs": []}
    for i in range(3):
        slab = gathered.at[:, i, 0:SLAB, :]
        loads["inputs"].append(
            [copies.start(grads_in.at[i], act.at[i]), copies.start(slab, weights.at[i])]
        )
    loads["hidden"] = copies.start(hidden_saved.at[0], hidden)
    zeros[...] = jnp.zeros_like(zeros)
    fills = []

    def fill():
        fills.extend(copies.start(zeros, out.at[:, :, :, :, 0:D]) for out in (own, other))

    gain = small[GAIN : GAIN + 1, :]
    col_lines = input_grads(
        loads, grad_in, gain, act, weights, hidden, da, grad_out, sums, lines, fill
    )
    packed = small_lines(sums, sums_col, sums_ffn).astype(F32).reshape(4, 4, 4, 2, 1, 128)
    owned_lines[...] = jnp.broadcast_to(packed, owned_lines.shape).astype(BF16)
    for copy in fills:
        copy.wait()
    sent = []
    for parity in range(2):
        for x in range(4):
            source, place = owned_lines.at[:, :, x, parity], (x, slice(None), slice(None), slice(0, 16), slice(D, WIDE))
            sent.append(copies.send(ints[3], parity, source, own.at[place], other.at[place]))
    send_tables(ints, copies, lines[...], col_lines, table, own, other)
    for copy in sent:
        copy.wait()


def send_tables(ints, copies, row_lines, col_lines, table, own, other):
    core = ints[3]

    def placed(values, offset, count):
        shape = (count, values.shape[0])
        here = lax.broadcasted_iota(jnp.int32, shape, 0) == (
            lax.broadcasted_iota(jnp.int32, shape, 1) + offset % 8
        )
        return dot(jnp.where(here, 1.0, 0.0).astype(BF16), values.astype(BF16)).astype(BF16)

    spots = []
    for first, count, values, offset, start in (
        (0, 2, row_lines, ints[1], 0),
        (2, 9, col_lines, ints[2], 8),
    ):
        table[first : first + count] = placed(values, offset, 8 * count).reshape(count, 8, D)
        spots += [(first + i, offset // 8 + i, start) for i in range(count)]
    waits = []
    for slot, owner, start in spots:
        real, dev = owner < DEVICES, jnp.minimum(owner, DEVICES - 1)
        x, y, z = (dev // 2) % 4, dev // 32, (dev // 8) % 4
        place = (x, y, z, slice(start, start + 8), slice(0, D))
        sem = copies.sems.at[copies.used]
        copies.used += 1
        here = pltpu.make_async_copy(table.at[slot], own.at[place], sem)
        there = pltpu.make_async_copy(table.at[slot], other.at[place], sem)
        pl.when(real & (dev % 2 == core))(here.start)
        pl.when(real & (dev % 2 != core))(there.start)
        waits.append((real, here))
    for real, copy in waits:
        pl.when(real)(copy.wait)


VMEM = pl.BlockSpec(memory_space=pltpu.VMEM)
ANY = pl.BlockSpec(memory_space=pl.ANY)
SMEM = pl.BlockSpec(memory_space=pltpu.SMEM)
SHAPE = jax.ShapeDtypeStruct


def params(mebibytes=62):
    return pltpu.CompilerParams(vmem_limit_bytes=mebibytes * 1024 * 1024)


def cost(flops, traffic):
    return pl.CostEstimate(flops=flops, transcendentals=0, bytes_accessed=traffic)


def forward_call(ints, tokens, cotangent, small, up_bias, gathered):
    plane = (TOKENS, D)
    return pl.pallas_call(
        forward_kernel,
        name="forward",
        in_specs=[SMEM, VMEM, VMEM, VMEM, VMEM, ANY],
        out_shape=(
            SHAPE(plane, BF16),
            SHAPE(plane, F32),
            SHAPE((10,) + plane, BF16),
            SHAPE((2,) + plane, F32),
            SHAPE((8, 16, 2 * SLAB, D), BF16),
            SHAPE((8, D), F32),
        ),
        out_specs=(VMEM, VMEM, ANY, ANY, ANY, VMEM),
        scratch_shapes=[
            pltpu.VMEM((12, GROUPS, SLAB, D), BF16),
            pltpu.VMEM((4, 8, MEMBERS, SLAB, D), BF16),
            pltpu.VMEM((88, D), BF16),
            pltpu.VMEM((10,) + plane, BF16),
            pltpu.VMEM((2,) + plane, F32),
            pltpu.VMEM(plane, F32),
            pltpu.VMEM(plane, BF16),
            pltpu.VMEM(plane, BF16),
            pltpu.VMEM((2,) + plane, BF16),
            pltpu.VMEM(plane, F32),
            pltpu.VMEM(plane, F32),
            pltpu.SemaphoreType.DMA((96,)),
        ],
        compiler_params=params(),
        cost_estimate=cost(24 * 10**9, 50 * 10**6),
    )(ints, tokens, cotangent, small, up_bias, gathered)


def row_heads_call(ints, grad, gathered, saved):
    plane = (TOKENS, D)
    return pl.pallas_call(
        row_heads_kernel,
        name="row_heads",
        in_specs=[SMEM, VMEM, ANY, ANY],
        out_shape=SHAPE((3,) + plane, BF16),
        out_specs=ANY,
        scratch_shapes=[
            pltpu.VMEM((1, GROUPS, SLAB, D), BF16),
            pltpu.VMEM((4,) + plane, BF16),
            pltpu.SemaphoreType.DMA((8,)),
        ],
        compiler_params=params(),
        cost_estimate=cost(10**10, 10**7),
    )(ints, grad, gathered, saved)


PLANE = (TOKENS, D)


def share_of(rows):
    return SHAPE((4, 4, 4, rows, D), BF16)


def column_call(ints, grad, small, gathered, saved, hidden):
    return pl.pallas_call(
        column_kernel,
        name="column_back",
        in_specs=[SMEM, VMEM, VMEM, ANY, ANY, ANY],
        out_shape=(SHAPE(PLANE, F32), share_of(SLAB), share_of(SLAB), SHAPE((8, D), F32)),
        out_specs=(VMEM, ANY, ANY, VMEM),
        scratch_shapes=[
            pltpu.VMEM((4, GROUPS, SLAB, D), BF16),
            pltpu.VMEM((4,) + PLANE, BF16),
            pltpu.VMEM(PLANE, BF16),
            pltpu.VMEM(PLANE, BF16),
            pltpu.VMEM(PLANE, BF16),
            pltpu.VMEM(PLANE, F32),
            pltpu.VMEM(PLANE, F32),
            pltpu.VMEM((4, 2, 4, 4, SLAB, D), BF16),
            pltpu.SemaphoreType.DMA((48,)),
        ],
        compiler_params=params(),
        cost_estimate=cost(10**10, 10**7),
    )(ints, grad, small, gathered, saved, hidden)


def row_weights_call(ints, grad, saved, grads):
    return pl.pallas_call(
        row_weights_kernel,
        name="row_weights",
        in_specs=[SMEM, VMEM, ANY, ANY],
        out_shape=(share_of(SLAB), share_of(SLAB)),
        out_specs=(ANY, ANY),
        scratch_shapes=[
            pltpu.VMEM((3,) + PLANE, BF16),
            pltpu.VMEM(PLANE, BF16),
            pltpu.VMEM(PLANE, BF16),
            pltpu.VMEM(PLANE, BF16),
            pltpu.VMEM((4, 2, 4, 4, SLAB, D), BF16),
            pltpu.SemaphoreType.DMA((32,)),
        ],
        compiler_params=params(),
        cost_estimate=cost(10**6, 10**5),
    )(ints, grad, saved, grads)


def row_input_call(ints, grad, small, sums_col, sums_ffn, gathered, hidden, grads):
    return pl.pallas_call(
        row_input_kernel,
        name="row_input",
        in_specs=[SMEM, VMEM, VMEM, VMEM, VMEM, ANY, ANY, ANY],
        out_shape=(SHAPE(PLANE, F32),) + (SHAPE((4, 4, 4, 16, WIDE), BF16),) * 2,
        out_specs=(VMEM, ANY, ANY),
        scratch_shapes=[
            pltpu.VMEM((3, GROUPS, SLAB, D), BF16),
            pltpu.VMEM((3,) + PLANE, BF16),
            pltpu.VMEM(PLANE, F32),
            pltpu.VMEM(PLANE, F32),
            pltpu.VMEM((4, 4, 4, 16, D), BF16),
            pltpu.VMEM((11, 8, D), BF16),
            pltpu.VMEM((ROWS, D), F32),
            pltpu.VMEM((8, D), F32),
            pltpu.VMEM((4, 4, 4, 2, 16, 128), BF16),
            pltpu.SemaphoreType.DMA((48,)),
        ],
        compiler_params=params(),
        cost_estimate=cost(2 * 10**10, 10**7),
    )(ints, grad, small, sums_col, sums_ffn, gathered, hidden, grads)


def sum_of(pieces, *index):
    value = pieces[0][index].astype(F32)
    for piece in pieces[1:]:
        value = value + piece[index].astype(F32)
    return value


def split_kernel(place, *refs):
    for hop in range(4):
        to = (place[0] + hop) & 3
        for j in range(refs[-1].shape[0]):
            refs[-4 + hop][j] = sum_of(refs[:-4], to, j).astype(BF16)


def split(inputs, place):
    shape = inputs[0].shape
    rest = (0,) * (len(shape) - 2)
    large = len(shape) == 5
    in_block = pl.BlockSpec((4, 1) + shape[2:], lambda j: (0, j) + rest) if large else VMEM
    out_block = pl.BlockSpec((1,) + shape[2:], lambda j: (j,) + rest) if large else VMEM
    return pl.pallas_call(
        split_kernel,
        name="split_shares",
        grid=(4,) if large else (),
        in_specs=[SMEM] + [in_block] * len(inputs),
        out_shape=(SHAPE(shape[1:], BF16),) * 4,
        out_specs=(out_block,) * 4,
        compiler_params=params(62 if large else 6),
        cost_estimate=cost(10**6, 10**6),
    )(place, *inputs)


def sum_kernel(*refs):
    def body(j):
        refs[-1][j] = sum_of(refs[:-1], j).astype(BF16)

    loop(4, body)


def summed(parts):
    return pl.pallas_call(
        sum_kernel,
        name="column_sum",
        in_specs=[VMEM] * 4,
        out_shape=SHAPE(parts[0].shape, BF16),
        out_specs=VMEM,
        compiler_params=params(8),
        cost_estimate=cost(10**6, 10**6),
    )(*parts)


def second_kernel(place, *refs):
    for hop in range(4):
        to = (place[0] + hop) & 3

        def body(j):
            refs[5 + hop][j, 0:SLAB, :] = sum_of(refs[:4], to, j).astype(BF16)
            refs[5 + hop][j, SLAB : 2 * SLAB, :] = refs[4][to, j]

        loop(4, body)


def second_split(row, col, place):
    return pl.pallas_call(
        second_kernel,
        name="second_split",
        in_specs=[SMEM] + [VMEM] * 5,
        out_shape=(SHAPE((4, 2 * SLAB, D), BF16),) * 4,
        out_specs=(VMEM,) * 4,
        compiler_params=params(10),
        cost_estimate=cost(10**6, 10**6),
    )(place, *row, col)


def third_kernel(place, table_place, ffn, *refs):
    rows, table, pieces = refs[:4], refs[4:8], refs[8:]
    for hop in range(4):
        pieces[hop][...] = sum_of(rows, (place[0] + hop) & 3).astype(BF16)
        to = (table_place[0] + hop) & 3
        value = sum_of(table, to).astype(BF16)
        pieces[4 + hop][0:16, :] = value[:, 0:D]
        pieces[4 + hop][16:24, :] = jnp.zeros((8, D), BF16)
        pieces[4 + hop][16:24, 0:128] = value[0:8, D:WIDE]
        pieces[4 + hop][SLAB : 3 * SLAB, :] = ffn[to]


def third_split(rows, table, ffn, place, table_place):
    return pl.pallas_call(
        third_kernel,
        name="third_split",
        in_specs=[SMEM] * 2 + [VMEM] * 9,
        out_shape=(SHAPE((2 * SLAB, D), BF16),) * 4 + (SHAPE((3 * SLAB, D), BF16),) * 4,
        out_specs=(VMEM,) * 8,
        compiler_params=params(6),
        cost_estimate=cost(10**6, 10**6),
    )(place, table_place, ffn, *rows, *table)


def last_kernel(me, *refs):
    rows, rest, (down, tables), small, pieces, held = refs[:4], refs[4:8], refs[8:10], refs[10:16], refs[16:20], refs[20]
    down[...] = sum_of(rest, slice(2 * SLAB, 3 * SLAB))
    for i in range(2):
        tables[i] = sum_of(rest, slice(8 * i, 8 * i + 8))
    line = sum_of(rest, slice(16, 24), slice(0, 128))[0:1]
    gain, shift, row_bias, col_bias, up_bias, down_bias = small
    up_bias[...] = line[:, 96:120]
    lines = jnp.broadcast_to(line, (16, 128))
    value, lane = (lax.broadcasted_iota(jnp.int32, lines.shape, axis) for axis in (0, 1))
    for j in range(6):
        column = jnp.sum(jnp.where(lane == 16 * j + value, lines, 0.0), axis=1, keepdims=True)
        at = slice(j, j + 1)
        for i, first in enumerate((0, 5, 11)):
            gain[i : i + 1, at] = column[first : first + 1]
            shift[i : i + 1, at] = column[first + 1 : first + 2]
        row_bias[:, at], col_bias[:, at] = column[2:5], column[7:10]
        down_bias[:, at] = column[10:11]
    for kind, (source, start) in enumerate(((rows, 0), (rows, SLAB), (rest, SLAB))):
        value = sum_of(source, slice(start, start + SLAB))
        for member in range(MEMBERS):
            held[member, kind] = value[6 * member : 6 * member + 6, :]
    for flip in range(4):
        pieces[flip][...] = held[me[0] ^ flip].astype(BF16)


def last_split(me, rows, rest):
    return pl.pallas_call(
        last_kernel,
        name="last_split",
        in_specs=[SMEM] + [VMEM] * 8,
        out_shape=(
            SHAPE((SLAB, D), F32),
            SHAPE((2, 8, D), F32),
        )
        + (SHAPE((3, 6), F32),) * 4
        + (SHAPE((1, SLAB), F32), SHAPE((1, 6), F32))
        + (SHAPE((3, 6, D), BF16),) * 4,
        out_specs=(VMEM,) * 12,
        scratch_shapes=[pltpu.VMEM((MEMBERS, 3, 6, D), F32)],
        compiler_params=params(6),
        cost_estimate=cost(10**6, 10**6),
    )(me, *rows, *rest)


def outputs_kernel(me, one, two, three, four, row_qkv, row_out, col_qkv, col_out, up, held):
    for flip, piece in enumerate((one, two, three, four)):
        held[me[0] ^ flip] = piece[...].astype(F32)
    for i in range(3):
        row_qkv[i], col_qkv[i] = held[i, 0], held[i, 1]
    row_out[...], col_out[...] = held[3, 0], held[3, 1]
    for i in range(MEMBERS):
        up[:, i * D : (i + 1) * D] = held[i, 2]


def outputs(me, pieces):
    return pl.pallas_call(
        outputs_kernel,
        name="outputs",
        in_specs=[SMEM] + [VMEM] * 4,
        out_shape=(
            SHAPE((3, 6, D), F32),
            SHAPE((6, D), F32),
            SHAPE((3, 6, D), F32),
            SHAPE((6, D), F32),
            SHAPE((6, FF), F32),
        ),
        out_specs=(VMEM,) * 5,
        scratch_shapes=[pltpu.VMEM((MEMBERS, 3, 6, D), F32)],
        compiler_params=params(6),
        cost_estimate=cost(10**6, 10**6),
    )(me, *pieces)


def take(value, index, dim):
    return lax.squeeze(lax.dynamic_slice_in_dim(value, index, 1, dim), (dim,))


def member():
    return (lax.axis_index("x") % 2) * 2 + lax.axis_index("c")


def trade(pieces):
    came = [pieces[0]]
    for flip in range(1, 4):
        pairs = [(i, (i // 4) * 4 + ((i % 4) ^ flip)) for i in range(8)]
        came.append(lax.ppermute(pieces[flip], ("x", "c"), pairs))
    return came


def exchange(blocks):
    me = member()
    parts = trade([take(blocks, me ^ flip, 0) for flip in range(4)])
    odd, high = (me & 1) == 1, (me & 2) == 2
    pairs = [jnp.where(odd, parts[i ^ 1], parts[i]) for i in range(4)]
    return [jnp.where(high, pairs[i ^ 2], pairs[i]) for i in range(4)]


def swap(value):
    return lax.ppermute(value, "c", [(0, 1), (1, 0)])


def scatter_chip_rows(shares):
    return lax.psum_scatter(shares, ("x", "c"), scatter_dimension=0, tiled=False)


STAGES = (("y", "z"), ("z", "y"), ("x", "x"))
TABLE_STAGES = (("x", "x"), ("y", "y"), ("z", "z"))
STRIDES = {"y": 32, "z": 8, "x": 2}


def place_on(axes):
    here = jnp.where(lax.axis_index("c") == 0, lax.axis_index(axes[0]), lax.axis_index(axes[1]))
    return here.astype(jnp.int32)[None]


def deliver(pieces, axes):
    came = [pieces[0]]
    for hop in range(1, 4):
        pairs = []
        for dev in range(DEVICES):
            stride = STRIDES[axes[dev % 2]]
            at = dev // stride % 4
            pairs.append((dev, dev + ((at + hop) % 4 - at) * stride))
        came.append(lax.ppermute(pieces[hop], AXES, pairs))
    return came


def gather(norm_gain, norm_bias, row_qkv, row_out, row_bias, col_qkv, col_out, col_bias,
           ffn_up, up_bias, ffn_down, down_bias, pos_tables):
    row = jnp.concatenate([row_qkv, row_out[None]], axis=0)
    col = jnp.concatenate([col_qkv, col_out[None]], axis=0)
    up = ffn_up.reshape(6, MEMBERS, D).transpose(1, 0, 2)
    slabs = jnp.stack(exchange(jnp.stack([row, col, up], axis=1)), axis=1)
    packed = jnp.concatenate(
        [slabs.reshape(3 * SLAB, D), ffn_down, pos_tables[0], pos_tables[1]], axis=0
    )
    gathered = lax.all_gather(packed, AXES, axis=0, tiled=False)
    sixes = jnp.concatenate([norm_gain, norm_bias, row_bias, col_bias, down_bias[None]], axis=0)
    line = jnp.pad(jnp.concatenate([sixes.reshape(-1), up_bias]), (0, 26))
    lines = lax.all_gather(line, AXES, axis=0, tiled=False).astype(F32)
    small = lines[:, :78].reshape(DEVICES, 13, 6).transpose(1, 0, 2).reshape(13, D)
    small = jnp.pad(small, ((0, 3), (0, 0)))
    return gathered.reshape(GROUPS, MEMBERS, PACK, D), small, lines[:, 78:102].reshape(4, D)


def on_device(tokens, cotangent, lengths, row_offset, col_offset, *weights):
    gathered, small, up_bias = gather(*weights)
    core = lax.axis_index("c").astype(jnp.int32)
    ints = jnp.concatenate([lengths, row_offset, col_offset, core[None]])
    act, g2, saved, hidden, ffn_shares, ffn_sums = forward_call(
        ints, tokens.reshape(TOKENS, D), cotangent.reshape(TOKENS, D), small, up_bias, gathered
    )
    barrier = lax.optimization_barrier
    ffn = scatter_chip_rows(ffn_shares)
    g1, own, other, col_sums = column_call(ints, g2, small, gathered, saved, hidden)
    row_heads = row_heads_call(ints, g1, gathered, saved)
    places = [place_on(axes) for axes in STAGES]
    other, row_heads = barrier((swap(other), row_heads))
    pieces, row_heads = barrier((split((own, other), places[0]), row_heads))
    col = deliver(pieces, STAGES[0])
    g0, table_own, table_other = row_input_call(
        ints, g1, small, col_sums, ffn_sums, gathered, hidden, row_heads
    )
    own, other = row_weights_call(ints, g1, saved, row_heads)
    table_other, col = barrier((table_other, col))
    other, table_other, ffn = barrier((other, swap(table_other), ffn))
    ffn = lax.psum_scatter(ffn.reshape(4, 4, 2 * SLAB, D), "y", scatter_dimension=0, tiled=False)
    y_place, z_place = place_on(TABLE_STAGES[1]), place_on(TABLE_STAGES[2])
    table, other = barrier((split((table_own, table_other), places[2]), swap(other)))
    table = deliver(table, TABLE_STAGES[0])
    pieces, col = barrier((split((own, other), places[0]), col))
    row = deliver(pieces, STAGES[0])
    col = summed(col)
    table = deliver(split(table, y_place), TABLE_STAGES[1])
    rows = deliver(second_split(row, col, places[1]), STAGES[1])
    pieces = third_split(rows, table, ffn, places[2], z_place)
    rows, rest = deliver(pieces[:4], STAGES[2]), deliver(pieces[4:], TABLE_STAGES[2])
    return (act.reshape(tokens.shape), g0.reshape(tokens.shape)) + owned(rows, rest)


def owned(rows, rest):
    me = member().astype(jnp.int32)[None]
    down, tables, gain, shift, row_bias, col_bias, up_bias, down_bias, *pieces = last_split(me, rows, rest)
    row_qkv, row_out, col_qkv, col_out, up = outputs(me, trade(pieces))
    return (
        gain,
        shift,
        row_qkv,
        row_out,
        row_bias,
        col_qkv,
        col_out,
        col_bias,
        up,
        up_bias[0],
        down,
        down_bias[0],
        tables,
    )


def solution(mesh):
    mesh = Mesh(mesh.devices.reshape(4, 4, 4, 2), AXES)
    first, second = P(AXES), P(None, AXES)
    weights = (second, second, second, first, second, second, first, second) + (first,) * 4 + (second,)
    return jax.shard_map(
        on_device,
        mesh=mesh,
        in_specs=(first,) * 5 + weights,
        out_specs=(first, first) + weights,
        check_vma=False,
    )
```

```python
import math

import jax
import jax.numpy as jnp
from jax import lax
from jax.experimental import pallas as pl
from jax.experimental.pallas import tpu as pltpu
from jax.sharding import Mesh, PartitionSpec as P

AXES = ("y", "z", "x", "c")
DEVICES = 128
GROUPS = 32
MEMBERS = 4
D = 768
FF = 3072
HEAD_DIM = 64
POSITIONS = 1024
ROWS = 8
COLS = 64
TOKENS = ROWS * COLS
SLAB = 24
WIDE = D + 128
PACK = 112
PAIRS = 6
EPS = 1e-05
MASKED = -1e30
ROW_SCALE = 1.0 / math.sqrt(HEAD_DIM * ROWS)
COL_SCALE = 1.0 / math.sqrt(HEAD_DIM)
BF16 = jnp.bfloat16
F32 = jnp.float32
GAIN, SHIFT, ROW_BIAS, COL_BIAS, DOWN_BIAS = 0, 3, 6, 9, 12
A1, Q1, K1, V1, M1, A2, Q2, K2, V2, M2 = range(10)


def dot(left, right):
    return jnp.dot(left, right, preferred_element_type=F32)


def dot_nt(left, right):
    return lax.dot_general(left, right, (((1,), (1,)), ((), ())), preferred_element_type=F32)


def dot_tn(left, right):
    return lax.dot_general(left, right, (((0,), (0,)), ((), ())), preferred_element_type=F32)


def chunk(index, size):
    return pl.ds(pl.multiple_of(index * size, size), size)


def loop(count, body, unroll=1):
    def step(index, carry):
        body(index)
        return carry

    lax.fori_loop(0, count, step, 0, unroll=unroll)


def unit_of(hidden):
    centred = hidden - jnp.mean(hidden, axis=-1, keepdims=True)
    inverse = lax.rsqrt(jnp.mean(centred * centred, axis=-1, keepdims=True) + EPS)
    return centred * inverse, inverse


def norm(hidden, small, which):
    unit, _ = unit_of(hidden)
    gain, shift = small[GAIN + which : GAIN + which + 1, :], small[SHIFT + which : SHIFT + which + 1, :]
    return (unit * gain + shift).astype(BF16)


def norm_back(grad, hidden, gain):
    unit, inverse = unit_of(hidden)
    inner = grad * gain
    mean = jnp.mean(inner, axis=-1, keepdims=True)
    cross = jnp.mean(inner * unit, axis=-1, keepdims=True)
    return inverse * (inner - mean - unit * cross), grad * unit


def total(value):
    return jnp.sum(value, axis=0, keepdims=True)


def first_head(shape):
    return (lax.broadcasted_iota(jnp.int32, shape, 1) & 127) < HEAD_DIM


def stack_heads(value):
    keep = jnp.where(first_head(value.shape), 1.0, 0.0)
    return jnp.concatenate([value * keep.astype(BF16), value * (1.0 - keep).astype(BF16)], axis=0)


def merge_heads(value):
    half = value.shape[0] // 2
    return jnp.where(first_head((half, value.shape[1])), value[:half], value[half:])


def softmax(scores):
    top = jnp.max(scores, axis=-1, keepdims=True)
    raised = jnp.exp(scores - top)
    return raised / jnp.sum(raised, axis=-1, keepdims=True)


class RowHeads:
    scale = ROW_SCALE
    steps = 2

    def __init__(self, length):
        self.length = length

    def blocks(self, step):
        return [chunk(3 * step + i, 128) for i in range(3)]

    def load(self, ref, plane, lanes):
        return jnp.concatenate(
            [ref[plane, r * COLS : (r + 1) * COLS, lanes] for r in range(ROWS)], axis=1
        )

    def store(self, ref, plane, lanes, value):
        for r in range(ROWS):
            ref[plane, r * COLS : (r + 1) * COLS, lanes] = value[:, r * 128 : (r + 1) * 128]

    def mask(self):
        shape = (2 * COLS, COLS)
        return lax.broadcasted_iota(jnp.int32, shape, 1) < self.length


class ColHeads:
    scale = COL_SCALE
    steps = PAIRS

    def blocks(self, step):
        return [(i * 16, chunk(step, 128)) for i in range(4)]

    def load(self, ref, plane, block):
        start, lanes = block
        return jnp.concatenate(
            [ref[plane, r * COLS + start : r * COLS + start + 16, lanes] for r in range(ROWS)], axis=0
        )

    def store(self, ref, plane, block, value):
        start, lanes = block
        for r in range(ROWS):
            ref[plane, r * COLS + start : r * COLS + start + 16, lanes] = value[16 * r : 16 * r + 16]

    def mask(self):
        row = lax.broadcasted_iota(jnp.int32, (256, 128), 0) & 15
        return row == (lax.broadcasted_iota(jnp.int32, (256, 128), 1) & 15)


def each(function, *lists):
    return [function(*values) for values in zip(*lists)]


def weights_of(heads, queries, keys):
    mask = heads.mask()
    scores = each(dot_nt, queries, keys)
    return each(lambda s: softmax(jnp.where(mask, s * heads.scale, MASKED)), scores)


def attend(heads, ref, q, k, v, m):
    def body(step):
        blocks = heads.blocks(step)
        queries, keys, values = (
            [heads.load(ref, plane, block) for block in blocks] for plane in (q, k, v)
        )
        probs = weights_of(heads, each(stack_heads, queries), keys)
        mixed = each(lambda p, value: dot(p.astype(BF16), value), probs, values)
        for block, value in zip(blocks, mixed):
            heads.store(ref, m, block, merge_heads(value).astype(BF16))

    loop(heads.steps, body)


def attend_back(heads, ref, q, k, v, dm):
    def body(step):
        blocks = heads.blocks(step)
        queries, keys, values, mixed = (
            [heads.load(ref, plane, block) for block in blocks] for plane in (q, k, v, dm)
        )
        queries, mixed = each(stack_heads, queries), each(stack_heads, mixed)
        probs = weights_of(heads, queries, keys)
        grad = each(dot_nt, mixed, values)
        grad_values = each(lambda p, value: dot_tn(p.astype(BF16), value), probs, mixed)
        inner = each(
            lambda p, g: (p * (g - jnp.sum(g * p, axis=-1, keepdims=True))).astype(BF16), probs, grad
        )
        grad_queries = each(lambda i, key: merge_heads(dot(i, key)) * heads.scale, inner, keys)
        grad_keys = each(lambda i, query: dot_tn(i, query) * heads.scale, inner, queries)
        for i, block in enumerate(blocks):
            heads.store(ref, q, block, grad_queries[i].astype(BF16))
            heads.store(ref, k, block, grad_keys[i].astype(BF16))
            heads.store(ref, v, block, grad_values[i].astype(BF16))

    loop(heads.steps, body)


def whole(ref, index):
    return ref[index].reshape(D, D)


def project(ref, source, planes, weights, first, small, bias_row):
    def body(index):
        rows = chunk(index, 256)
        normed = ref[source, rows, :]
        for i, plane in enumerate(planes):
            value = dot(normed, whole(weights, first + i))
            if i != 1:
                row = bias_row + (0 if i == 0 else 1)
                value = value + small[row : row + 1, :]
            ref[plane, rows, :] = value.astype(BF16)

    loop(2, body)


class Copies:
    def __init__(self, sems):
        self.sems, self.used = sems, 0

    def start(self, source, target):
        copy = pltpu.make_async_copy(source, target, self.sems.at[self.used])
        self.used += 1
        copy.start()
        return copy

    def send(self, core, parity, source, own, other):
        sem = self.sems.at[self.used]
        self.used += 1
        here = pltpu.make_async_copy(source, own, sem)
        there = pltpu.make_async_copy(source, other, sem)
        pl.when(core == parity)(here.start)
        pl.when(core != parity)(there.start)
        return here


def position_rows(window, offset, count):
    shape = (count, window.shape[0])
    pick = lax.broadcasted_iota(jnp.int32, shape, 1) == (
        lax.broadcasted_iota(jnp.int32, shape, 0) + offset % 8
    )
    return dot(jnp.where(pick, 1.0, 0.0).astype(BF16), window)


def forward_kernel(
    ints, tokens, cotangent, small, up_bias, gathered,
    act_out, g2_out, saved_out, hidden_out, shares, sums,
    weights, down, window, act, hidden, h2, a3, gy, wide, y, da, sems,
):
    grads = weights
    length, row_offset, col_offset = ints[0], ints[1], ints[2]
    copies = Copies(sems)
    near = []
    for i in range(2):
        dev = jnp.minimum(row_offset // 8 + i, DEVICES - 1)
        near.append(
            copies.start(gathered.at[dev // 4, dev % 4, 96:104, :], window.at[8 * i : 8 * i + 8, :])
        )
    for i in range(9):
        dev = jnp.minimum(col_offset // 8 + i, DEVICES - 1)
        near.append(
            copies.start(
                gathered.at[dev // 4, dev % 4, 104:112, :], window.at[16 + 8 * i : 24 + 8 * i, :]
            )
        )
    loads = [
        copies.start(gathered.at[:, i % 4, 24 * (i // 4) : 24 * (i // 4) + 24, :], weights.at[i])
        for i in range(12)
    ]
    loads += [
        copies.start(gathered.at[8 * f : 8 * f + 8, :, 72:96, :], down.at[f]) for f in range(4)
    ]
    for copy in near:
        copy.wait()
    row_pos = position_rows(window[0:16, :], row_offset, ROWS)
    col_pos = position_rows(window[16:88, :], col_offset, COLS)
    for r in range(ROWS):
        rows = slice(r * COLS, (r + 1) * COLS)
        value = tokens[rows, :].astype(F32) + row_pos[r : r + 1, :] + col_pos
        hidden[0, rows, :] = value
        act[A1, rows, :] = norm(value, small, 0)
    stores = [copies.start(hidden.at[0], hidden_out.at[0]), copies.start(act.at[A1], saved_out.at[A1])]

    def branch(first, source, planes, heads, bias, target, which, last):
        for i in range(3):
            loads[first + i].wait()
        project(act, source, planes[:3], weights, first, small, bias)
        for plane in planes[:3]:
            stores.append(copies.start(act.at[plane], saved_out.at[plane]))
        attend(heads, act, *planes)
        stores.append(copies.start(act.at[planes[3]], saved_out.at[planes[3]]))
        loads[first + 3].wait()

        def body(index):
            rows = chunk(index, 256)
            branch_out = dot(act[planes[3], rows, :], whole(weights, first + 3))
            before = hidden[which - 1, rows, :]
            after = before + (branch_out + small[bias + 2 : bias + 3, :])
            if last:
                h2[rows, :] = after
                a3[rows, :] = norm(after, small, which)
            else:
                hidden[which, rows, :] = after
                act[target, rows, :] = norm(after, small, which)

        loop(2, body)

    branch(0, A1, (Q1, K1, V1, M1), RowHeads(length), ROW_BIAS, A2, 1, False)
    stores.append(copies.start(hidden.at[1], hidden_out.at[1]))
    stores.append(copies.start(act.at[A2], saved_out.at[A2]))
    branch(4, A2, (Q2, K2, V2, M2), ColHeads(), COL_BIAS, None, 2, True)

    in_use = lax.broadcasted_iota(jnp.int32, (COLS, D), 0) < length
    for r in range(ROWS):
        rows = slice(r * COLS, (r + 1) * COLS)
        gy[rows, :] = jnp.where(in_use, cotangent[rows, :].astype(F32), 0.0).astype(BF16)
    for copy in loads[8:]:
        copy.wait()

    def ffn(f):
        up, low = whole(weights, 8 + f), down[f].reshape(D, D)
        bias = up_bias[pl.ds(f, 1), :]

        def body(index):
            rows = chunk(index, 512)
            z = dot(a3[rows, :], up) + bias
            cdf = 0.5 * (1.0 + lax.erf(z * math.sqrt(0.5)))
            slope = cdf + z * (jnp.exp(-0.5 * z * z) * (1.0 / math.sqrt(2.0 * math.pi)))
            u = (z * cdf).astype(BF16)
            wide[0, rows, :] = u
            du = dot_nt(gy[rows, :], low).astype(BF16).astype(F32)
            dz = (du * slope).astype(BF16)
            wide[1, rows, :] = dz
            more, more_da = dot(u, low), dot_nt(dz, up)

            @pl.when(f == 0)
            def _():
                y[rows, :] = more
                da[rows, :] = more_da

            @pl.when(f != 0)
            def _():
                y[rows, :] += more
                da[rows, :] += more_da

        loop(1, body)
        sums[pl.ds(f, 1), :] = total(wide[1].astype(F32))

        value = dot_tn(wide[0], gy[...]).astype(BF16).reshape(4, 8, SLAB, D)
        for k in range(8):
            grads[4 + f, 4 * k : 4 * k + 4] = value[:, k]
        value = dot_tn(a3[...], wide[1]).astype(BF16).reshape(16, 2, SLAB, D)
        for half in range(2):
            grads[f, 16 * half : 16 * half + 16] = value[:, half]
        for copy in ffn_sends(f):
            copy.start()

    first_sem = copies.used

    def ffn_sends(f):
        sends = []
        for half in range(2):
            place = (4 * half + f, slice(None), slice(0, SLAB))
            sends.append((grads.at[f, 16 * half : 16 * half + 16], shares.at[place]))
        for k in range(8):
            place = (k, pl.ds(4 * f, 4), slice(SLAB, 2 * SLAB))
            sends.append((grads.at[4 + f, 4 * k : 4 * k + 4], shares.at[place]))
        return [
            pltpu.make_async_copy(source, target, sems.at[first_sem + 10 * f + i])
            for i, (source, target) in enumerate(sends)
        ]

    loop(4, ffn)
    gain = small[GAIN + 2 : GAIN + 3, :]

    def finish(index, carry):
        rows = chunk(index, 64)
        late = h2[rows, :]
        act_out[rows, :] = (late + (y[rows, :] + small[DOWN_BIAS : DOWN_BIAS + 1, :])).astype(BF16)
        grad = da[rows, :]
        inner, unit = norm_back(grad, late, gain)
        cot = gy[rows, :].astype(F32)
        g2_out[rows, :] = cot + inner
        return carry[0] + total(unit), carry[1] + total(grad), carry[2] + total(cot)

    zero = jnp.zeros((1, D), F32)
    gain_sum, shift_sum, down_sum = lax.fori_loop(0, 8, finish, (zero, zero, zero))
    sums[4:5, :] = down_sum
    sums[5:6, :] = gain_sum
    sums[6:7, :] = shift_sum
    sums[7:8, :] = zero
    for copy in stores + [copy for f in range(4) for copy in ffn_sends(f)]:
        copy.wait()


def row_heads_kernel(ints, grad_in, gathered, saved, grads_out, weight, act, sems):
    copies = Copies(sems)
    load = copies.start(gathered.at[:, 3, 0:SLAB, :], weight.at[0])
    act_loads = [copies.start(saved.at[plane], act.at[i]) for i, plane in enumerate((Q1, K1, V1))]
    load.wait()

    def mixed_back(index):
        rows = chunk(index, 256)
        act[3, rows, :] = dot_nt(grad_in[rows, :].astype(BF16), whole(weight, 0)).astype(BF16)

    loop(2, mixed_back)
    for copy in act_loads:
        copy.wait()
    attend_back(RowHeads(ints[0]), act, 0, 1, 2, 3)
    stores = [copies.start(act.at[i], grads_out.at[i]) for i in range(3)]
    for copy in stores:
        copy.wait()


class Shares:
    def __init__(self, core, copies, own, other):
        self.core, self.copies, self.own, self.other, self.sent = core, copies, own, other, []

    def send(self, grads, member):
        every, parity = slice(None), member % 2
        for half in range(2):
            x = 2 * half + member // 2
            if parity == 0:
                places = [(grads.at[member, half], (every, every, x))]
            else:
                places = [(grads.at[member, half, y], (every, y, x)) for y in range(4)]
            for source, place in places:
                self.sent.append(
                    self.copies.send(self.core, parity, source, self.own.at[place], self.other.at[place])
                )

    def wait(self):
        for copy in self.sent:
            copy.wait()


def keep(grads, which, value):
    value = value.astype(BF16).reshape(4, 4, 2, SLAB, D)
    for half in range(2):
        grads[which, half] = value[:, :, half]


def weight_grads(loads, act_loads, grad_in, act, out_grad, normed, mixed, grads, shares):
    def low(index):
        rows = chunk(index, 128)
        out_grad[rows, :] = grad_in[rows, :].astype(BF16)

    loop(4, low)
    loads["mixed"].wait()

    keep(grads, 3, dot_tn(mixed[...], out_grad[...]))
    shares.send(grads, 3)
    for copy in [loads["normed"]] + act_loads:
        copy.wait()

    def weight_back(which):
        keep(grads, which, dot_tn(normed[...], act[which]))

    loop(3, weight_back)
    for member in range(3):
        shares.send(grads, member)


def input_grads(loads, grad_in, gain, act, weights, hidden, da, grad_out, sums, lines=None, loaded=None):
    for i in range(3):
        for copy in loads["inputs"][i]:
            copy.wait()

        def input_back(index):
            rows = chunk(index, 256)
            value = dot_nt(act[i, rows, :], whole(weights, i))
            da[rows, :] = value if i == 0 else da[rows, :] + value

        if i == 2 and loaded is not None:
            loaded()
        loop(2, input_back)
    loads["hidden"].wait()

    def finish(index, carry):
        rows = chunk(index, 64)
        grad, before = da[rows, :], grad_in[rows, :]
        inner, unit = norm_back(grad, hidden[rows, :], gain)
        value = before + inner
        grad_out[rows, :] = value
        added = [unit, grad, act[0, rows, :], act[2, rows, :], before.astype(BF16)]
        added = [total(extra.astype(F32)) for extra in added]
        if lines is not None:
            lines[pl.ds(index, 1), :] = total(value)
            added.append(value)
        return tuple(a + b for a, b in zip(carry, added))

    carry = (jnp.zeros((1, D), F32),) * 5
    if lines is not None:
        carry = carry + (jnp.zeros((COLS, D), F32),)
    carry = lax.fori_loop(0, 8, finish, carry)
    for i in range(5):
        sums[i : i + 1, :] = carry[i]
    sums[5:8, :] = jnp.zeros((3, D), F32)
    return carry[-1]


def column_kernel(
    ints, grad_in, small, gathered, saved, hidden_saved,
    grad_out, own, other, sums,
    weights, act, out_grad, normed, mixed, hidden, da, grads, sems,
):
    copies = Copies(sems)
    shares = Shares(ints[3], copies, own, other)
    slabs = [gathered.at[:, i, SLAB : 2 * SLAB, :] for i in range(4)]
    out_load = copies.start(slabs[3], weights.at[3])
    act_loads = [copies.start(saved.at[plane], act.at[i]) for i, plane in enumerate((Q2, K2, V2))]
    loads = {"mixed": copies.start(saved.at[M2], mixed), "normed": copies.start(saved.at[A2], normed)}
    loads["inputs"] = [[copies.start(slabs[i], weights.at[i])] for i in range(3)]
    loads["hidden"] = copies.start(hidden_saved.at[1], hidden)
    out_load.wait()

    def mixed_back(index):
        rows = chunk(index, 256)
        act[3, rows, :] = dot_nt(grad_in[rows, :].astype(BF16), whole(weights, 3)).astype(BF16)

    loop(2, mixed_back)
    for copy in act_loads:
        copy.wait()
    attend_back(ColHeads(), act, 0, 1, 2, 3)
    weight_grads(loads, [], grad_in, act, out_grad, normed, mixed, grads, shares)
    input_grads(loads, grad_in, small[GAIN + 1 : GAIN + 2, :], act, weights, hidden, da, grad_out, sums)
    shares.wait()


def row_weights_kernel(
    ints, grad_in, saved, grads_in, own, other, act, out_grad, normed, mixed, grads, sems
):
    copies = Copies(sems)
    shares = Shares(ints[3], copies, own, other)
    loads = {"mixed": copies.start(saved.at[M1], mixed), "normed": copies.start(saved.at[A1], normed)}
    act_loads = [copies.start(grads_in.at[i], act.at[i]) for i in range(3)]
    weight_grads(loads, act_loads, grad_in, act, out_grad, normed, mixed, grads, shares)
    shares.wait()


def small_lines(sums, sums_col, sums_ffn):
    lines = jnp.concatenate([sums[0:5, :], sums_col[0:5, :], sums_ffn[4:7, :], sums[5:8, :]], axis=0)
    shape = (DEVICES, D)
    dev, lane = (lax.broadcasted_iota(jnp.int32, shape, axis) for axis in (0, 1))
    packed = jnp.zeros((DEVICES, 128), F32)
    for j in range(6):
        pick = jnp.where(lane == 6 * dev + j, 1.0, 0.0).astype(BF16)
        blank = [jnp.zeros((16, D), F32)] * 8
        blank[j] = lines
        packed = packed + dot_nt(pick, jnp.concatenate(blank, axis=0).astype(BF16))
    up = jnp.concatenate(
        [jnp.broadcast_to(sums_ffn[f : f + 1, :], (32, D)) for f in range(4)], axis=0
    )
    first = 24 * (dev & 31)
    up = jnp.where((lane >= first) & (lane < first + 24), up, 0.0).astype(BF16)
    shape = (128, D)
    to, lane = (lax.broadcasted_iota(jnp.int32, shape, axis) for axis in (0, 1))
    fold = jnp.where(to - 96 == lane % 24, 1.0, 0.0).astype(BF16)
    return (packed + dot_nt(up, fold)).astype(BF16)


def row_input_kernel(
    ints, grad_in, small, sums_col, sums_ffn, gathered, hidden_saved, grads_in,
    grad_out, own, other,
    weights, act, hidden, da, zeros, table, lines, sums, owned_lines, sems,
):
    copies = Copies(sems)
    loads = {"inputs": []}
    for i in range(3):
        slab = gathered.at[:, i, 0:SLAB, :]
        loads["inputs"].append(
            [copies.start(grads_in.at[i], act.at[i]), copies.start(slab, weights.at[i])]
        )
    loads["hidden"] = copies.start(hidden_saved.at[0], hidden)
    zeros[...] = jnp.zeros_like(zeros)
    fills = []

    def fill():
        fills.extend(copies.start(zeros, out.at[:, :, :, :, 0:D]) for out in (own, other))

    gain = small[GAIN : GAIN + 1, :]
    col_lines = input_grads(
        loads, grad_in, gain, act, weights, hidden, da, grad_out, sums, lines, fill
    )
    packed = small_lines(sums, sums_col, sums_ffn).astype(F32).reshape(4, 4, 4, 2, 1, 128)
    owned_lines[...] = jnp.broadcast_to(packed, owned_lines.shape).astype(BF16)
    for copy in fills:
        copy.wait()
    sent = []
    for parity in range(2):
        for x in range(4):
            source, place = owned_lines.at[:, :, x, parity], (x, slice(None), slice(None), slice(0, 16), slice(D, WIDE))
            sent.append(copies.send(ints[3], parity, source, own.at[place], other.at[place]))
    send_tables(ints, copies, lines[...], col_lines, table, own, other)
    for copy in sent:
        copy.wait()


def send_tables(ints, copies, row_lines, col_lines, table, own, other):
    core = ints[3]

    def placed(values, offset, count):
        shape = (count, values.shape[0])
        here = lax.broadcasted_iota(jnp.int32, shape, 0) == (
            lax.broadcasted_iota(jnp.int32, shape, 1) + offset % 8
        )
        return dot(jnp.where(here, 1.0, 0.0).astype(BF16), values.astype(BF16)).astype(BF16)

    spots = []
    for first, count, values, offset, start in (
        (0, 2, row_lines, ints[1], 0),
        (2, 9, col_lines, ints[2], 8),
    ):
        table[first : first + count] = placed(values, offset, 8 * count).reshape(count, 8, D)
        spots += [(first + i, offset // 8 + i, start) for i in range(count)]
    waits = []
    for slot, owner, start in spots:
        real, dev = owner < DEVICES, jnp.minimum(owner, DEVICES - 1)
        x, y, z = (dev // 2) % 4, dev // 32, (dev // 8) % 4
        place = (x, y, z, slice(start, start + 8), slice(0, D))
        sem = copies.sems.at[copies.used]
        copies.used += 1
        here = pltpu.make_async_copy(table.at[slot], own.at[place], sem)
        there = pltpu.make_async_copy(table.at[slot], other.at[place], sem)
        pl.when(real & (dev % 2 == core))(here.start)
        pl.when(real & (dev % 2 != core))(there.start)
        waits.append((real, here))
    for real, copy in waits:
        pl.when(real)(copy.wait)


VMEM = pl.BlockSpec(memory_space=pltpu.VMEM)
ANY = pl.BlockSpec(memory_space=pl.ANY)
SMEM = pl.BlockSpec(memory_space=pltpu.SMEM)
SHAPE = jax.ShapeDtypeStruct


def params(mebibytes=62):
    return pltpu.CompilerParams(vmem_limit_bytes=mebibytes * 1024 * 1024)


def cost(flops, traffic):
    return pl.CostEstimate(flops=flops, transcendentals=0, bytes_accessed=traffic)


def forward_call(ints, tokens, cotangent, small, up_bias, gathered):
    plane = (TOKENS, D)
    return pl.pallas_call(
        forward_kernel,
        name="forward",
        in_specs=[SMEM, VMEM, VMEM, VMEM, VMEM, ANY],
        out_shape=(
            SHAPE(plane, BF16),
            SHAPE(plane, F32),
            SHAPE((10,) + plane, BF16),
            SHAPE((2,) + plane, F32),
            SHAPE((8, 16, 2 * SLAB, D), BF16),
            SHAPE((8, D), F32),
        ),
        out_specs=(VMEM, VMEM, ANY, ANY, ANY, VMEM),
        scratch_shapes=[
            pltpu.VMEM((12, GROUPS, SLAB, D), BF16),
            pltpu.VMEM((4, 8, MEMBERS, SLAB, D), BF16),
            pltpu.VMEM((88, D), BF16),
            pltpu.VMEM((10,) + plane, BF16),
            pltpu.VMEM((2,) + plane, F32),
            pltpu.VMEM(plane, F32),
            pltpu.VMEM(plane, BF16),
            pltpu.VMEM(plane, BF16),
            pltpu.VMEM((2,) + plane, BF16),
            pltpu.VMEM(plane, F32),
            pltpu.VMEM(plane, F32),
            pltpu.SemaphoreType.DMA((96,)),
        ],
        compiler_params=params(),
        cost_estimate=cost(24 * 10**9, 50 * 10**6),
    )(ints, tokens, cotangent, small, up_bias, gathered)


def row_heads_call(ints, grad, gathered, saved):
    plane = (TOKENS, D)
    return pl.pallas_call(
        row_heads_kernel,
        name="row_heads",
        in_specs=[SMEM, VMEM, ANY, ANY],
        out_shape=SHAPE((3,) + plane, BF16),
        out_specs=ANY,
        scratch_shapes=[
            pltpu.VMEM((1, GROUPS, SLAB, D), BF16),
            pltpu.VMEM((4,) + plane, BF16),
            pltpu.SemaphoreType.DMA((8,)),
        ],
        compiler_params=params(),
        cost_estimate=cost(10**10, 10**7),
    )(ints, grad, gathered, saved)


PLANE = (TOKENS, D)


def share_of(rows):
    return SHAPE((4, 4, 4, rows, D), BF16)


def column_call(ints, grad, small, gathered, saved, hidden):
    return pl.pallas_call(
        column_kernel,
        name="column_back",
        in_specs=[SMEM, VMEM, VMEM, ANY, ANY, ANY],
        out_shape=(SHAPE(PLANE, F32), share_of(SLAB), share_of(SLAB), SHAPE((8, D), F32)),
        out_specs=(VMEM, ANY, ANY, VMEM),
        scratch_shapes=[
            pltpu.VMEM((4, GROUPS, SLAB, D), BF16),
            pltpu.VMEM((4,) + PLANE, BF16),
            pltpu.VMEM(PLANE, BF16),
            pltpu.VMEM(PLANE, BF16),
            pltpu.VMEM(PLANE, BF16),
            pltpu.VMEM(PLANE, F32),
            pltpu.VMEM(PLANE, F32),
            pltpu.VMEM((4, 2, 4, 4, SLAB, D), BF16),
            pltpu.SemaphoreType.DMA((48,)),
        ],
        compiler_params=params(),
        cost_estimate=cost(10**10, 10**7),
    )(ints, grad, small, gathered, saved, hidden)


def row_weights_call(ints, grad, saved, grads):
    return pl.pallas_call(
        row_weights_kernel,
        name="row_weights",
        in_specs=[SMEM, VMEM, ANY, ANY],
        out_shape=(share_of(SLAB), share_of(SLAB)),
        out_specs=(ANY, ANY),
        scratch_shapes=[
            pltpu.VMEM((3,) + PLANE, BF16),
            pltpu.VMEM(PLANE, BF16),
            pltpu.VMEM(PLANE, BF16),
            pltpu.VMEM(PLANE, BF16),
            pltpu.VMEM((4, 2, 4, 4, SLAB, D), BF16),
            pltpu.SemaphoreType.DMA((32,)),
        ],
        compiler_params=params(),
        cost_estimate=cost(10**6, 10**5),
    )(ints, grad, saved, grads)


def row_input_call(ints, grad, small, sums_col, sums_ffn, gathered, hidden, grads):
    return pl.pallas_call(
        row_input_kernel,
        name="row_input",
        in_specs=[SMEM, VMEM, VMEM, VMEM, VMEM, ANY, ANY, ANY],
        out_shape=(SHAPE(PLANE, F32),) + (SHAPE((4, 4, 4, 16, WIDE), BF16),) * 2,
        out_specs=(VMEM, ANY, ANY),
        scratch_shapes=[
            pltpu.VMEM((3, GROUPS, SLAB, D), BF16),
            pltpu.VMEM((3,) + PLANE, BF16),
            pltpu.VMEM(PLANE, F32),
            pltpu.VMEM(PLANE, F32),
            pltpu.VMEM((4, 4, 4, 16, D), BF16),
            pltpu.VMEM((11, 8, D), BF16),
            pltpu.VMEM((ROWS, D), F32),
            pltpu.VMEM((8, D), F32),
            pltpu.VMEM((4, 4, 4, 2, 16, 128), BF16),
            pltpu.SemaphoreType.DMA((48,)),
        ],
        compiler_params=params(),
        cost_estimate=cost(2 * 10**10, 10**7),
    )(ints, grad, small, sums_col, sums_ffn, gathered, hidden, grads)


def sum_of(pieces, *index):
    value = pieces[0][index].astype(F32)
    for piece in pieces[1:]:
        value = value + piece[index].astype(F32)
    return value


def split_kernel(place, *refs):
    for hop in range(4):
        to = (place[0] + hop) & 3
        for j in range(refs[-1].shape[0]):
            refs[-4 + hop][j] = sum_of(refs[:-4], to, j).astype(BF16)


def split(inputs, place):
    shape = inputs[0].shape
    rest = (0,) * (len(shape) - 2)
    large = len(shape) == 5
    in_block = pl.BlockSpec((4, 1) + shape[2:], lambda j: (0, j) + rest) if large else VMEM
    out_block = pl.BlockSpec((1,) + shape[2:], lambda j: (j,) + rest) if large else VMEM
    return pl.pallas_call(
        split_kernel,
        name="split_shares",
        grid=(4,) if large else (),
        in_specs=[SMEM] + [in_block] * len(inputs),
        out_shape=(SHAPE(shape[1:], BF16),) * 4,
        out_specs=(out_block,) * 4,
        compiler_params=params(62 if large else 6),
        cost_estimate=cost(10**6, 10**6),
    )(place, *inputs)


def sum_kernel(*refs):
    def body(j):
        refs[-1][j] = sum_of(refs[:-1], j).astype(BF16)

    loop(4, body)


def summed(parts):
    return pl.pallas_call(
        sum_kernel,
        name="column_sum",
        in_specs=[VMEM] * 4,
        out_shape=SHAPE(parts[0].shape, BF16),
        out_specs=VMEM,
        compiler_params=params(8),
        cost_estimate=cost(10**6, 10**6),
    )(*parts)


def second_kernel(place, *refs):
    for hop in range(4):
        to = (place[0] + hop) & 3

        def body(j):
            refs[5 + hop][j, 0:SLAB, :] = sum_of(refs[:4], to, j).astype(BF16)
            refs[5 + hop][j, SLAB : 2 * SLAB, :] = refs[4][to, j]

        loop(4, body)


def second_split(row, col, place):
    return pl.pallas_call(
        second_kernel,
        name="second_split",
        in_specs=[SMEM] + [VMEM] * 5,
        out_shape=(SHAPE((4, 2 * SLAB, D), BF16),) * 4,
        out_specs=(VMEM,) * 4,
        compiler_params=params(10),
        cost_estimate=cost(10**6, 10**6),
    )(place, *row, col)


def third_kernel(place, table_place, ffn, *refs):
    rows, table, pieces = refs[:4], refs[4:8], refs[8:]
    for hop in range(4):
        pieces[hop][...] = sum_of(rows, (place[0] + hop) & 3).astype(BF16)
        to = (table_place[0] + hop) & 3
        value = sum_of(table, to).astype(BF16)
        pieces[4 + hop][0:16, :] = value[:, 0:D]
        pieces[4 + hop][16:24, :] = jnp.zeros((8, D), BF16)
        pieces[4 + hop][16:24, 0:128] = value[0:8, D:WIDE]
        pieces[4 + hop][SLAB : 3 * SLAB, :] = ffn[to]


def third_split(rows, table, ffn, place, table_place):
    return pl.pallas_call(
        third_kernel,
        name="third_split",
        in_specs=[SMEM] * 2 + [VMEM] * 9,
        out_shape=(SHAPE((2 * SLAB, D), BF16),) * 4 + (SHAPE((3 * SLAB, D), BF16),) * 4,
        out_specs=(VMEM,) * 8,
        compiler_params=params(6),
        cost_estimate=cost(10**6, 10**6),
    )(place, table_place, ffn, *rows, *table)


def last_kernel(me, *refs):
    rows, rest, (down, tables), small, pieces, held = refs[:4], refs[4:8], refs[8:10], refs[10:16], refs[16:20], refs[20]
    down[...] = sum_of(rest, slice(2 * SLAB, 3 * SLAB))
    for i in range(2):
        tables[i] = sum_of(rest, slice(8 * i, 8 * i + 8))
    line = sum_of(rest, slice(16, 24), slice(0, 128))[0:1]
    gain, shift, row_bias, col_bias, up_bias, down_bias = small
    up_bias[...] = line[:, 96:120]
    lines = jnp.broadcast_to(line, (16, 128))
    value, lane = (lax.broadcasted_iota(jnp.int32, lines.shape, axis) for axis in (0, 1))
    for j in range(6):
        column = jnp.sum(jnp.where(lane == 16 * j + value, lines, 0.0), axis=1, keepdims=True)
        at = slice(j, j + 1)
        for i, first in enumerate((0, 5, 11)):
            gain[i : i + 1, at] = column[first : first + 1]
            shift[i : i + 1, at] = column[first + 1 : first + 2]
        row_bias[:, at], col_bias[:, at] = column[2:5], column[7:10]
        down_bias[:, at] = column[10:11]
    for kind, (source, start) in enumerate(((rows, 0), (rows, SLAB), (rest, SLAB))):
        value = sum_of(source, slice(start, start + SLAB))
        for member in range(MEMBERS):
            held[member, kind] = value[6 * member : 6 * member + 6, :]
    for flip in range(4):
        pieces[flip][...] = held[me[0] ^ flip].astype(BF16)


def last_split(me, rows, rest):
    return pl.pallas_call(
        last_kernel,
        name="last_split",
        in_specs=[SMEM] + [VMEM] * 8,
        out_shape=(
            SHAPE((SLAB, D), F32),
            SHAPE((2, 8, D), F32),
        )
        + (SHAPE((3, 6), F32),) * 4
        + (SHAPE((1, SLAB), F32), SHAPE((1, 6), F32))
        + (SHAPE((3, 6, D), BF16),) * 4,
        out_specs=(VMEM,) * 12,
        scratch_shapes=[pltpu.VMEM((MEMBERS, 3, 6, D), F32)],
        compiler_params=params(6),
        cost_estimate=cost(10**6, 10**6),
    )(me, *rows, *rest)


def outputs_kernel(me, one, two, three, four, row_qkv, row_out, col_qkv, col_out, up, held):
    for flip, piece in enumerate((one, two, three, four)):
        held[me[0] ^ flip] = piece[...].astype(F32)
    for i in range(3):
        row_qkv[i], col_qkv[i] = held[i, 0], held[i, 1]
    row_out[...], col_out[...] = held[3, 0], held[3, 1]
    for i in range(MEMBERS):
        up[:, i * D : (i + 1) * D] = held[i, 2]


def outputs(me, pieces):
    return pl.pallas_call(
        outputs_kernel,
        name="outputs",
        in_specs=[SMEM] + [VMEM] * 4,
        out_shape=(
            SHAPE((3, 6, D), F32),
            SHAPE((6, D), F32),
            SHAPE((3, 6, D), F32),
            SHAPE((6, D), F32),
            SHAPE((6, FF), F32),
        ),
        out_specs=(VMEM,) * 5,
        scratch_shapes=[pltpu.VMEM((MEMBERS, 3, 6, D), F32)],
        compiler_params=params(6),
        cost_estimate=cost(10**6, 10**6),
    )(me, *pieces)


def take(value, index, dim):
    return lax.squeeze(lax.dynamic_slice_in_dim(value, index, 1, dim), (dim,))


def member():
    return (lax.axis_index("x") % 2) * 2 + lax.axis_index("c")


def trade(pieces):
    came = [pieces[0]]
    for flip in range(1, 4):
        pairs = [(i, (i // 4) * 4 + ((i % 4) ^ flip)) for i in range(8)]
        came.append(lax.ppermute(pieces[flip], ("x", "c"), pairs))
    return came


def exchange(blocks):
    me = member()
    parts = trade([take(blocks, me ^ flip, 0) for flip in range(4)])
    odd, high = (me & 1) == 1, (me & 2) == 2
    pairs = [jnp.where(odd, parts[i ^ 1], parts[i]) for i in range(4)]
    return [jnp.where(high, pairs[i ^ 2], pairs[i]) for i in range(4)]


def swap(value):
    return lax.ppermute(value, "c", [(0, 1), (1, 0)])


def scatter_chip_rows(shares):
    return lax.psum_scatter(shares, ("x", "c"), scatter_dimension=0, tiled=False)


STAGES = (("y", "z"), ("z", "y"), ("x", "x"))
TABLE_STAGES = (("x", "x"), ("y", "y"), ("z", "z"))
STRIDES = {"y": 32, "z": 8, "x": 2}


def place_on(axes):
    here = jnp.where(lax.axis_index("c") == 0, lax.axis_index(axes[0]), lax.axis_index(axes[1]))
    return here.astype(jnp.int32)[None]


def deliver(pieces, axes):
    came = [pieces[0]]
    for hop in (2, 1, 3):
        pairs = []
        for dev in range(DEVICES):
            stride = STRIDES[axes[dev % 2]]
            at = dev // stride % 4
            pairs.append((dev, dev + ((at + hop) % 4 - at) * stride))
        came.append(lax.ppermute(pieces[hop], AXES, pairs))
    return came


def gather(norm_gain, norm_bias, row_qkv, row_out, row_bias, col_qkv, col_out, col_bias,
           ffn_up, up_bias, ffn_down, down_bias, pos_tables):
    row = jnp.concatenate([row_qkv, row_out[None]], axis=0)
    col = jnp.concatenate([col_qkv, col_out[None]], axis=0)
    up = ffn_up.reshape(6, MEMBERS, D).transpose(1, 0, 2)
    slabs = jnp.stack(exchange(jnp.stack([row, col, up], axis=1)), axis=1)
    packed = jnp.concatenate(
        [slabs.reshape(3 * SLAB, D), ffn_down, pos_tables[0], pos_tables[1]], axis=0
    )
    gathered = lax.all_gather(packed, AXES, axis=0, tiled=False)
    sixes = jnp.concatenate([norm_gain, norm_bias, row_bias, col_bias, down_bias[None]], axis=0)
    line = jnp.pad(jnp.concatenate([sixes.reshape(-1), up_bias]), (0, 26))
    lines = lax.all_gather(line, AXES, axis=0, tiled=False).astype(F32)
    small = lines[:, :78].reshape(DEVICES, 13, 6).transpose(1, 0, 2).reshape(13, D)
    small = jnp.pad(small, ((0, 3), (0, 0)))
    return gathered.reshape(GROUPS, MEMBERS, PACK, D), small, lines[:, 78:102].reshape(4, D)


def on_device(tokens, cotangent, lengths, row_offset, col_offset, *weights):
    gathered, small, up_bias = gather(*weights)
    core = lax.axis_index("c").astype(jnp.int32)
    ints = jnp.concatenate([lengths, row_offset, col_offset, core[None]])
    act, g2, saved, hidden, ffn_shares, ffn_sums = forward_call(
        ints, tokens.reshape(TOKENS, D), cotangent.reshape(TOKENS, D), small, up_bias, gathered
    )
    barrier = lax.optimization_barrier
    ffn = scatter_chip_rows(ffn_shares)
    g1, own, other, col_sums = column_call(ints, g2, small, gathered, saved, hidden)
    row_heads = row_heads_call(ints, g1, gathered, saved)
    places = [place_on(axes) for axes in STAGES]
    other, row_heads = barrier((swap(other), row_heads))
    pieces, row_heads = barrier((split((own, other), places[0]), row_heads))
    col = deliver(pieces, STAGES[0])
    g0, table_own, table_other = row_input_call(
        ints, g1, small, col_sums, ffn_sums, gathered, hidden, row_heads
    )
    own, other = row_weights_call(ints, g1, saved, row_heads)
    table_other, col = barrier((table_other, col))
    other, table_other, ffn = barrier((other, swap(table_other), ffn))
    ffn = lax.psum_scatter(ffn.reshape(4, 4, 2 * SLAB, D), "y", scatter_dimension=0, tiled=False)
    y_place, z_place = place_on(TABLE_STAGES[1]), place_on(TABLE_STAGES[2])
    table, other = barrier((split((table_own, table_other), places[2]), swap(other)))
    table = deliver(table, TABLE_STAGES[0])
    pieces, col = barrier((split((own, other), places[0]), col))
    row = deliver(pieces, STAGES[0])
    col = summed(col)
    table, ffn = barrier((table, ffn))
    table = deliver(split(table, y_place), TABLE_STAGES[1])
    rows = deliver(second_split(row, col, places[1]), STAGES[1])
    pieces = third_split(rows, table, ffn, places[2], z_place)
    rows, rest = deliver(pieces[:4], STAGES[2]), deliver(pieces[4:], TABLE_STAGES[2])
    return (act.reshape(tokens.shape), g0.reshape(tokens.shape)) + owned(rows, rest)


def owned(rows, rest):
    me = member().astype(jnp.int32)[None]
    down, tables, gain, shift, row_bias, col_bias, up_bias, down_bias, *pieces = last_split(me, rows, rest)
    row_qkv, row_out, col_qkv, col_out, up = outputs(me, trade(pieces))
    return (
        gain,
        shift,
        row_qkv,
        row_out,
        row_bias,
        col_qkv,
        col_out,
        col_bias,
        up,
        up_bias[0],
        down,
        down_bias[0],
        tables,
    )


def solution(mesh):
    mesh = Mesh(mesh.devices.reshape(4, 4, 4, 2), AXES)
    first, second = P(AXES), P(None, AXES)
    weights = (second, second, second, first, second, second, first, second) + (first,) * 4 + (second,)
    return jax.shard_map(
        on_device,
        mesh=mesh,
        in_specs=(first,) * 5 + weights,
        out_specs=(first, first) + weights,
        check_vma=False,
    )
```
